32 devices in a mesh: groups: 1, wide: 32 (over z, y, x, core).
Axes of the slice: x: 2, y: 2, z: 4, core: 2. Of those that a mesh axis runs over, the one named last changes fastest.
Arguments:
- queries: bfloat16 [256, 1152], P('groups'), may hold values from -4 to 4
- patch_keys: bfloat16 [4096, 1152], P(('groups', 'wide')), may hold values from -173 to 173
- patch_values: bfloat16 [4096, 2560], P(('groups', 'wide')), may hold values from -6 to 6
- norm_gain: float32 [2560], replicated, may hold values from 0.1 to 1.9
- route_experts: int32 [512, 6], P(('groups', 'wide')), may hold values from 0 to 15, all different within a row; in each aligned block of 16 rows (0 to 15, 16 to 31, ...) at most 16 rows name the same one
- route_weights: int32 [512, 6], P(('groups', 'wide')), may hold values from 1 to 16
- w_gate: bfloat16 [16384, 2560], P('wide'), may hold values from -0.125 to 0.125
- w_up: bfloat16 [16384, 2560], P('wide'), may hold values from -0.125 to 0.125
- w_down: bfloat16 [16384, 2560], P('wide'), may hold values from -0.1875 to 0.1875
Outputs:
- mixed_rows: bfloat16 [512, 2560], P(('groups', 'wide'))
The draws below stay inside these ranges and needn't reach their ends.
Inputs may be any that keep to these rules, and one draw needn't show every extreme that they name: `route_experts`: each row names 6 different experts. In each aligned block of 16 rows (the rows of one device) no expert is named by more than 16 rows, a bound that some block reaches.
All inputs are finite; a program needn't handle non-finite values.
Results may differ from the reference program's by a relative error of at most 0.02.
Values may be sent and summed in bfloat16 or wider, within the bound.
No kernel may reach another device: no remote copies, remote signals or barrier semaphores. Data moves between devices by JAX's collectives and lax.ppermute only.
A program may use at most 128 MiB of HBM per device.

```python
import math
import jax
import jax.numpy as jnp
import numpy as np
from jax import lax

D = 2560
FF = 1024
VIS = 1152
HEADS = 16
HD = 72
QUERIES = 256
TOP = 6
ROWS_DEV = 16
EXPERTS = 16
CAP = 16
IMGS = 2
PATCHES = 2048
TOKENS = 512
N_WIDE = 32


def query_table(key):
    return jnp.clip(jax.random.normal(jax.random.fold_in(key, 11), (QUERIES, VIS), jnp.float32), -4.0, 4.0)


def draw_queries(key, part):
    return query_table(key).astype(jnp.bfloat16)


def draw_patch_keys(key, part):
    total_rows = IMGS * PATCHES
    drawn = jax.random.normal(jax.random.fold_in(key, 23), (total_rows, VIS), jnp.float32)
    return jnp.clip(drawn, -4.0, 4.0).astype(jnp.bfloat16)


def set_ends(entries, own_key, least, top_value):
    spot = [jax.random.randint(jax.random.fold_in(own_key, axis), (), 0, length) for axis, length in enumerate(entries.shape)]
    widest = entries.shape.index(max(entries.shape))
    next_to = spot[:widest] + [(spot[widest] + 1) % entries.shape[widest]] + spot[widest + 1:]
    return entries.at[tuple(spot)].set(least).at[tuple(next_to)].set(top_value)


def levels(stream_key, extent, cuts, least, largest):
    def one(dim, parts):
        heights = jax.random.uniform(jax.random.fold_in(jax.random.fold_in(stream_key, 6), dim), (parts,), jnp.float32, least / len(cuts), largest / len(cuts))
        return jnp.repeat(jnp.exp(heights), extent[dim] // parts).reshape((-1,) + (1,) * (len(extent) - dim - 1))

    level = one(*cuts[0])
    for cut in cuts[1:]:
        level = level * one(*cut)
    return level


def assign_block(own_key, own, number, rows, number_of, top, limit, lean):
    order = jax.random.permutation(own_key, number_of)
    packed, common = portions_of(number_of, rows * top, limit, lean, True), portions_of(number_of, rows * top, limit, lean, False)
    places = jnp.arange(number_of)

    def named(sizes, offset_by):
        used = int((sizes > 0).sum())
        fixed = max(1, used // 4)
        moved = fixed + (places - fixed + offset_by * (used - fixed)) % max(1, number_of - fixed)
        return jnp.zeros((number_of,), jnp.int32).at[order[jnp.where(places < fixed, places, moved)]].set(jnp.asarray(sizes, jnp.int32))

    sizes = jnp.where(number % 4 == 0, named(packed, number // 4), named(common, number - number // 4 - 1))
    mixed = jax.random.permutation(jax.random.fold_in(own, 3), number_of)
    source_of, receiver = mixed[0:number_of // 2 * 2:2], mixed[1:number_of // 2 * 2:2]
    room = jnp.minimum(sizes[source_of] - 1, limit - sizes[receiver]) // 2
    room = jnp.where((source_of == order[0]) | (receiver == order[0]) | (sizes[receiver] == 0), 0, jnp.maximum(room, 0))
    moved = jax.random.randint(jax.random.fold_in(own, 4), (number_of // 2,), 0, 1 << 20) % (room + 1)
    sizes = sizes.at[source_of].add(-moved).at[receiver].add(moved)
    members = jnp.searchsorted(jnp.cumsum(sizes), jnp.arange(rows * top), side="right").astype(jnp.int32)
    grid = members.reshape(top, rows).T
    grid = grid[jax.random.permutation(jax.random.fold_in(own, 1), rows)]
    offset_by = jax.random.randint(jax.random.fold_in(own, 2), (rows, 1), 0, top)
    return jnp.take_along_axis(grid, (jnp.arange(top)[None, :] + offset_by) % top, axis=1)


def portions_of(amount, total, most, lean, full):
    loads = [(1 << 20) // math.isqrt(grade ** lean) + 1 for grade in range(1, amount + 1)]
    largest = most if full else min(most, max(-(-total // amount), total * loads[0] // sum(loads)))
    least = 1 if total - largest >= amount - 1 else 0
    counts, surplus = [largest] + [least] * (amount - 1), total - largest - least * (amount - 1)
    while surplus > 0:
        movable = [i for i in range(1, amount) if counts[i] < largest] or [i for i in range(1, amount) if counts[i] < most]
        whole, budget = sum([loads[i] for i in movable]), surplus
        for i in movable:
            more = min(most - counts[i], max(1, budget * loads[i] // whole), surplus)
            counts[i] = counts[i] + more
            surplus = surplus - more
    return np.array(counts)


def gaussian(stream_key, dims, deviation, most, shards=(), held_as=jnp.bfloat16):
    gain = levels(stream_key, dims, shards, -0.22, 0.18) if shards else 1.0
    drawn = jax.random.normal(stream_key, dims, jnp.float32) * deviation * gain
    return jnp.minimum(jnp.maximum(drawn, -most), most).astype(held_as)


def setup_inputs(seed: int = 0, part: int = 0) -> dict:
    arg_keys = jax.random.split(jax.random.key(seed), 10)
    part_splits = jax.random.split(jax.random.fold_in(arg_keys[9], part), 10)
    queries = draw_queries(jax.random.fold_in(jax.random.fold_in(arg_keys[9], part), 71), part)
    patch_keys = draw_patch_keys(jax.random.fold_in(jax.random.fold_in(arg_keys[9], part), 71), part)
    patch_values = gaussian(part_splits[2], (IMGS * PATCHES, D), 1.0, 6.0, ((0, 32),))
    norm_gain = jnp.clip(1.0 + 0.18 * jax.random.normal(arg_keys[3], (D,), jnp.float32), 0.1, 1.9)
    route_experts_keys = jax.random.split(jax.random.fold_in(part_splits[4], 1), TOKENS // ROWS_DEV)
    route_experts_turns = jax.random.permutation(jax.random.fold_in(part_splits[4], 3), TOKENS // ROWS_DEV)
    route_experts = jax.vmap(lambda own, number: assign_block(jax.random.fold_in(part_splits[4], 2), own, number, ROWS_DEV, EXPERTS, TOP, CAP, 2))(route_experts_keys, route_experts_turns).reshape((TOKENS, TOP))
    route_weights = set_ends(jax.random.randint(part_splits[5], (TOKENS, TOP), 1, 17), jax.random.fold_in(part_splits[5], 1), 1, 16).astype(jnp.int32)
    w_gate = gaussian(arg_keys[6], (EXPERTS * FF, D), D ** -0.5, 0.125, ((0, 32),))
    w_up = gaussian(arg_keys[7], (EXPERTS * FF, D), D ** -0.5, 0.125, ((0, 32),))
    w_down = gaussian(arg_keys[8], (EXPERTS * FF, D), FF ** -0.5, 0.1875, ((0, 32),))
    return dict(queries=queries, patch_keys=patch_keys, patch_values=patch_values, norm_gain=norm_gain, route_experts=route_experts, route_weights=route_weights, w_gate=w_gate, w_up=w_up, w_down=w_down)


precise = lax.Precision.HIGHEST

def reference(queries, patch_keys, patch_values, norm_gain, route_experts, route_weights, w_gate, w_up, w_down):
    value_size = D // HEADS
    score_scale = HD ** (-0.5)
    query_heads = queries.astype(jnp.float32).reshape(QUERIES, HEADS, HD)
    key_blocks = patch_keys.reshape(IMGS, PATCHES, HEADS, HD)
    value_blocks = patch_values.reshape(IMGS, PATCHES, HEADS, value_size)

    def attend(key_value):
        key_block, value_block = key_value
        scores = jnp.einsum('qhc,phc->qhp', query_heads, key_block.astype(jnp.float32), precision=precise) * score_scale
        row_peak = lax.optimization_barrier(jnp.max(scores, axis=2, keepdims=True))
        raised = jnp.exp(scores - row_peak)
        row_total = lax.optimization_barrier(jnp.sum(raised, axis=2))
        rounded = lax.optimization_barrier(raised.astype(jnp.bfloat16))
        attended = jnp.einsum('qhp,phc->qhc', rounded.astype(jnp.float32), value_block.astype(jnp.float32), precision=precise)
        attended = attended / row_total[:, :, None]
        return attended.reshape(QUERIES, D).astype(jnp.bfloat16)
    projected = lax.map(attend, (key_blocks, value_blocks)).reshape(TOKENS, D)
    residual = projected.astype(jnp.float32)
    normed = (residual * lax.rsqrt(lax.optimization_barrier(jnp.mean(residual * residual, axis=1, keepdims=True)) + 1e-06) * norm_gain).astype(jnp.bfloat16)
    blocks = route_experts.reshape(N_WIDE, ROWS_DEV * TOP)
    onehot = (blocks[:, :, None] == jnp.arange(EXPERTS, dtype=jnp.int32)[None, None, :]).astype(jnp.int32)
    earlier = jnp.cumsum(onehot, axis=1) - onehot
    slot_index = lax.optimization_barrier(jnp.sum(earlier * onehot, axis=2)).astype(jnp.int32)
    place = (jnp.arange(N_WIDE, dtype=jnp.int32)[:, None] * CAP + slot_index).reshape(-1).astype(jnp.int32)
    expert_id = route_experts.reshape(-1).astype(jnp.int32)
    row_id = (jnp.arange(TOKENS * TOP, dtype=jnp.int32) // TOP).astype(jnp.int32)
    scores_int = route_weights.astype(jnp.float32)
    gate_share = (scores_int / lax.optimization_barrier(jnp.sum(scores_int, axis=1, keepdims=True))).reshape(-1)
    row_table = jnp.zeros((EXPERTS, N_WIDE * CAP), jnp.int32).at[expert_id, place].set(row_id)
    gate_table = jnp.zeros((EXPERTS, N_WIDE * CAP), jnp.float32).at[expert_id, place].set(gate_share)
    gate_blocks = w_gate.reshape(EXPERTS, FF, D)
    up_blocks = w_up.reshape(EXPERTS, FF, D)
    down_blocks = w_down.reshape(EXPERTS, FF, D)

    def expert_step(combined, expert_item):
        table_row, gate_row, gate_matrix, up_matrix, down_matrix = expert_item
        rows_in = normed[table_row]
        gate_part = jnp.dot(rows_in, gate_matrix.T, preferred_element_type=jnp.float32)
        up_part = jnp.dot(rows_in, up_matrix.T, preferred_element_type=jnp.float32)
        hidden = (jax.nn.silu(gate_part) * up_part).astype(jnp.bfloat16)
        expert_out = jnp.dot(hidden, down_matrix, preferred_element_type=jnp.float32).astype(jnp.bfloat16)
        expert_out = lax.optimization_barrier(expert_out)
        combined = combined.at[table_row].add(gate_row[:, None] * expert_out.astype(jnp.float32))
        return (combined, None)
    combined, _ = lax.scan(expert_step, jnp.zeros((TOKENS, D), jnp.float32), (row_table, gate_table, gate_blocks, up_blocks, down_blocks))
    return (residual + combined).astype(jnp.bfloat16)
```

```python
import jax
import jax.numpy as jnp
from jax import lax
from jax.sharding import PartitionSpec as P

HEADS = 16


def partner(value, axis, stride):
    mask = 2**stride
    pairs = [(source, source ^ mask) for source in range(lax.axis_size(axis))]
    return lax.ppermute(value, axis, pairs)


def stage_orders(devices):
    bits = list(reversed(range(1, devices.bit_length() - 1)))
    other = bits[:-2] + bits[-2:][::-1]
    other = other[:2][::-1] + other[2:] if len(other) > 3 else other
    return (bits, other)


def exchange(value, orders, stage):
    pairs = [
        (source, source ^ (1 << orders[source % 2][stage]))
        for source in range(lax.axis_size("wide"))
    ]
    return lax.ppermute(value, "wide", pairs)


def merge_partials(first_part, second_part, head_count):
    sum_first, peak_first, total_first = first_part
    sum_second, peak_second, total_second = second_part
    row_peak = jnp.maximum(peak_first, peak_second)
    factor_first = jnp.exp(peak_first - row_peak)
    factor_second = jnp.exp(peak_second - row_peak)
    row_total = total_first * factor_first + total_second * factor_second
    row_count = sum_first.shape[0]
    summed = sum_first.reshape(row_count, head_count, -1) * factor_first[:, :, None]
    summed = summed + sum_second.reshape(row_count, head_count, -1) * factor_second[:, :, None]
    return (summed.reshape(row_count, -1), row_peak, row_total)


def on_device(
    queries, patch_keys, patch_values, norm_gain, route_experts, route_weights, w_gate, w_up, w_down
):
    row_count = route_experts.shape[0]
    top_k = route_experts.shape[1]
    model_width = patch_values.shape[1]
    vision_width = patch_keys.shape[1]
    head_count = HEADS
    key_size = vision_width // head_count
    value_size = model_width // head_count
    group_size = queries.shape[0] // row_count
    levels = group_size.bit_length() - 1
    devices = lax.axis_size("wide")
    device_index = lax.axis_index("wide")
    score_scale = key_size ** (-0.5)
    scores = (
        jnp.einsum(
            "qhc,phc->qhp",
            queries.reshape(-1, head_count, key_size),
            patch_keys.reshape(-1, head_count, key_size),
            preferred_element_type=jnp.float32,
        )
        * score_scale
    )
    row_peak = jnp.max(scores, axis=2)
    raised = jnp.exp(scores - row_peak[:, :, None])
    row_total = jnp.sum(raised, axis=2)
    summed = jnp.einsum(
        "qhp,phc->qhc",
        raised.astype(jnp.bfloat16),
        patch_values.reshape(-1, head_count, value_size),
        preferred_element_type=jnp.float32,
    ).reshape(-1, model_width)
    for bit_number in reversed(range(levels)):
        half_rows = summed.shape[0] // 2
        upper_half = device_index // (1 << bit_number) % 2 == 1
        kept_part = (
            jnp.where(upper_half, summed[half_rows:], summed[:half_rows]),
            jnp.where(upper_half, row_peak[half_rows:], row_peak[:half_rows]),
            jnp.where(upper_half, row_total[half_rows:], row_total[:half_rows]),
        )
        sent_sum = jnp.where(upper_half, summed[:half_rows], summed[half_rows:])
        sent_peak = jnp.where(upper_half, row_peak[:half_rows], row_peak[half_rows:])
        sent_total = jnp.where(upper_half, row_total[:half_rows], row_total[half_rows:])
        partner_part = partner((sent_sum, sent_peak, sent_total), "wide", bit_number)
        summed, row_peak, row_total = merge_partials(kept_part, partner_part, head_count)
    attended = summed.reshape(row_count, head_count, value_size) / row_total[:, :, None]
    projected = attended.reshape(row_count, model_width).astype(jnp.bfloat16)
    residual = projected.astype(jnp.float32)
    normed = (
        residual
        * lax.rsqrt(jnp.mean(residual * residual, axis=1, keepdims=True) + 1e-06)
        * norm_gain
    ).astype(jnp.bfloat16)
    experts = devices // 2
    lane_pad = -experts % 128
    score_table = jnp.sum(
        jnp.where(
            route_experts[:, :, None] == jnp.arange(experts, dtype=jnp.int32)[None, None, :],
            route_weights[:, :, None],
            0,
        ),
        axis=1,
    ).astype(jnp.bfloat16)
    block = jnp.concatenate(
        [normed, score_table, jnp.zeros((row_count, lane_pad), jnp.bfloat16)], axis=1
    )
    orders = stage_orders(devices)
    for stage in range(len(orders[0])):
        block = jnp.concatenate([block, exchange(block, orders, stage)], axis=0)
    block = jnp.concatenate([block, partner(block, "wide", 0)], axis=0)
    rows_in = block[:, :model_width]
    score_rows = block[:, model_width : model_width + experts].astype(jnp.float32)
    own_expert = jnp.arange(experts, dtype=jnp.int32)[None, :] == device_index // 2
    share = jnp.sum(jnp.where(own_expert, score_rows, 0.0), axis=1, keepdims=True) / jnp.sum(
        score_rows, axis=1, keepdims=True
    )
    gate_part = lax.dot_general(
        rows_in, w_gate, (((1,), (1,)), ((), ())), preferred_element_type=jnp.float32
    )
    up_part = lax.dot_general(
        rows_in, w_up, (((1,), (1,)), ((), ())), preferred_element_type=jnp.float32
    )
    hidden = (jax.nn.silu(gate_part) * up_part * share).astype(jnp.bfloat16)
    partial_value = lax.dot_general(
        hidden, w_down, (((1,), (0,)), ((), ())), preferred_element_type=jnp.float32
    )
    half_rows = partial_value.shape[0] // 2
    total = partial_value[:half_rows] + partner(
        partial_value[half_rows:].astype(jnp.bfloat16), "wide", 0
    ).astype(jnp.float32)
    for stage in reversed(range(len(orders[0]))):
        half_rows = total.shape[0] // 2
        total = total[:half_rows] + exchange(
            total[half_rows:].astype(jnp.bfloat16), orders, stage
        ).astype(jnp.float32)
    return (residual + total).astype(jnp.bfloat16)


def solution(mesh):
    return jax.shard_map(
        on_device,
        mesh=mesh,
        in_specs=(
            P("groups", None),
            P(("groups", "wide"), None),
            P(("groups", "wide"), None),
            P(),
            P(("groups", "wide"), None),
            P(("groups", "wide"), None),
            P("wide", None),
            P("wide", None),
            P("wide", None),
        ),
        out_specs=P(("groups", "wide"), None),
        check_vma=False,
    )
```

```python
import functools

import jax
import jax.numpy as jnp
from jax import lax
from jax.experimental import pallas as pl
from jax.experimental.pallas import tpu as pltpu
from jax.sharding import PartitionSpec as P

HEADS = 16
LANES = 128


def partner(value, axis, stride):
    mask = 2**stride
    pairs = [(source, source ^ mask) for source in range(lax.axis_size(axis))]
    return lax.ppermute(value, axis, pairs)


def stage_orders(devices):
    bits = list(reversed(range(1, devices.bit_length() - 1)))
    other = bits[:-2] + bits[-2:][::-1]
    other = other[:2][::-1] + other[2:] if len(other) > 3 else other
    return (bits, other)


def merge_orders(group_size):
    bits = list(range(1, group_size.bit_length() - 1))
    return (bits, bits[1:] + bits[:1])


def exchange(value, orders, stage):
    pairs = [
        (source, source ^ (1 << orders[source % 2][stage]))
        for source in range(lax.axis_size("wide"))
    ]
    return lax.ppermute(value, "wide", pairs)


def lane_iota(shape):
    return lax.broadcasted_iota(jnp.int32, shape, 1)


def expand_tile(columns, tile, value_size):
    first = tile * LANES // value_size
    last = (tile * LANES + LANES - 1) // value_size
    rows = columns[0].shape[0]
    out = jnp.broadcast_to(columns[first], (rows, LANES))
    for head in range(first + 1, last + 1):
        edge = head * value_size - tile * LANES
        out = jnp.where(lane_iota((rows, LANES)) < edge, out, columns[head])
    return out


def pack_stats(peak, total, head_count):
    lane = lane_iota(peak.shape)
    high = total.astype(jnp.bfloat16).astype(jnp.float32)
    low = total - high
    packed = jnp.where(lane < head_count, peak, 0.0)
    shifted = pltpu.roll(jnp.where(lane < head_count, high, 0.0), head_count, 1)
    shifted_low = pltpu.roll(jnp.where(lane < head_count, low, 0.0), 2 * head_count, 1)
    return packed + shifted + shifted_low


def total_of(stats, head_count):
    return pltpu.roll(stats, LANES - head_count, 1) + pltpu.roll(
        stats, LANES - 2 * head_count, 1
    )


def attend_kernel(
    head_count,
    row_count,
    blocks_ref,
    queries_ref,
    keys_a_ref,
    keys_b_ref,
    values_a_ref,
    values_b_ref,
    sent_ref,
    kept_ref,
    query_scratch,
):
    block_count = blocks_ref.shape[0]
    rows = block_count * row_count
    half = rows // 2
    vision_width = queries_ref.shape[1]
    model_width = values_a_ref.shape[1]
    key_size = vision_width // head_count
    value_size = model_width // head_count
    scale = key_size ** (-0.5)
    for slot in range(block_count):
        start = pl.multiple_of(blocks_ref[slot] * row_count, row_count)
        query_scratch[slot * row_count : (slot + 1) * row_count, :] = queries_ref[
            pl.ds(start, row_count), :
        ]
    peaks = jnp.zeros((rows, LANES), jnp.float32)
    totals = jnp.zeros((rows, LANES), jnp.float32)
    lane = lane_iota((rows, LANES))
    contract_last = (((1,), (1,)), ((), ()))
    contract_rows = (((1,), (0,)), ((), ()))
    waiting = None

    def put(tile, value):
        columns = slice(tile * LANES, (tile + 1) * LANES)
        kept_ref[:, columns] = value[:half]
        sent_ref[:, columns] = value[half:].astype(jnp.bfloat16)

    for head in range(head_count):
        low = head * key_size // LANES * LANES
        high = -(-(head + 1) * key_size // LANES) * LANES
        window = lane_iota((rows, high - low)) + low
        inside = (window >= head * key_size) & (window < (head + 1) * key_size)
        query = jnp.where(inside, query_scratch[:, low:high], jnp.zeros((), jnp.bfloat16))
        score_a = scale * lax.dot_general(
            query, keys_a_ref[:, low:high], contract_last, preferred_element_type=jnp.float32
        )
        score_b = scale * lax.dot_general(
            query, keys_b_ref[:, low:high], contract_last, preferred_element_type=jnp.float32
        )
        peak = jnp.maximum(
            jnp.max(score_a, axis=1, keepdims=True), jnp.max(score_b, axis=1, keepdims=True)
        )
        peak = peak.astype(jnp.bfloat16).astype(jnp.float32)
        raised_a = jnp.exp(score_a - peak)
        raised_b = jnp.exp(score_b - peak)
        total = jnp.sum(raised_a, axis=1, keepdims=True) + jnp.sum(
            raised_b, axis=1, keepdims=True
        )
        peaks = jnp.where(lane == head, peak, peaks)
        totals = jnp.where(lane == head, total, totals)
        low = head * value_size // LANES
        high = -(-(head + 1) * value_size // LANES)
        summed = lax.dot_general(
            raised_a.astype(jnp.bfloat16),
            values_a_ref[:, low * LANES : high * LANES],
            contract_rows,
            preferred_element_type=jnp.float32,
        ) + lax.dot_general(
            raised_b.astype(jnp.bfloat16),
            values_b_ref[:, low * LANES : high * LANES],
            contract_rows,
            preferred_element_type=jnp.float32,
        )
        for tile in range(low, high):
            value = summed[:, (tile - low) * LANES : (tile - low + 1) * LANES]
            edge = head * value_size - tile * LANES
            if edge > 0:
                value = jnp.where(lane < edge, waiting, value)
            if (tile + 1) * LANES > (head + 1) * value_size:
                waiting = value
            else:
                put(tile, value)
    put(model_width // LANES, pack_stats(peaks, totals, head_count))


def merged_parts(kept_ref, came_ref, head_count, model_width):
    stats_a = kept_ref[:, model_width:]
    stats_b = came_ref[:, model_width:].astype(jnp.float32)
    peak = jnp.maximum(stats_a, stats_b)
    factor_a = jnp.exp(stats_a - peak)
    factor_b = jnp.exp(stats_b - peak)
    total = total_of(stats_a, head_count) * factor_a + total_of(stats_b, head_count) * factor_b
    return peak, total, factor_a, factor_b


def head_columns(array, head_count):
    return [array[:, head : head + 1] for head in range(head_count)]


def merge_kernel(head_count, kept_ref, came_ref, sent_ref, next_ref):
    model_width = kept_ref.shape[1] - LANES
    half = kept_ref.shape[0] // 2
    peak, total, factor_a, factor_b = merged_parts(kept_ref, came_ref, head_count, model_width)
    columns_a = head_columns(factor_a, head_count)
    columns_b = head_columns(factor_b, head_count)
    for tile in range(model_width // LANES + 1):
        columns = slice(tile * LANES, (tile + 1) * LANES)
        if tile * LANES == model_width:
            value = pack_stats(peak, total, head_count)
        else:
            value = kept_ref[:, columns] * expand_tile(
                columns_a, tile, model_width // head_count
            ) + came_ref[:, columns].astype(jnp.float32) * expand_tile(
                columns_b, tile, model_width // head_count
            )
        next_ref[:, columns] = value[:half]
        sent_ref[:, columns] = value[half:].astype(jnp.bfloat16)


def finish_kernel(head_count, kept_ref, came_ref, gain_ref, table_ref, block_ref, projected_ref):
    model_width = kept_ref.shape[1] - LANES
    _, total, factor_a, factor_b = merged_parts(kept_ref, came_ref, head_count, model_width)
    columns_a = head_columns(factor_a / total, head_count)
    columns_b = head_columns(factor_b / total, head_count)
    square = jnp.zeros((kept_ref.shape[0], LANES), jnp.float32)
    for tile in range(model_width // LANES):
        columns = slice(tile * LANES, (tile + 1) * LANES)
        value = kept_ref[:, columns] * expand_tile(
            columns_a, tile, model_width // head_count
        ) + came_ref[:, columns].astype(jnp.float32) * expand_tile(
            columns_b, tile, model_width // head_count
        )
        rounded = value.astype(jnp.bfloat16)
        projected_ref[:, columns] = rounded
        residual = rounded.astype(jnp.float32)
        square = square + residual * residual
    mean = jnp.sum(square, axis=1, keepdims=True) / model_width
    inverse = lax.rsqrt(mean + 1e-06)
    normed = projected_ref[...].astype(jnp.float32) * inverse * gain_ref[...]
    block_ref[:, :model_width] = normed.astype(jnp.bfloat16)
    block_ref[:, model_width:] = table_ref[...]


def attention_rows(queries, patch_keys, patch_values, norm_gain, table, row_count):
    model_width = patch_values.shape[1]
    packed_width = model_width + LANES
    group_size = queries.shape[0] // row_count
    orders = merge_orders(group_size)
    stages = len(orders[0])
    device_index = lax.axis_index("wide")
    masks = [
        [
            sum(
                (1 << order[stage])
                for stage in range(stages)
                if slot >> (stages - 1 - stage) & 1
            )
            for slot in range(1 << stages)
        ]
        for order in orders
    ]
    masks = jnp.array(masks, jnp.int32)
    blocks = (device_index % group_size) ^ jnp.where(device_index % 2 == 1, masks[1], masks[0])
    rows = row_count << stages
    other_keys = partner(patch_keys, "wide", 0)
    other_values = partner(patch_values, "wide", 0)
    whole = pl.BlockSpec(memory_space=pltpu.VMEM)

    def pair_shapes(rows):
        return (
            jax.ShapeDtypeStruct((rows, packed_width), jnp.bfloat16),
            jax.ShapeDtypeStruct((rows, packed_width), jnp.float32),
        )

    sent, kept = pl.pallas_call(
        functools.partial(attend_kernel, HEADS, row_count),
        name="attend",
        out_shape=pair_shapes(rows // 2),
        in_specs=[pl.BlockSpec(memory_space=pltpu.SMEM)] + [whole] * 5,
        out_specs=(whole, whole),
        scratch_shapes=[pltpu.VMEM((rows, queries.shape[1]), jnp.bfloat16)],
    )(blocks, queries, patch_keys, other_keys, patch_values, other_values)
    for stage in range(stages - 1):
        came = exchange(sent, orders, stage)
        sent, kept = pl.pallas_call(
            functools.partial(merge_kernel, HEADS),
            name="merge",
            out_shape=pair_shapes(kept.shape[0] // 2),
            in_specs=[whole] * 2,
            out_specs=(whole, whole),
        )(kept, came)
    came = exchange(sent, orders, stages - 1)
    return pl.pallas_call(
        functools.partial(finish_kernel, HEADS),
        name="finish",
        out_shape=(
            jax.ShapeDtypeStruct((row_count, packed_width), jnp.bfloat16),
            jax.ShapeDtypeStruct((row_count, model_width), jnp.bfloat16),
        ),
        in_specs=[whole] * 4,
        out_specs=(whole, whole),
    )(kept, came, norm_gain.reshape(1, model_width), table)


def on_device(
    queries, patch_keys, patch_values, norm_gain, route_experts, route_weights, w_gate, w_up, w_down
):
    row_count = route_experts.shape[0]
    model_width = patch_values.shape[1]
    devices = lax.axis_size("wide")
    device_index = lax.axis_index("wide")
    experts = devices // 2
    score_table = jnp.sum(
        jnp.where(
            route_experts[:, :, None] == jnp.arange(LANES, dtype=jnp.int32)[None, None, :],
            route_weights[:, :, None],
            0,
        ),
        axis=1,
    ).astype(jnp.bfloat16)
    block, projected = attention_rows(
        queries, patch_keys, patch_values, norm_gain, score_table, row_count
    )
    orders = stage_orders(devices)
    for stage in range(len(orders[0])):
        block = jnp.concatenate([block, exchange(block, orders, stage)], axis=0)
    block = jnp.concatenate([block, partner(block, "wide", 0)], axis=0)
    rows_in = block[:, :model_width]
    score_rows = block[:, model_width : model_width + experts].astype(jnp.float32)
    own_expert = jnp.arange(experts, dtype=jnp.int32)[None, :] == device_index // 2
    share = jnp.sum(jnp.where(own_expert, score_rows, 0.0), axis=1, keepdims=True) / jnp.sum(
        score_rows, axis=1, keepdims=True
    )
    gate_part = lax.dot_general(
        rows_in, w_gate, (((1,), (1,)), ((), ())), preferred_element_type=jnp.float32
    )
    up_part = lax.dot_general(
        rows_in, w_up, (((1,), (1,)), ((), ())), preferred_element_type=jnp.float32
    )
    hidden = (jax.nn.silu(gate_part) * up_part * share).astype(jnp.bfloat16)
    partial_value = lax.dot_general(
        hidden, w_down, (((1,), (0,)), ((), ())), preferred_element_type=jnp.float32
    )
    half_rows = partial_value.shape[0] // 2
    total = partial_value[:half_rows] + partner(
        partial_value[half_rows:].astype(jnp.bfloat16), "wide", 0
    ).astype(jnp.float32)
    for stage in reversed(range(len(orders[0]))):
        half_rows = total.shape[0] // 2
        total = total[:half_rows] + exchange(
            total[half_rows:].astype(jnp.bfloat16), orders, stage
        ).astype(jnp.float32)
    return (projected.astype(jnp.float32) + total).astype(jnp.bfloat16)


def solution(mesh):
    return jax.shard_map(
        on_device,
        mesh=mesh,
        in_specs=(
            P("groups", None),
            P(("groups", "wide"), None),
            P(("groups", "wide"), None),
            P(),
            P(("groups", "wide"), None),
            P(("groups", "wide"), None),
            P("wide", None),
            P("wide", None),
            P("wide", None),
        ),
        out_specs=P(("groups", "wide"), None),
        check_vma=False,
    )
```

```python
import functools

import jax
import jax.numpy as jnp
from jax import lax
from jax.experimental import pallas as pl
from jax.experimental.pallas import tpu as pltpu
from jax.sharding import PartitionSpec as P


HEADS = 16
LANES = 128


def near(value):
    return pltpu.with_memory_space_constraint(value, pltpu.VMEM)


def far(value):
    return pltpu.with_memory_space_constraint(value, pltpu.HBM)


def near_shape(shape, dtype):
    return pltpu.VMEM(shape, dtype)


def partner(value, axis, stride):
    mask = 2**stride
    pairs = [(source, source ^ mask) for source in range(lax.axis_size(axis))]
    return lax.ppermute(value, axis, pairs)


def stage_orders(devices):
    bits = list(reversed(range(1, devices.bit_length() - 1)))
    other = bits[:-2] + bits[-2:][::-1]
    other = other[:2][::-1] + other[2:] if len(other) > 3 else other
    return (bits, other)


def merge_orders(group_size):
    bits = list(range(1, group_size.bit_length() - 1))
    return (bits, bits[1:] + bits[:1])


def exchange(value, orders, stage):
    pairs = [
        (source, source ^ (1 << orders[source % 2][stage]))
        for source in range(lax.axis_size("wide"))
    ]
    return lax.ppermute(value, "wide", pairs)


def lane_iota(shape):
    return lax.broadcasted_iota(jnp.int32, shape, 1)


def expand_tile(columns, tile, value_size):
    first = tile * LANES // value_size
    last = (tile * LANES + LANES - 1) // value_size
    rows = columns[0].shape[0]
    out = jnp.broadcast_to(columns[first], (rows, LANES))
    for head in range(first + 1, last + 1):
        edge = head * value_size - tile * LANES
        out = jnp.where(lane_iota((rows, LANES)) < edge, out, columns[head])
    return out


def pack_stats(peak, total, head_count):
    lane = lane_iota(peak.shape)
    high = total.astype(jnp.bfloat16).astype(jnp.float32)
    low = total - high
    packed = jnp.where(lane < head_count, peak, 0.0)
    shifted = pltpu.roll(jnp.where(lane < head_count, high, 0.0), head_count, 1)
    shifted_low = pltpu.roll(jnp.where(lane < head_count, low, 0.0), 2 * head_count, 1)
    return packed + shifted + shifted_low


def total_of(stats, head_count):
    return pltpu.roll(stats, LANES - head_count, 1) + pltpu.roll(
        stats, LANES - 2 * head_count, 1
    )


def attend_kernel(
    head_count,
    row_count,
    blocks_ref,
    queries_ref,
    keys_a_ref,
    keys_b_ref,
    values_a_ref,
    values_b_ref,
    sent_ref,
    kept_ref,
    query_scratch,
):
    block_count = blocks_ref.shape[0]
    rows = block_count * row_count
    half = rows // 2
    vision_width = queries_ref.shape[1]
    model_width = values_a_ref.shape[1]
    key_size = vision_width // head_count
    value_size = model_width // head_count
    scale = key_size ** (-0.5)
    for slot in range(block_count):
        start = pl.multiple_of(blocks_ref[slot] * row_count, row_count)
        query_scratch[slot * row_count : (slot + 1) * row_count, :] = queries_ref[
            pl.ds(start, row_count), :
        ]
    peaks = jnp.zeros((rows, LANES), jnp.float32)
    totals = jnp.zeros((rows, LANES), jnp.float32)
    lane = lane_iota((rows, LANES))
    contract_last = (((1,), (1,)), ((), ()))
    contract_rows = (((1,), (0,)), ((), ()))
    waiting = None

    def put(tile, value):
        columns = slice(tile * LANES, (tile + 1) * LANES)
        kept_ref[:, columns] = value[:half]
        sent_ref[:, columns] = value[half:].astype(jnp.bfloat16)

    for head in range(head_count):
        low = head * key_size // LANES * LANES
        high = -(-(head + 1) * key_size // LANES) * LANES
        window = lane_iota((rows, high - low)) + low
        inside = (window >= head * key_size) & (window < (head + 1) * key_size)
        query = jnp.where(inside, query_scratch[:, low:high], jnp.zeros((), jnp.bfloat16))
        score_a = scale * lax.dot_general(
            query, keys_a_ref[:, low:high], contract_last, preferred_element_type=jnp.float32
        )
        score_b = scale * lax.dot_general(
            query, keys_b_ref[:, low:high], contract_last, preferred_element_type=jnp.float32
        )
        peak = jnp.maximum(
            jnp.max(score_a, axis=1, keepdims=True), jnp.max(score_b, axis=1, keepdims=True)
        )
        peak = peak.astype(jnp.bfloat16).astype(jnp.float32)
        raised_a = jnp.exp(score_a - peak)
        raised_b = jnp.exp(score_b - peak)
        total = jnp.sum(raised_a, axis=1, keepdims=True) + jnp.sum(
            raised_b, axis=1, keepdims=True
        )
        peaks = jnp.where(lane == head, peak, peaks)
        totals = jnp.where(lane == head, total, totals)
        low = head * value_size // LANES
        high = -(-(head + 1) * value_size // LANES)
        summed = lax.dot_general(
            raised_a.astype(jnp.bfloat16),
            values_a_ref[:, low * LANES : high * LANES],
            contract_rows,
            preferred_element_type=jnp.float32,
        ) + lax.dot_general(
            raised_b.astype(jnp.bfloat16),
            values_b_ref[:, low * LANES : high * LANES],
            contract_rows,
            preferred_element_type=jnp.float32,
        )
        for tile in range(low, high):
            value = summed[:, (tile - low) * LANES : (tile - low + 1) * LANES]
            edge = head * value_size - tile * LANES
            if edge > 0:
                value = jnp.where(lane < edge, waiting, value)
            if (tile + 1) * LANES > (head + 1) * value_size:
                waiting = value
            else:
                put(tile, value)
    put(model_width // LANES, pack_stats(peaks, totals, head_count))


def merged_parts(kept_ref, came_ref, head_count, model_width):
    stats_a = kept_ref[:, model_width:]
    stats_b = came_ref[:, model_width:].astype(jnp.float32)
    peak = jnp.maximum(stats_a, stats_b)
    factor_a = jnp.exp(stats_a - peak)
    factor_b = jnp.exp(stats_b - peak)
    total = total_of(stats_a, head_count) * factor_a + total_of(stats_b, head_count) * factor_b
    return peak, total, factor_a, factor_b


def head_columns(array, head_count):
    return [array[:, head : head + 1] for head in range(head_count)]


def merge_kernel(head_count, kept_ref, came_ref, sent_ref, next_ref):
    model_width = kept_ref.shape[1] - LANES
    half = kept_ref.shape[0] // 2
    peak, total, factor_a, factor_b = merged_parts(kept_ref, came_ref, head_count, model_width)
    columns_a = head_columns(factor_a, head_count)
    columns_b = head_columns(factor_b, head_count)
    for tile in range(model_width // LANES + 1):
        columns = slice(tile * LANES, (tile + 1) * LANES)
        if tile * LANES == model_width:
            value = pack_stats(peak, total, head_count)
        else:
            value = kept_ref[:, columns] * expand_tile(
                columns_a, tile, model_width // head_count
            ) + came_ref[:, columns].astype(jnp.float32) * expand_tile(
                columns_b, tile, model_width // head_count
            )
        next_ref[:, columns] = value[:half]
        sent_ref[:, columns] = value[half:].astype(jnp.bfloat16)


def finish_kernel(head_count, kept_ref, came_ref, gain_ref, table_ref, block_ref, projected_ref):
    model_width = kept_ref.shape[1] - LANES
    _, total, factor_a, factor_b = merged_parts(kept_ref, came_ref, head_count, model_width)
    columns_a = head_columns(factor_a / total, head_count)
    columns_b = head_columns(factor_b / total, head_count)
    square = jnp.zeros((kept_ref.shape[0], LANES), jnp.float32)
    for tile in range(model_width // LANES):
        columns = slice(tile * LANES, (tile + 1) * LANES)
        value = kept_ref[:, columns] * expand_tile(
            columns_a, tile, model_width // head_count
        ) + came_ref[:, columns].astype(jnp.float32) * expand_tile(
            columns_b, tile, model_width // head_count
        )
        rounded = value.astype(jnp.bfloat16)
        projected_ref[:, columns] = rounded
        residual = rounded.astype(jnp.float32)
        square = square + residual * residual
    mean = jnp.sum(square, axis=1, keepdims=True) / model_width
    inverse = lax.rsqrt(mean + 1e-06)
    normed = projected_ref[...].astype(jnp.float32) * inverse * gain_ref[...]
    block_ref[:, :model_width] = normed.astype(jnp.bfloat16)
    block_ref[:, model_width:] = table_ref[...]


def expert_kernel(
    steps, expert_ref, rows_ref, gate_a, gate_b, up_a, up_b, down_a, down_b, out_ref, total_ref
):
    step = pl.program_id(0)
    model_width = total_ref.shape[1]
    contract_last = (((1,), (1,)), ((), ()))

    def add_units(gate_ref, up_ref, down_ref):
        rows = rows_ref[:, :model_width]
        scores = rows_ref[:, model_width:].astype(jnp.float32)
        chosen = jnp.where(lane_iota(scores.shape) == expert_ref[0], scores, 0.0)
        share = jnp.sum(chosen, axis=1, keepdims=True) / jnp.sum(scores, axis=1, keepdims=True)
        gate_part = lax.dot_general(
            rows, gate_ref[...], contract_last, preferred_element_type=jnp.float32
        )
        up_part = lax.dot_general(
            rows, up_ref[...], contract_last, preferred_element_type=jnp.float32
        )
        silu = gate_part / (1.0 + jnp.exp(-gate_part))
        hidden = (silu * up_part * share).astype(jnp.bfloat16)
        total_ref[...] += jnp.dot(hidden, down_ref[...], preferred_element_type=jnp.float32)

    @pl.when(step == 0)
    def _():
        total_ref[...] = jnp.zeros_like(total_ref)

    @pl.when(step < steps)
    def _():
        add_units(gate_a, up_a, down_a)

    @pl.when(step >= steps)
    def _():
        add_units(gate_b, up_b, down_b)

    @pl.when(step == 2 * steps - 1)
    def _():
        out_ref[...] = total_ref[...].astype(out_ref.dtype)


def expert_rows(expert, rows, weights, out_dtype):
    units, model_width = weights[0].shape
    row_count = rows.shape[0]
    whole = pl.BlockSpec(memory_space=pltpu.VMEM)
    tile = min(2 * LANES, units)
    steps = units // tile
    first = pl.BlockSpec((tile, model_width), lambda step: (jnp.minimum(step, steps - 1), 0))
    second = pl.BlockSpec((tile, model_width), lambda step: (jnp.maximum(step - steps, 0), 0))
    flops = 2 * 3 * row_count * model_width * units * 2
    return pl.pallas_call(
        functools.partial(expert_kernel, steps),
        name="expert",
        grid=(2 * steps,),
        compiler_params=pltpu.CompilerParams(vmem_limit_bytes=36 << 20),
        out_shape=near_shape((row_count, model_width), out_dtype),
        in_specs=[pl.BlockSpec(memory_space=pltpu.SMEM), whole] + [first, second] * 3,
        out_specs=whole,
        scratch_shapes=[pltpu.VMEM((row_count, model_width), jnp.float32)],
        cost_estimate=pl.CostEstimate(
            flops=flops,
            transcendentals=0,
            bytes_accessed=12 * units * model_width,
        ),
    )(expert, near(rows), *[far(weight) for weight in weights])


def attention_rows(
    queries, patch_keys, patch_values, other_keys, other_values, norm_gain, table, row_count
):
    model_width = patch_values.shape[1]
    packed_width = model_width + LANES
    group_size = queries.shape[0] // row_count
    orders = merge_orders(group_size)
    stages = len(orders[0])
    device_index = lax.axis_index("wide")
    masks = [
        [
            sum(
                (1 << order[stage])
                for stage in range(stages)
                if slot >> (stages - 1 - stage) & 1
            )
            for slot in range(1 << stages)
        ]
        for order in orders
    ]
    masks = jnp.array(masks, jnp.int32)
    blocks = (device_index % group_size) ^ jnp.where(device_index % 2 == 1, masks[1], masks[0])
    rows = row_count << stages
    whole = pl.BlockSpec(memory_space=pltpu.VMEM)

    def pair_shapes(rows):
        return (
            near_shape((rows, packed_width), jnp.bfloat16),
            near_shape((rows, packed_width), jnp.float32),
        )

    sent, kept = pl.pallas_call(
        functools.partial(attend_kernel, HEADS, row_count),
        name="attend",
        compiler_params=pltpu.CompilerParams(vmem_limit_bytes=12 << 20),
        out_shape=pair_shapes(rows // 2),
        in_specs=[pl.BlockSpec(memory_space=pltpu.SMEM)] + [whole] * 5,
        out_specs=(whole, whole),
        scratch_shapes=[pltpu.VMEM((rows, queries.shape[1]), jnp.bfloat16)],
    )(
        blocks,
        far(queries),
        far(patch_keys),
        near(other_keys),
        far(patch_values),
        near(other_values),
    )
    for stage in range(stages - 1):
        came = exchange(sent, orders, stage)
        sent, kept = pl.pallas_call(
            functools.partial(merge_kernel, HEADS),
            name="merge",
            compiler_params=pltpu.CompilerParams(vmem_limit_bytes=6 << 20),
            out_shape=pair_shapes(kept.shape[0] // 2),
            in_specs=[whole] * 2,
            out_specs=(whole, whole),
        )(near(kept), near(came))
    came = exchange(sent, orders, stages - 1)
    return pl.pallas_call(
        functools.partial(finish_kernel, HEADS),
        name="finish",
        compiler_params=pltpu.CompilerParams(vmem_limit_bytes=6 << 20),
        out_shape=(
            near_shape((row_count, packed_width), jnp.bfloat16),
            near_shape((row_count, model_width), jnp.bfloat16),
        ),
        in_specs=[whole] * 4,
        out_specs=(whole, whole),
    )(near(kept), near(came), near(norm_gain.reshape(1, model_width)), near(table))


def on_device(
    queries, patch_keys, patch_values, norm_gain, route_experts, route_weights, w_gate, w_up, w_down
):
    row_count = route_experts.shape[0]
    devices = lax.axis_size("wide")
    device_index = lax.axis_index("wide")
    score_table = jnp.sum(
        jnp.where(
            route_experts[:, :, None] == jnp.arange(LANES, dtype=jnp.int32)[None, None, :],
            route_weights[:, :, None],
            0,
        ),
        axis=1,
    ).astype(jnp.bfloat16)
    other_keys = partner(patch_keys, "wide", 0)
    other_values = partner(patch_values, "wide", 0)
    halves, other_keys, other_values = lax.optimization_barrier(
        ((w_gate, w_up, w_down), other_keys, other_values)
    )
    weights = []
    for own in halves:
        weights += [own, partner(own, "wide", 0)]
    block, projected = attention_rows(
        queries,
        patch_keys,
        patch_values,
        other_keys,
        other_values,
        norm_gain,
        score_table,
        row_count,
    )
    orders = stage_orders(devices)
    stages = len(orders[0])
    for stage in range(stages - 1):
        block = jnp.concatenate([block, exchange(block, orders, stage)], axis=0)
    came = exchange(block, orders, stages - 1)
    expert = (device_index // 2).reshape(1)
    total = expert_rows(expert, block, weights, jnp.float32)
    sent = expert_rows(expert, came, weights, jnp.bfloat16)
    total = total + exchange(sent, orders, stages - 1).astype(jnp.float32)
    for stage in reversed(range(stages - 1)):
        half_rows = total.shape[0] // 2
        total = total[:half_rows] + exchange(
            total[half_rows:].astype(jnp.bfloat16), orders, stage
        ).astype(jnp.float32)
    return (projected.astype(jnp.float32) + total).astype(jnp.bfloat16)


def solution(mesh):
    return mapped(mesh)


def mapped(mesh):
    return jax.shard_map(
        on_device,
        mesh=mesh,
        in_specs=(
            P("groups", None),
            P(("groups", "wide"), None),
            P(("groups", "wide"), None),
            P(),
            P(("groups", "wide"), None),
            P(("groups", "wide"), None),
            P("wide", None),
            P("wide", None),
            P("wide", None),
        ),
        out_specs=P(("groups", "wide"), None),
        check_vma=False,
    )
```

```python
import functools

import jax
import jax.numpy as jnp
from jax import lax
from jax.experimental import pallas as pl
from jax.experimental.pallas import tpu as pltpu
from jax.sharding import PartitionSpec as P


HEADS = 16
LANES = 128
TABLE_LANE = 64
UNITS = 256


def near(value):
    return pltpu.with_memory_space_constraint(value, pltpu.VMEM)


def far(value):
    return pltpu.with_memory_space_constraint(value, pltpu.HBM)


def near_shape(shape, dtype):
    return pltpu.VMEM(shape, dtype)


def partner(value, axis, stride):
    mask = 2**stride
    pairs = [(source, source ^ mask) for source in range(lax.axis_size(axis))]
    return lax.ppermute(value, axis, pairs)


def plan_orders(devices, group_size):
    near_bits = list(range(1, group_size.bit_length() - 1))
    all_bits = list(range(1, devices.bit_length() - 1))
    merge = (near_bits, near_bits[1:] + near_bits[:1])
    rest = [[bit for bit in all_bits if bit != order[-1]] for order in merge]
    gather = (rest[0][::-1], rest[1][2:][::-1] + rest[1][:2])
    scatter = [order[::-1] + kept[-1:] for order, kept in zip(gather, merge)]
    return merge, gather, scatter


def exchange(value, orders, stage):
    pairs = [
        (source, source ^ (1 << orders[source % 2][stage]))
        for source in range(lax.axis_size("wide"))
    ]
    return lax.ppermute(value, "wide", pairs)


def lane_iota(shape):
    return lax.broadcasted_iota(jnp.int32, shape, 1)


def expand_tile(columns, tile, value_size):
    first = tile * LANES // value_size
    last = (tile * LANES + LANES - 1) // value_size
    rows = columns[0].shape[0]
    out = jnp.broadcast_to(columns[first], (rows, LANES))
    for head in range(first + 1, last + 1):
        edge = head * value_size - tile * LANES
        out = jnp.where(lane_iota((rows, LANES)) < edge, out, columns[head])
    return out


def pack_stats(peak, total, head_count):
    lane = lane_iota(peak.shape)
    high = total.astype(jnp.bfloat16).astype(jnp.float32)
    low = total - high
    packed = jnp.where(lane < head_count, peak, 0.0)
    shifted = pltpu.roll(jnp.where(lane < head_count, high, 0.0), head_count, 1)
    shifted_low = pltpu.roll(jnp.where(lane < head_count, low, 0.0), 2 * head_count, 1)
    return packed + shifted + shifted_low


def total_of(stats, head_count):
    return pltpu.roll(stats, LANES - head_count, 1) + pltpu.roll(
        stats, LANES - 2 * head_count, 1
    )


def attend_kernel(
    head_count,
    row_count,
    blocks_ref,
    queries_ref,
    keys_a_ref,
    keys_b_ref,
    values_a_ref,
    values_b_ref,
    sent_ref,
    kept_ref,
    query_scratch,
):
    block_count = blocks_ref.shape[0]
    rows = block_count * row_count
    half = rows // 2
    vision_width = queries_ref.shape[1]
    model_width = values_a_ref.shape[1]
    key_size = vision_width // head_count
    value_size = model_width // head_count
    scale = key_size ** (-0.5)
    for slot in range(block_count):
        start = pl.multiple_of(blocks_ref[slot] * row_count, row_count)
        query_scratch[slot * row_count : (slot + 1) * row_count, :] = queries_ref[
            pl.ds(start, row_count), :
        ]
    peaks = jnp.zeros((rows, LANES), jnp.float32)
    totals = jnp.zeros((rows, LANES), jnp.float32)
    lane = lane_iota((rows, LANES))
    contract_last = (((1,), (1,)), ((), ()))
    contract_rows = (((1,), (0,)), ((), ()))
    waiting = None

    def put(tile, value):
        columns = slice(tile * LANES, (tile + 1) * LANES)
        kept_ref[:, columns] = value[:half]
        sent_ref[:, columns] = value[half:].astype(jnp.bfloat16)

    for head in range(head_count):
        low = head * key_size // LANES * LANES
        high = -(-(head + 1) * key_size // LANES) * LANES
        window = lane_iota((rows, high - low)) + low
        inside = (window >= head * key_size) & (window < (head + 1) * key_size)
        query = jnp.where(inside, query_scratch[:, low:high], jnp.zeros((), jnp.bfloat16))
        score_a = scale * lax.dot_general(
            query, keys_a_ref[:, low:high], contract_last, preferred_element_type=jnp.float32
        )
        score_b = scale * lax.dot_general(
            query, keys_b_ref[:, low:high], contract_last, preferred_element_type=jnp.float32
        )
        peak = jnp.maximum(
            jnp.max(score_a, axis=1, keepdims=True), jnp.max(score_b, axis=1, keepdims=True)
        )
        peak = peak.astype(jnp.bfloat16).astype(jnp.float32)
        raised_a = jnp.exp(score_a - peak)
        raised_b = jnp.exp(score_b - peak)
        total = jnp.sum(raised_a, axis=1, keepdims=True) + jnp.sum(
            raised_b, axis=1, keepdims=True
        )
        peaks = jnp.where(lane == head, peak, peaks)
        totals = jnp.where(lane == head, total, totals)
        low = head * value_size // LANES
        high = -(-(head + 1) * value_size // LANES)
        summed = lax.dot_general(
            raised_a.astype(jnp.bfloat16),
            values_a_ref[:, low * LANES : high * LANES],
            contract_rows,
            preferred_element_type=jnp.float32,
        ) + lax.dot_general(
            raised_b.astype(jnp.bfloat16),
            values_b_ref[:, low * LANES : high * LANES],
            contract_rows,
            preferred_element_type=jnp.float32,
        )
        for tile in range(low, high):
            value = summed[:, (tile - low) * LANES : (tile - low + 1) * LANES]
            edge = head * value_size - tile * LANES
            if edge > 0:
                value = jnp.where(lane < edge, waiting, value)
            if (tile + 1) * LANES > (head + 1) * value_size:
                waiting = value
            else:
                put(tile, value)
    put(model_width // LANES, pack_stats(peaks, totals, head_count))


def merged_parts(kept_ref, came_ref, head_count, model_width):
    stats_a = kept_ref[:, model_width:]
    stats_b = came_ref[:, model_width:].astype(jnp.float32)
    peak = jnp.maximum(stats_a, stats_b)
    factor_a = jnp.exp(stats_a - peak)
    factor_b = jnp.exp(stats_b - peak)
    total = total_of(stats_a, head_count) * factor_a + total_of(stats_b, head_count) * factor_b
    return peak, total, factor_a, factor_b


def head_columns(array, head_count):
    return [array[:, head : head + 1] for head in range(head_count)]


def merge_kernel(head_count, kept_ref, came_ref, sent_ref, next_ref):
    model_width = kept_ref.shape[1] - LANES
    half = kept_ref.shape[0] // 2
    peak, total, factor_a, factor_b = merged_parts(kept_ref, came_ref, head_count, model_width)
    columns_a = head_columns(factor_a, head_count)
    columns_b = head_columns(factor_b, head_count)
    for tile in range(model_width // LANES + 1):
        columns = slice(tile * LANES, (tile + 1) * LANES)
        if tile * LANES == model_width:
            value = pack_stats(peak, total, head_count)
        else:
            value = kept_ref[:, columns] * expand_tile(
                columns_a, tile, model_width // head_count
            ) + came_ref[:, columns].astype(jnp.float32) * expand_tile(
                columns_b, tile, model_width // head_count
            )
        next_ref[:, columns] = value[:half]
        sent_ref[:, columns] = value[half:].astype(jnp.bfloat16)


def last_merge_kernel(head_count, kept_ref, came_ref, table_ref, sent_ref, next_ref):
    model_width = kept_ref.shape[1] - LANES
    half = kept_ref.shape[0] // 2
    peak, total, factor_a, factor_b = merged_parts(kept_ref, came_ref, head_count, model_width)
    columns_a = head_columns(factor_a, head_count)
    columns_b = head_columns(factor_b, head_count)
    for tile in range(model_width // LANES + 1):
        columns = slice(tile * LANES, (tile + 1) * LANES)
        if tile * LANES == model_width:
            value = pack_stats(peak, total, head_count)
            own = value[:half] + table_ref[...].astype(jnp.float32)
        else:
            value = kept_ref[:, columns] * expand_tile(
                columns_a, tile, model_width // head_count
            ) + came_ref[:, columns].astype(jnp.float32) * expand_tile(
                columns_b, tile, model_width // head_count
            )
            own = value[:half]
        next_ref[:, columns] = value
        sent_ref[:half, columns] = value[half:].astype(jnp.bfloat16)
        sent_ref[half:, columns] = own.astype(jnp.bfloat16)


def finish_kernel(head_count, kept_ref, came_ref, gain_ref, table_ref, block_ref, projected_ref):
    model_width = kept_ref.shape[1] - LANES
    half = kept_ref.shape[0] // 2
    _, total, factor_a, factor_b = merged_parts(kept_ref, came_ref, head_count, model_width)
    columns_a = head_columns(factor_a / total, head_count)
    columns_b = head_columns(factor_b / total, head_count)
    square = jnp.zeros((kept_ref.shape[0], LANES), jnp.float32)
    for tile in range(model_width // LANES):
        columns = slice(tile * LANES, (tile + 1) * LANES)
        value = kept_ref[:, columns] * expand_tile(
            columns_a, tile, model_width // head_count
        ) + came_ref[:, columns].astype(jnp.float32) * expand_tile(
            columns_b, tile, model_width // head_count
        )
        rounded = value.astype(jnp.bfloat16)
        block_ref[:, columns] = rounded
        projected_ref[:, columns] = rounded[:half]
        residual = rounded.astype(jnp.float32)
        square = square + residual * residual
    mean = jnp.sum(square, axis=1, keepdims=True) / model_width
    inverse = lax.rsqrt(mean + 1e-06)
    normed = block_ref[:, :model_width].astype(jnp.float32) * inverse * gain_ref[...]
    block_ref[:, :model_width] = normed.astype(jnp.bfloat16)
    came_table = came_ref[half:, model_width:]
    lane = lane_iota(came_table.shape)
    block_ref[:half, model_width:] = table_ref[...]
    block_ref[half:, model_width:] = jnp.where(
        lane >= TABLE_LANE, came_table.astype(jnp.float32), 0.0
    ).astype(jnp.bfloat16)


def expert_math(expert_ref, rows_ref, gate_ref, up_ref, down_ref, out_ref, turned, hidden, ready):
    model_width = out_ref.shape[1]
    for low in range(0, rows_ref.shape[1], LANES):
        turned[low : low + LANES, :] = rows_ref[:, low : low + LANES].T
    scores = turned[model_width:, :].astype(jnp.float32)
    lane = lax.broadcasted_iota(jnp.int32, scores.shape, 0)
    chosen = jnp.where(lane == expert_ref[0] + TABLE_LANE, scores, 0.0)
    share = jnp.sum(chosen, axis=0, keepdims=True) / jnp.sum(scores, axis=0, keepdims=True)
    rows = turned[:model_width, :]
    for chunk in range(gate_ref.shape[0] // UNITS):
        ready(chunk)
        units = slice(chunk * UNITS, (chunk + 1) * UNITS)
        gate_part = jnp.dot(gate_ref[units, :], rows, preferred_element_type=jnp.float32)
        up_part = jnp.dot(up_ref[units, :], rows, preferred_element_type=jnp.float32)
        silu = gate_part / (1.0 + jnp.exp(-gate_part))
        hidden[:, units] = (silu * up_part * share).T.astype(jnp.bfloat16)
    ready(None)
    for low in range(0, model_width, 4 * LANES):
        columns = slice(low, low + 4 * LANES)
        out_ref[:, columns] = jnp.dot(
            hidden[...], down_ref[:, columns], preferred_element_type=jnp.float32
        ).astype(out_ref.dtype)


def first_expert_kernel(
    expert_ref,
    rows_ref,
    gate_a,
    gate_b,
    up_a,
    up_b,
    down_a,
    down_b,
    out_ref,
    gate_ref,
    up_ref,
    down_ref,
    turned,
    hidden,
    arrived,
):
    per_half = gate_a.shape[0] // UNITS
    chunks = 2 * per_half

    def copy_of(part, chunk):
        pair, target = ((gate_a, gate_b), (up_a, up_b), (down_a, down_b))[part], (
            gate_ref,
            up_ref,
            down_ref,
        )[part]
        low = chunk % per_half * UNITS
        return pltpu.make_async_copy(
            pair[chunk // per_half].at[low : low + UNITS, :],
            target.at[chunk * UNITS : (chunk + 1) * UNITS, :],
            arrived.at[part, chunk],
        )

    for chunk in range(chunks):
        for part in range(2):
            copy_of(part, chunk).start()
    for chunk in range(chunks):
        copy_of(2, chunk).start()

    def ready(chunk):
        if chunk is None:
            for piece in range(chunks):
                copy_of(2, piece).wait()
        else:
            copy_of(0, chunk).wait()
            copy_of(1, chunk).wait()

    expert_math(
        expert_ref, rows_ref, gate_ref, up_ref, down_ref, out_ref, turned, hidden, ready
    )


def second_expert_kernel(
    expert_ref, rows_ref, gate_ref, up_ref, down_ref, out_ref, turned, hidden
):
    expert_math(
        expert_ref,
        rows_ref,
        gate_ref,
        up_ref,
        down_ref,
        out_ref,
        turned,
        hidden,
        lambda chunk: None,
    )


def first_expert_rows(expert, rows, weights):
    units, model_width = weights[0].shape
    row_count, packed_width = rows.shape
    whole = pl.BlockSpec(memory_space=pltpu.VMEM)
    anywhere = pl.BlockSpec(memory_space=pltpu.HBM)
    chunks = 2 * units // UNITS
    return pl.pallas_call(
        first_expert_kernel,
        name="expert_first",
        compiler_params=pltpu.CompilerParams(vmem_limit_bytes=12 << 20),
        out_shape=(near_shape((row_count, model_width), jnp.float32),)
        + (near_shape((2 * units, model_width), jnp.bfloat16),) * 3,
        in_specs=[pl.BlockSpec(memory_space=pltpu.SMEM), whole] + [anywhere] * 6,
        out_specs=(whole,) * 4,
        scratch_shapes=[
            pltpu.VMEM((packed_width, row_count), jnp.bfloat16),
            pltpu.VMEM((row_count, 2 * units), jnp.bfloat16),
            pltpu.SemaphoreType.DMA((3, chunks)),
        ],
        cost_estimate=pl.CostEstimate(
            flops=12 * row_count * model_width * units,
            transcendentals=0,
            bytes_accessed=12 * units * model_width,
        ),
    )(expert, near(rows), *[far(weight) for weight in weights])


def second_expert_rows(expert, rows, weights):
    units, model_width = weights[0].shape
    row_count, packed_width = rows.shape
    whole = pl.BlockSpec(memory_space=pltpu.VMEM)
    return pl.pallas_call(
        second_expert_kernel,
        name="expert_second",
        compiler_params=pltpu.CompilerParams(vmem_limit_bytes=12 << 20),
        out_shape=near_shape((row_count, model_width), jnp.bfloat16),
        in_specs=[pl.BlockSpec(memory_space=pltpu.SMEM)] + [whole] * 4,
        out_specs=whole,
        scratch_shapes=[
            pltpu.VMEM((packed_width, row_count), jnp.bfloat16),
            pltpu.VMEM((row_count, units), jnp.bfloat16),
        ],
    )(expert, near(rows), *[near(weight) for weight in weights])


def attention_rows(
    queries, patch_keys, patch_values, other_keys, other_values, norm_gain, table, row_count, orders
):
    model_width = patch_values.shape[1]
    packed_width = model_width + LANES
    group_size = queries.shape[0] // row_count
    stages = len(orders[0])
    device_index = lax.axis_index("wide")
    masks = [
        [
            sum(
                (1 << order[stage])
                for stage in range(stages)
                if slot >> (stages - 1 - stage) & 1
            )
            for slot in range(1 << stages)
        ]
        for order in orders
    ]
    masks = jnp.array(masks, jnp.int32)
    blocks = (device_index % group_size) ^ jnp.where(device_index % 2 == 1, masks[1], masks[0])
    rows = row_count << stages
    whole = pl.BlockSpec(memory_space=pltpu.VMEM)

    def pair_shapes(rows):
        return (
            near_shape((rows, packed_width), jnp.bfloat16),
            near_shape((rows, packed_width), jnp.float32),
        )

    sent, kept = pl.pallas_call(
        functools.partial(attend_kernel, HEADS, row_count),
        name="attend",
        compiler_params=pltpu.CompilerParams(vmem_limit_bytes=12 << 20),
        out_shape=pair_shapes(rows // 2),
        in_specs=[pl.BlockSpec(memory_space=pltpu.SMEM)] + [whole] * 5,
        out_specs=(whole, whole),
        scratch_shapes=[pltpu.VMEM((rows, queries.shape[1]), jnp.bfloat16)],
    )(
        blocks,
        far(queries),
        far(patch_keys),
        near(other_keys),
        far(patch_values),
        near(other_values),
    )
    for stage in range(stages - 1):
        came = exchange(sent, orders, stage)
        rows = kept.shape[0]
        if stage < stages - 2:
            sent, kept = pl.pallas_call(
                functools.partial(merge_kernel, HEADS),
                name="merge",
                compiler_params=pltpu.CompilerParams(vmem_limit_bytes=6 << 20),
                out_shape=pair_shapes(rows // 2),
                in_specs=[whole] * 2,
                out_specs=(whole, whole),
            )(near(kept), near(came))
        else:
            sent, kept = pl.pallas_call(
                functools.partial(last_merge_kernel, HEADS),
                name="last_merge",
                compiler_params=pltpu.CompilerParams(vmem_limit_bytes=6 << 20),
                out_shape=pair_shapes(rows),
                in_specs=[whole] * 3,
                out_specs=(whole, whole),
            )(near(kept), near(came), near(table))
    came = exchange(sent, orders, stages - 1)
    rows = kept.shape[0]
    return pl.pallas_call(
        functools.partial(finish_kernel, HEADS),
        name="finish",
        compiler_params=pltpu.CompilerParams(vmem_limit_bytes=6 << 20),
        out_shape=(
            near_shape((rows, packed_width), jnp.bfloat16),
            near_shape((row_count, model_width), jnp.bfloat16),
        ),
        in_specs=[whole] * 4,
        out_specs=(whole, whole),
    )(near(kept), near(came), near(norm_gain.reshape(1, model_width)), near(table))


def on_device(
    queries, patch_keys, patch_values, norm_gain, route_experts, route_weights, w_gate, w_up, w_down
):
    row_count = route_experts.shape[0]
    devices = lax.axis_size("wide")
    device_index = lax.axis_index("wide")
    score_table = jnp.sum(
        jnp.where(
            route_experts[:, :, None] == jnp.arange(-TABLE_LANE, LANES - TABLE_LANE, dtype=jnp.int32),
            route_weights[:, :, None],
            0,
        ),
        axis=1,
    ).astype(jnp.bfloat16)
    merge_order, gather_order, scatter_order = plan_orders(
        devices, queries.shape[0] // row_count
    )
    other_keys = partner(patch_keys, "wide", 0)
    other_values = partner(patch_values, "wide", 0)
    halves, other_keys, other_values = lax.optimization_barrier(
        ((w_gate, w_up, w_down), other_keys, other_values)
    )
    weights = []
    for own in halves:
        weights += [own, partner(own, "wide", 0)]
    block, projected = attention_rows(
        queries,
        patch_keys,
        patch_values,
        other_keys,
        other_values,
        norm_gain,
        score_table,
        row_count,
        merge_order,
    )
    stages = len(gather_order[0])
    for stage in range(stages - 1):
        block = jnp.concatenate([block, exchange(block, gather_order, stage)], axis=0)
    came = exchange(block, gather_order, stages - 1)
    expert = (device_index // 2).reshape(1)
    total, *weights = first_expert_rows(expert, block, weights)
    sent = second_expert_rows(expert, came, weights)
    total = total + exchange(sent, scatter_order, 0).astype(jnp.float32)
    for stage in range(1, len(scatter_order[0])):
        half_rows = total.shape[0] // 2
        total = total[:half_rows] + exchange(
            total[half_rows:].astype(jnp.bfloat16), scatter_order, stage
        ).astype(jnp.float32)
    return (projected.astype(jnp.float32) + total).astype(jnp.bfloat16)


def solution(mesh):
    return mapped(mesh)


def mapped(mesh):
    return jax.shard_map(
        on_device,
        mesh=mesh,
        in_specs=(
            P("groups", None),
            P(("groups", "wide"), None),
            P(("groups", "wide"), None),
            P(),
            P(("groups", "wide"), None),
            P(("groups", "wide"), None),
            P("wide", None),
            P("wide", None),
            P("wide", None),
        ),
        out_specs=P(("groups", "wide"), None),
        check_vma=False,
    )
```

```python
import functools

import jax
import jax.numpy as jnp
from jax import lax
from jax.experimental import pallas as pl
from jax.experimental.pallas import tpu as pltpu
from jax.sharding import PartitionSpec as P


HEADS = 16
LANES = 128
TABLE_LANE = 64
UNITS = 256
PARTS = 2


def near(value):
    return pltpu.with_memory_space_constraint(value, pltpu.VMEM)


def far(value):
    return pltpu.with_memory_space_constraint(value, pltpu.HBM)


def near_shape(shape, dtype):
    return pltpu.VMEM(shape, dtype)


def partner(value, axis, stride):
    mask = 2**stride
    pairs = [(source, source ^ mask) for source in range(lax.axis_size(axis))]
    return lax.ppermute(value, axis, pairs)


def plan_orders(devices, group_size):
    near_bits = list(range(1, group_size.bit_length() - 1))
    all_bits = list(range(1, devices.bit_length() - 1))
    merge = (near_bits, near_bits[1:] + near_bits[:1])
    rest = [[bit for bit in all_bits if bit != order[-1]] for order in merge]
    gather = (rest[0][::-1], rest[1][2:][::-1] + rest[1][:2])
    scatter = [order[::-1] + kept[-1:] for order, kept in zip(gather, merge)]
    return merge, gather, scatter


def exchange(value, orders, stage):
    pairs = [
        (source, source ^ (1 << orders[source % 2][stage]))
        for source in range(lax.axis_size("wide"))
    ]
    return lax.ppermute(value, "wide", pairs)


def lane_iota(shape):
    return lax.broadcasted_iota(jnp.int32, shape, 1)


def expand_tile(columns, tile, value_size):
    first = tile * LANES // value_size
    last = (tile * LANES + LANES - 1) // value_size
    rows = columns[0].shape[0]
    out = jnp.broadcast_to(columns[first], (rows, LANES))
    for head in range(first + 1, last + 1):
        edge = head * value_size - tile * LANES
        out = jnp.where(lane_iota((rows, LANES)) < edge, out, columns[head])
    return out


def pack_stats(peak, total, head_count):
    lane = lane_iota(peak.shape)
    high = total.astype(jnp.bfloat16).astype(jnp.float32)
    low = total - high
    packed = jnp.where(lane < head_count, peak, 0.0)
    shifted = pltpu.roll(jnp.where(lane < head_count, high, 0.0), head_count, 1)
    shifted_low = pltpu.roll(jnp.where(lane < head_count, low, 0.0), 2 * head_count, 1)
    return packed + shifted + shifted_low


def total_of(stats, head_count):
    return pltpu.roll(stats, LANES - head_count, 1) + pltpu.roll(
        stats, LANES - 2 * head_count, 1
    )


def attend_kernel(
    head_count,
    row_count,
    blocks_ref,
    queries_ref,
    keys_a_ref,
    keys_b_ref,
    values_a_ref,
    values_b_ref,
    *rest,
):
    outputs, query_scratch = rest[:-1], rest[-1]
    parts = len(outputs) // 2
    part_heads = head_count // parts
    block_count = blocks_ref.shape[0]
    rows = block_count * row_count
    half = rows // 2
    vision_width = queries_ref.shape[1]
    model_width = values_a_ref.shape[1]
    key_size = vision_width // head_count
    value_size = model_width // head_count
    scale = key_size ** (-0.5)
    for slot in range(block_count):
        start = pl.multiple_of(blocks_ref[slot] * row_count, row_count)
        query_scratch[slot * row_count : (slot + 1) * row_count, :] = queries_ref[
            pl.ds(start, row_count), :
        ]
    lane = lane_iota((rows, LANES))
    contract_last = (((1,), (1,)), ((), ()))
    contract_rows = (((1,), (0,)), ((), ()))
    waiting = None

    def put(part, tile, value):
        columns = slice(tile * LANES, (tile + 1) * LANES)
        outputs[2 * part + 1][:, columns] = value[:half]
        outputs[2 * part][:, columns] = value[half:].astype(jnp.bfloat16)

    for head in range(head_count):
        part = head // part_heads
        part_tiles = model_width // parts // LANES
        if head % part_heads == 0:
            peaks = jnp.zeros((rows, LANES), jnp.float32)
            totals = jnp.zeros((rows, LANES), jnp.float32)
        low = head * key_size // LANES * LANES
        high = -(-(head + 1) * key_size // LANES) * LANES
        window = lane_iota((rows, high - low)) + low
        inside = (window >= head * key_size) & (window < (head + 1) * key_size)
        query = jnp.where(inside, query_scratch[:, low:high], jnp.zeros((), jnp.bfloat16))
        score_a = scale * lax.dot_general(
            query, keys_a_ref[:, low:high], contract_last, preferred_element_type=jnp.float32
        )
        score_b = scale * lax.dot_general(
            query, keys_b_ref[:, low:high], contract_last, preferred_element_type=jnp.float32
        )
        peak = jnp.maximum(
            jnp.max(score_a, axis=1, keepdims=True), jnp.max(score_b, axis=1, keepdims=True)
        )
        peak = peak.astype(jnp.bfloat16).astype(jnp.float32)
        raised_a = jnp.exp(score_a - peak)
        raised_b = jnp.exp(score_b - peak)
        total = jnp.sum(raised_a, axis=1, keepdims=True) + jnp.sum(
            raised_b, axis=1, keepdims=True
        )
        peaks = jnp.where(lane == head % part_heads, peak, peaks)
        totals = jnp.where(lane == head % part_heads, total, totals)
        low = head * value_size // LANES
        high = -(-(head + 1) * value_size // LANES)
        summed = lax.dot_general(
            raised_a.astype(jnp.bfloat16),
            values_a_ref[:, low * LANES : high * LANES],
            contract_rows,
            preferred_element_type=jnp.float32,
        ) + lax.dot_general(
            raised_b.astype(jnp.bfloat16),
            values_b_ref[:, low * LANES : high * LANES],
            contract_rows,
            preferred_element_type=jnp.float32,
        )
        for tile in range(low, high):
            value = summed[:, (tile - low) * LANES : (tile - low + 1) * LANES]
            edge = head * value_size - tile * LANES
            if edge > 0:
                value = jnp.where(lane < edge, waiting, value)
            if (tile + 1) * LANES > (head + 1) * value_size:
                waiting = value
            else:
                put(part, tile - part * part_tiles, value)
        if (head + 1) % part_heads == 0:
            put(part, part_tiles, pack_stats(peaks, totals, part_heads))


def merged_parts(kept_ref, came_ref, head_count, model_width):
    stats_a = kept_ref[:, model_width:]
    stats_b = came_ref[:, model_width:].astype(jnp.float32)
    peak = jnp.maximum(stats_a, stats_b)
    factor_a = jnp.exp(stats_a - peak)
    factor_b = jnp.exp(stats_b - peak)
    total = total_of(stats_a, head_count) * factor_a + total_of(stats_b, head_count) * factor_b
    return peak, total, factor_a, factor_b


def head_columns(array, head_count):
    return [array[:, head : head + 1] for head in range(head_count)]


def merge_kernel(head_count, kept_ref, came_ref, sent_ref, next_ref):
    model_width = kept_ref.shape[1] - LANES
    half = kept_ref.shape[0] // 2
    peak, total, factor_a, factor_b = merged_parts(kept_ref, came_ref, head_count, model_width)
    columns_a = head_columns(factor_a, head_count)
    columns_b = head_columns(factor_b, head_count)
    for tile in range(model_width // LANES + 1):
        columns = slice(tile * LANES, (tile + 1) * LANES)
        if tile * LANES == model_width:
            value = pack_stats(peak, total, head_count)
        else:
            value = kept_ref[:, columns] * expand_tile(
                columns_a, tile, model_width // head_count
            ) + came_ref[:, columns].astype(jnp.float32) * expand_tile(
                columns_b, tile, model_width // head_count
            )
        next_ref[:, columns] = value[:half]
        sent_ref[:, columns] = value[half:].astype(jnp.bfloat16)


def last_merge_kernel(head_count, kept_ref, came_ref, *rest):
    tables, (sent_ref, next_ref) = rest[:-2], rest[-2:]
    model_width = kept_ref.shape[1] - LANES
    half = kept_ref.shape[0] // 2
    peak, total, factor_a, factor_b = merged_parts(kept_ref, came_ref, head_count, model_width)
    columns_a = head_columns(factor_a, head_count)
    columns_b = head_columns(factor_b, head_count)
    for tile in range(model_width // LANES + 1):
        columns = slice(tile * LANES, (tile + 1) * LANES)
        if tile * LANES == model_width:
            value = pack_stats(peak, total, head_count)
            own = value[:half]
            for table_ref in tables:
                own = own + table_ref[...].astype(jnp.float32)
        else:
            value = kept_ref[:, columns] * expand_tile(
                columns_a, tile, model_width // head_count
            ) + came_ref[:, columns].astype(jnp.float32) * expand_tile(
                columns_b, tile, model_width // head_count
            )
            own = value[:half]
        next_ref[:, columns] = value
        sent_ref[:half, columns] = value[half:].astype(jnp.bfloat16)
        sent_ref[half:, columns] = own.astype(jnp.bfloat16)


def finish_kernel(head_count, gain_ref, table_ref, *rest):
    parts = (len(rest) - 1) // 3
    pairs, blocks, projected_ref = rest[: 2 * parts], rest[2 * parts : 3 * parts], rest[-1]
    part_heads = head_count // parts
    rows = pairs[0].shape[0]
    half = rows // 2
    width = pairs[0].shape[1] - LANES
    square = jnp.zeros((rows, LANES), jnp.float32)
    for part in range(parts):
        kept_ref, came_ref = pairs[2 * part : 2 * part + 2]
        _, total, factor_a, factor_b = merged_parts(kept_ref, came_ref, part_heads, width)
        columns_a = head_columns(factor_a / total, part_heads)
        columns_b = head_columns(factor_b / total, part_heads)
        for tile in range(width // LANES):
            columns = slice(tile * LANES, (tile + 1) * LANES)
            value = kept_ref[:, columns] * expand_tile(
                columns_a, tile, width // part_heads
            ) + came_ref[:, columns].astype(jnp.float32) * expand_tile(
                columns_b, tile, width // part_heads
            )
            rounded = value.astype(jnp.bfloat16)
            blocks[part][:, columns] = rounded
            low = part * width + tile * LANES
            projected_ref[:, low : low + LANES] = rounded[:half]
            residual = rounded.astype(jnp.float32)
            square = square + residual * residual
    mean = jnp.sum(square, axis=1, keepdims=True) / (parts * width)
    inverse = lax.rsqrt(mean + 1e-06)
    for part in range(parts):
        gain = gain_ref[:, part * width : (part + 1) * width]
        normed = blocks[part][:, :width].astype(jnp.float32) * inverse * gain
        blocks[part][:, :width] = normed.astype(jnp.bfloat16)
    came_table = pairs[1][half:, width:]
    lane = lane_iota(came_table.shape)
    blocks[0][:half, width:] = table_ref[...]
    blocks[0][half:, width:] = jnp.where(
        lane >= TABLE_LANE, came_table.astype(jnp.float32), 0.0
    ).astype(jnp.bfloat16)


def hidden_units(expert_ref, row_refs, gate_ref, up_ref, turned, hidden, ready):
    width = row_refs[1].shape[1]
    model_width = width * len(row_refs)
    for part, rows_ref in enumerate(row_refs):
        for low in range(0, width, LANES):
            at = part * width + low
            turned[at : at + LANES, :] = rows_ref[:, low : low + LANES].T
    turned[model_width:, :] = row_refs[0][:, width:].T
    scores = turned[model_width:, :].astype(jnp.float32)
    lane = lax.broadcasted_iota(jnp.int32, scores.shape, 0)
    chosen = jnp.where(lane == expert_ref[0] + TABLE_LANE, scores, 0.0)
    share = jnp.sum(chosen, axis=0, keepdims=True) / jnp.sum(scores, axis=0, keepdims=True)
    rows = turned[:model_width, :]
    for chunk in range(gate_ref.shape[0] // UNITS):
        ready(chunk)
        units = slice(chunk * UNITS, (chunk + 1) * UNITS)
        gate_part = jnp.dot(gate_ref[units, :], rows, preferred_element_type=jnp.float32)
        up_part = jnp.dot(up_ref[units, :], rows, preferred_element_type=jnp.float32)
        silu = gate_part / (1.0 + jnp.exp(-gate_part))
        hidden[:, units] = (silu * up_part * share).T.astype(jnp.bfloat16)


def down_product(hidden_ref, down_ref, out_ref, start):
    width = out_ref.shape[1]
    step = width // 2 if width % (4 * LANES) else 4 * LANES
    for low in range(0, width, step):
        out_ref[:, low : low + step] = jnp.dot(
            hidden_ref[...],
            down_ref[:, start + low : start + low + step],
            preferred_element_type=jnp.float32,
        ).astype(out_ref.dtype)


def first_expert_kernel(
    expert_ref,
    rows_a,
    rows_b,
    gate_a,
    gate_b,
    up_a,
    up_b,
    down_a,
    down_b,
    out_a,
    out_b,
    gate_ref,
    up_ref,
    down_ref,
    turned,
    hidden,
    arrived,
):
    per_half = gate_a.shape[0] // UNITS
    chunks = 2 * per_half
    pairs = ((gate_a, gate_b), (up_a, up_b), (down_a, down_b))
    targets = (gate_ref, up_ref, down_ref)

    def copy_of(part, chunk):
        low = chunk % per_half * UNITS
        return pltpu.make_async_copy(
            pairs[part][chunk // per_half].at[low : low + UNITS, :],
            targets[part].at[chunk * UNITS : (chunk + 1) * UNITS, :],
            arrived.at[part, chunk],
        )

    for chunk in range(chunks):
        for part in range(2):
            copy_of(part, chunk).start()
    for chunk in range(chunks):
        copy_of(2, chunk).start()

    def ready(chunk):
        copy_of(0, chunk).wait()
        copy_of(1, chunk).wait()

    hidden_units(expert_ref, (rows_a, rows_b), gate_ref, up_ref, turned, hidden, ready)
    for chunk in range(chunks):
        copy_of(2, chunk).wait()
    down_product(hidden, down_ref, out_a, 0)
    down_product(hidden, down_ref, out_b, out_a.shape[1])


def second_expert_kernel(
    expert_ref, rows_a, rows_b, gate_ref, up_ref, down_ref, out_ref, hidden, turned
):
    hidden_units(
        expert_ref, (rows_a, rows_b), gate_ref, up_ref, turned, hidden, lambda chunk: None
    )
    down_product(hidden, down_ref, out_ref, 0)


def rest_expert_kernel(start, hidden_ref, down_ref, out_ref):
    down_product(hidden_ref, down_ref, out_ref, start)


def first_expert_rows(expert, halves, weights):
    units, model_width = weights[0].shape
    row_count = halves[0].shape[0]
    whole = pl.BlockSpec(memory_space=pltpu.VMEM)
    anywhere = pl.BlockSpec(memory_space=pltpu.HBM)
    chunks = 2 * units // UNITS
    return pl.pallas_call(
        first_expert_kernel,
        name="expert_first",
        compiler_params=pltpu.CompilerParams(vmem_limit_bytes=12 << 20),
        out_shape=(near_shape((row_count, model_width // 2), jnp.float32),) * 2
        + (near_shape((2 * units, model_width), jnp.bfloat16),) * 3,
        in_specs=[pl.BlockSpec(memory_space=pltpu.SMEM)] + [whole] * 2 + [anywhere] * 6,
        out_specs=(whole,) * 5,
        scratch_shapes=[
            pltpu.VMEM((model_width + LANES, row_count), jnp.bfloat16),
            pltpu.VMEM((row_count, 2 * units), jnp.bfloat16),
            pltpu.SemaphoreType.DMA((3, chunks)),
        ],
        cost_estimate=pl.CostEstimate(
            flops=12 * row_count * model_width * units,
            transcendentals=0,
            bytes_accessed=12 * units * model_width,
        ),
    )(expert, *[near(half) for half in halves], *[far(weight) for weight in weights])


def second_expert_rows(expert, halves, weights):
    units, model_width = weights[0].shape
    row_count = halves[0].shape[0]
    width = model_width // 2
    whole = pl.BlockSpec(memory_space=pltpu.VMEM)
    first, hidden = pl.pallas_call(
        second_expert_kernel,
        name="expert_second",
        compiler_params=pltpu.CompilerParams(vmem_limit_bytes=12 << 20),
        out_shape=(
            near_shape((row_count, width), jnp.bfloat16),
            near_shape((row_count, units), jnp.bfloat16),
        ),
        in_specs=[pl.BlockSpec(memory_space=pltpu.SMEM)] + [whole] * 5,
        out_specs=(whole, whole),
        scratch_shapes=[pltpu.VMEM((model_width + LANES, row_count), jnp.bfloat16)],
    )(expert, *[near(half) for half in halves], *[near(weight) for weight in weights])
    second = pl.pallas_call(
        functools.partial(rest_expert_kernel, width),
        name="expert_rest",
        compiler_params=pltpu.CompilerParams(vmem_limit_bytes=12 << 20),
        out_shape=near_shape((row_count, width), jnp.bfloat16),
        in_specs=[whole] * 2,
        out_specs=whole,
    )(near(hidden), near(weights[2]))
    return [first, second]


def attention_rows(
    queries, patch_keys, patch_values, other_keys, other_values, norm_gain, table, row_count, orders
):
    model_width = patch_values.shape[1]
    part_width = model_width // PARTS + LANES
    part_heads = HEADS // PARTS
    group_size = queries.shape[0] // row_count
    stages = len(orders[0])
    device_index = lax.axis_index("wide")
    masks = [
        [
            sum(
                (1 << order[stage])
                for stage in range(stages)
                if slot >> (stages - 1 - stage) & 1
            )
            for slot in range(1 << stages)
        ]
        for order in orders
    ]
    masks = jnp.array(masks, jnp.int32)
    blocks = (device_index % group_size) ^ jnp.where(device_index % 2 == 1, masks[1], masks[0])
    rows = row_count << stages
    whole = pl.BlockSpec(memory_space=pltpu.VMEM)

    def pair_shapes(rows):
        return (
            near_shape((rows, part_width), jnp.bfloat16),
            near_shape((rows, part_width), jnp.float32),
        )

    chains = pl.pallas_call(
        functools.partial(attend_kernel, HEADS, row_count),
        name="attend",
        compiler_params=pltpu.CompilerParams(vmem_limit_bytes=12 << 20),
        out_shape=pair_shapes(rows // 2) * PARTS,
        in_specs=[pl.BlockSpec(memory_space=pltpu.SMEM)] + [whole] * 5,
        out_specs=(whole,) * (2 * PARTS),
        scratch_shapes=[pltpu.VMEM((rows, queries.shape[1]), jnp.bfloat16)],
    )(
        blocks,
        far(queries),
        far(patch_keys),
        near(other_keys),
        far(patch_values),
        near(other_values),
    )
    finished = []
    for part in range(PARTS):
        sent, kept = chains[2 * part : 2 * part + 2]
        for stage in range(stages - 1):
            came = exchange(sent, orders, stage)
            rows = kept.shape[0]
            last = stage == stages - 2
            operands = [near(kept), near(came)]
            if last and part == 0:
                operands.append(near(table))
            sent, kept = pl.pallas_call(
                functools.partial(last_merge_kernel if last else merge_kernel, part_heads),
                compiler_params=pltpu.CompilerParams(vmem_limit_bytes=6 << 20),
                out_shape=pair_shapes(rows if last else rows // 2),
                in_specs=[whole] * len(operands),
                out_specs=(whole, whole),
            )(*operands)
        came = exchange(sent, orders, stages - 1)
        finished += [near(kept), near(came)]
    rows = kept.shape[0]
    *blocks, projected = pl.pallas_call(
        functools.partial(finish_kernel, HEADS),
        name="finish",
        compiler_params=pltpu.CompilerParams(vmem_limit_bytes=6 << 20),
        out_shape=tuple(
            near_shape((rows, model_width // PARTS + (LANES if part == 0 else 0)), jnp.bfloat16)
            for part in range(PARTS)
        )
        + (near_shape((row_count, model_width), jnp.bfloat16),),
        in_specs=[whole] * (2 + 2 * PARTS),
        out_specs=(whole,) * (PARTS + 1),
    )(near(norm_gain.reshape(1, model_width)), near(table), *finished)
    return blocks, projected


def on_device(
    queries, patch_keys, patch_values, norm_gain, route_experts, route_weights, w_gate, w_up, w_down
):
    row_count = route_experts.shape[0]
    devices = lax.axis_size("wide")
    device_index = lax.axis_index("wide")
    score_table = jnp.sum(
        jnp.where(
            route_experts[:, :, None] == jnp.arange(-TABLE_LANE, LANES - TABLE_LANE, dtype=jnp.int32),
            route_weights[:, :, None],
            0,
        ),
        axis=1,
    ).astype(jnp.bfloat16)
    merge_order, gather_order, scatter_order = plan_orders(
        devices, queries.shape[0] // row_count
    )
    other_keys = partner(patch_keys, "wide", 0)
    other_values = partner(patch_values, "wide", 0)
    halves, other_keys, other_values = lax.optimization_barrier(
        ((w_gate, w_up, w_down), other_keys, other_values)
    )
    weights = []
    for own in halves:
        weights += [own, partner(own, "wide", 0)]
    blocks, projected = attention_rows(
        queries,
        patch_keys,
        patch_values,
        other_keys,
        other_values,
        norm_gain,
        score_table,
        row_count,
        merge_order,
    )
    stages = len(gather_order[0])
    came = []
    for part in range(PARTS):
        for stage in range(stages - 1):
            arrived = exchange(blocks[part], gather_order, stage)
            blocks[part] = jnp.concatenate([blocks[part], arrived], axis=0)
        came.append(exchange(blocks[part], gather_order, stages - 1))
    expert = (device_index // 2).reshape(1)
    *totals, gate, up, down = first_expert_rows(expert, blocks, weights)
    outputs = []
    for part, sent in enumerate(second_expert_rows(expert, came, (gate, up, down))):
        kept = totals[part]
        for stage in range(len(scatter_order[0])):
            arrived = exchange(sent, scatter_order, stage)
            kept = kept + arrived.astype(jnp.float32)
            half_rows = kept.shape[0] // 2
            if stage < len(scatter_order[0]) - 1:
                sent = kept[half_rows:].astype(jnp.bfloat16)
                kept = kept[:half_rows]
        outputs.append(kept)
    total = jnp.concatenate(outputs, axis=1)
    return (projected.astype(jnp.float32) + total).astype(jnp.bfloat16)


def solution(mesh):
    return mapped(mesh)


def mapped(mesh):
    return jax.shard_map(
        on_device,
        mesh=mesh,
        in_specs=(
            P("groups", None),
            P(("groups", "wide"), None),
            P(("groups", "wide"), None),
            P(),
            P(("groups", "wide"), None),
            P(("groups", "wide"), None),
            P("wide", None),
            P("wide", None),
            P("wide", None),
        ),
        out_specs=P(("groups", "wide"), None),
        check_vma=False,
    )
```

```python
import functools

import jax
import jax.numpy as jnp
from jax import lax
from jax.experimental import pallas as pl
from jax.experimental.pallas import tpu as pltpu
from jax.sharding import PartitionSpec as P


HEADS = 16
LANES = 128
TABLE_LANE = 64
UNITS = 256
PARTS = 2


def near(value):
    return pltpu.with_memory_space_constraint(value, pltpu.VMEM)


def far(value):
    return pltpu.with_memory_space_constraint(value, pltpu.HBM)


def near_shape(shape, dtype):
    return pltpu.VMEM(shape, dtype)


def partner(value, axis, stride):
    mask = 2**stride
    pairs = [(source, source ^ mask) for source in range(lax.axis_size(axis))]
    return lax.ppermute(value, axis, pairs)


def plan_orders(devices, group_size):
    near_bits = list(range(1, group_size.bit_length() - 1))
    all_bits = list(range(1, devices.bit_length() - 1))
    merge = (near_bits, near_bits[1:] + near_bits[:1])
    rest = [[bit for bit in all_bits if bit != order[-1]] for order in merge]
    gather = (rest[0][::-1], rest[1][2:][::-1] + rest[1][:2])
    scatter = [order[::-1] + kept[-1:] for order, kept in zip(gather, merge)]
    crossed = [order[1::-1] + order[2:] for order in scatter]
    return merge, gather, (scatter, crossed)


def exchange(value, orders, stage):
    pairs = [
        (source, source ^ (1 << orders[source % 2][stage]))
        for source in range(lax.axis_size("wide"))
    ]
    return lax.ppermute(value, "wide", pairs)


def lane_iota(shape):
    return lax.broadcasted_iota(jnp.int32, shape, 1)


def expand_tile(columns, tile, value_size):
    first = tile * LANES // value_size
    last = (tile * LANES + LANES - 1) // value_size
    rows = columns[0].shape[0]
    out = jnp.broadcast_to(columns[first], (rows, LANES))
    for head in range(first + 1, last + 1):
        edge = head * value_size - tile * LANES
        out = jnp.where(lane_iota((rows, LANES)) < edge, out, columns[head])
    return out


def pack_stats(peak, total, head_count):
    lane = lane_iota(peak.shape)
    high = total.astype(jnp.bfloat16).astype(jnp.float32)
    low = total - high
    packed = jnp.where(lane < head_count, peak, 0.0)
    shifted = pltpu.roll(jnp.where(lane < head_count, high, 0.0), head_count, 1)
    shifted_low = pltpu.roll(jnp.where(lane < head_count, low, 0.0), 2 * head_count, 1)
    return packed + shifted + shifted_low


def total_of(stats, head_count):
    return pltpu.roll(stats, LANES - head_count, 1) + pltpu.roll(
        stats, LANES - 2 * head_count, 1
    )


def head_windows(head, size):
    return head * size // LANES, -(-(head + 1) * size // LANES)


def head_scores(head, head_count, query_ref, keys_ref):
    key_size = query_ref.shape[1] // head_count
    low, high = [LANES * tile for tile in head_windows(head, key_size)]
    window = lane_iota((query_ref.shape[0], high - low)) + low
    inside = (window >= head * key_size) & (window < (head + 1) * key_size)
    query = jnp.where(inside, query_ref[:, low:high], jnp.zeros((), jnp.bfloat16))
    return key_size ** (-0.5) * lax.dot_general(
        query,
        keys_ref[:, low:high],
        (((1,), (1,)), ((), ())),
        preferred_element_type=jnp.float32,
    )


def rounded_peak(scores):
    peak = jnp.max(scores, axis=1, keepdims=True)
    return peak.astype(jnp.bfloat16).astype(jnp.float32)


def head_sums(head, value_size, raised, values_ref):
    low, high = head_windows(head, value_size)
    return jnp.dot(
        raised.astype(jnp.bfloat16),
        values_ref[:, low * LANES : high * LANES],
        preferred_element_type=jnp.float32,
    )


def attend_own_kernel(
    head_count, row_count, masks, device_ref, queries_ref, keys_ref, values_ref, query_ref, *parts
):
    group_size = queries_ref.shape[0] // row_count
    device = device_ref[0]
    odd = lax.rem(device, 2) == 1
    own_block = lax.rem(device, group_size)
    for slot, (even_mask, odd_mask) in enumerate(zip(*masks)):
        block = own_block ^ jnp.where(odd, odd_mask, even_mask)
        start = pl.multiple_of(block * row_count, row_count)
        query_ref[slot * row_count : (slot + 1) * row_count, :] = queries_ref[
            pl.ds(start, row_count), :
        ]
    rows = query_ref.shape[0]
    value_size = values_ref.shape[1] // head_count
    part_heads = head_count // len(parts)
    part_tiles = values_ref.shape[1] // len(parts) // LANES
    lane = lane_iota((rows, LANES))
    for head in range(head_count):
        part_ref = parts[head // part_heads]
        base = head // part_heads * part_tiles
        if head % part_heads == 0:
            stats = jnp.zeros((rows, LANES), jnp.float32)
        scores = head_scores(head, head_count, query_ref, keys_ref)
        peak = rounded_peak(scores)
        raised = jnp.exp(scores - peak)
        total = jnp.sum(raised, axis=1, keepdims=True)
        stats = jnp.where(lane == head % part_heads, peak, stats)
        stats = jnp.where(lane == head % part_heads + part_heads, total, stats)
        summed = head_sums(head, value_size, raised, values_ref)
        low, high = head_windows(head, value_size)
        for tile in range(low, high):
            value = summed[:, (tile - low) * LANES : (tile - low + 1) * LANES]
            edge = head * value_size - tile * LANES
            if edge > 0:
                value = jnp.where(lane < edge, waiting, value)
            waiting = value
            if (tile + 1) * LANES <= (head + 1) * value_size:
                part_ref[:, (tile - base) * LANES : (tile - base + 1) * LANES] = value
        if (head + 1) % part_heads == 0:
            part_ref[:, part_tiles * LANES :] = stats


def attend_other_kernel(head_count, query_ref, keys_ref, values_ref, *rest):
    part_count = len(rest) // 3
    parts, outputs = rest[:part_count], rest[part_count:]
    rows = query_ref.shape[0]
    half = rows // 2
    value_size = values_ref.shape[1] // head_count
    part_heads = head_count // part_count
    part_tiles = values_ref.shape[1] // part_count // LANES
    lane = lane_iota((rows, LANES))

    def put(part, tile, value):
        columns = slice(tile * LANES, (tile + 1) * LANES)
        outputs[2 * part + 1][:, columns] = value[:half]
        outputs[2 * part][:, columns] = value[half:].astype(jnp.bfloat16)

    for head in range(head_count):
        part = head // part_heads
        at = head % part_heads
        base = part * part_tiles
        if at == 0:
            stats = parts[part][:, part_tiles * LANES :]
            peaks = jnp.zeros((rows, LANES), jnp.float32)
            totals = jnp.zeros((rows, LANES), jnp.float32)
        scores = head_scores(head, head_count, query_ref, keys_ref)
        old_peak = stats[:, at : at + 1]
        peak = jnp.maximum(rounded_peak(scores), old_peak)
        factor = jnp.exp(old_peak - peak)
        raised = jnp.exp(scores - peak)
        total = jnp.sum(raised, axis=1, keepdims=True)
        total = total + stats[:, part_heads + at : part_heads + at + 1] * factor
        peaks = jnp.where(lane == at, peak, peaks)
        totals = jnp.where(lane == at, total, totals)
        summed = head_sums(head, value_size, raised, values_ref)
        low, high = head_windows(head, value_size)
        for tile in range(low, high):
            value = summed[:, (tile - low) * LANES : (tile - low + 1) * LANES]
            old = parts[part][:, (tile - base) * LANES : (tile - base + 1) * LANES]
            value = value + old * factor
            edge = head * value_size - tile * LANES
            if edge > 0:
                value = jnp.where(lane < edge, waiting, value)
            waiting = value
            if (tile + 1) * LANES <= (head + 1) * value_size:
                put(part, tile - base, value)
        if at == part_heads - 1:
            put(part, part_tiles, pack_stats(peaks, totals, part_heads))


def merged_parts(kept_ref, came_ref, head_count, model_width):
    stats_a = kept_ref[:, model_width:]
    stats_b = came_ref[:, model_width:].astype(jnp.float32)
    peak = jnp.maximum(stats_a, stats_b)
    factor_a = jnp.exp(stats_a - peak)
    factor_b = jnp.exp(stats_b - peak)
    total = total_of(stats_a, head_count) * factor_a + total_of(stats_b, head_count) * factor_b
    return peak, total, factor_a, factor_b


def head_columns(array, head_count):
    return [array[:, head : head + 1] for head in range(head_count)]


def merge_kernel(head_count, kept_ref, came_ref, sent_ref, next_ref):
    model_width = kept_ref.shape[1] - LANES
    half = kept_ref.shape[0] // 2
    peak, total, factor_a, factor_b = merged_parts(kept_ref, came_ref, head_count, model_width)
    columns_a = head_columns(factor_a, head_count)
    columns_b = head_columns(factor_b, head_count)
    for tile in range(model_width // LANES + 1):
        columns = slice(tile * LANES, (tile + 1) * LANES)
        if tile * LANES == model_width:
            value = pack_stats(peak, total, head_count)
        else:
            value = kept_ref[:, columns] * expand_tile(
                columns_a, tile, model_width // head_count
            ) + came_ref[:, columns].astype(jnp.float32) * expand_tile(
                columns_b, tile, model_width // head_count
            )
        next_ref[:, columns] = value[:half]
        sent_ref[:, columns] = value[half:].astype(jnp.bfloat16)


def last_merge_kernel(head_count, kept_ref, came_ref, *rest):
    tables, (sent_ref, next_ref) = rest[:-2], rest[-2:]
    model_width = kept_ref.shape[1] - LANES
    half = kept_ref.shape[0] // 2
    peak, total, factor_a, factor_b = merged_parts(kept_ref, came_ref, head_count, model_width)
    columns_a = head_columns(factor_a, head_count)
    columns_b = head_columns(factor_b, head_count)
    for tile in range(model_width // LANES + 1):
        columns = slice(tile * LANES, (tile + 1) * LANES)
        if tile * LANES == model_width:
            value = pack_stats(peak, total, head_count)
            own = value[:half]
            for table_ref in tables:
                own = own + table_ref[...].astype(jnp.float32)
        else:
            value = kept_ref[:, columns] * expand_tile(
                columns_a, tile, model_width // head_count
            ) + came_ref[:, columns].astype(jnp.float32) * expand_tile(
                columns_b, tile, model_width // head_count
            )
            own = value[:half]
        next_ref[:, columns] = value
        sent_ref[:half, columns] = value[half:].astype(jnp.bfloat16)
        sent_ref[half:, columns] = own.astype(jnp.bfloat16)


def finish_kernel(head_count, gain_ref, table_ref, *rest):
    parts = (len(rest) - 1) // 3
    pairs, blocks, projected_ref = rest[: 2 * parts], rest[2 * parts : 3 * parts], rest[-1]
    part_heads = head_count // parts
    rows = pairs[0].shape[0]
    half = rows // 2
    width = pairs[0].shape[1] - LANES
    square = jnp.zeros((rows, LANES), jnp.float32)
    for part in range(parts):
        kept_ref, came_ref = pairs[2 * part : 2 * part + 2]
        _, total, factor_a, factor_b = merged_parts(kept_ref, came_ref, part_heads, width)
        columns_a = head_columns(factor_a / total, part_heads)
        columns_b = head_columns(factor_b / total, part_heads)
        for tile in range(width // LANES):
            columns = slice(tile * LANES, (tile + 1) * LANES)
            value = kept_ref[:, columns] * expand_tile(
                columns_a, tile, width // part_heads
            ) + came_ref[:, columns].astype(jnp.float32) * expand_tile(
                columns_b, tile, width // part_heads
            )
            rounded = value.astype(jnp.bfloat16)
            blocks[part][:, columns] = rounded
            low = part * width + tile * LANES
            projected_ref[:, low : low + LANES] = rounded[:half]
            residual = rounded.astype(jnp.float32)
            square = square + residual * residual
    mean = jnp.sum(square, axis=1, keepdims=True) / (parts * width)
    inverse = lax.rsqrt(mean + 1e-06)
    for part in range(parts):
        gain = gain_ref[:, part * width : (part + 1) * width]
        normed = blocks[part][:, :width].astype(jnp.float32) * inverse * gain
        blocks[part][:, :width] = normed.astype(jnp.bfloat16)
    came_table = pairs[1][half:, width:]
    lane = lane_iota(came_table.shape)
    blocks[0][:half, width:] = table_ref[...]
    blocks[0][half:, width:] = jnp.where(
        lane >= TABLE_LANE, came_table.astype(jnp.float32), 0.0
    ).astype(jnp.bfloat16)


def hidden_units(expert_ref, row_refs, gate_ref, up_ref, turned, hidden, ready):
    width = row_refs[1].shape[1]
    model_width = width * len(row_refs)
    for part, rows_ref in enumerate(row_refs):
        for low in range(0, width, LANES):
            at = part * width + low
            turned[at : at + LANES, :] = rows_ref[:, low : low + LANES].T
    turned[model_width:, :] = row_refs[0][:, width:].T
    scores = turned[model_width:, :].astype(jnp.float32)
    lane = lax.broadcasted_iota(jnp.int32, scores.shape, 0)
    chosen = jnp.where(lane == expert_ref[0] + TABLE_LANE, scores, 0.0)
    share = jnp.sum(chosen, axis=0, keepdims=True) / jnp.sum(scores, axis=0, keepdims=True)
    rows = turned[:model_width, :]
    for chunk in range(gate_ref.shape[0] // UNITS):
        ready(chunk)
        units = slice(chunk * UNITS, (chunk + 1) * UNITS)
        gate_part = jnp.dot(gate_ref[units, :], rows, preferred_element_type=jnp.float32)
        up_part = jnp.dot(up_ref[units, :], rows, preferred_element_type=jnp.float32)
        silu = gate_part / (1.0 + jnp.exp(-gate_part))
        hidden[:, units] = (silu * up_part * share).T.astype(jnp.bfloat16)


def down_product(hidden_ref, down_ref, out_ref, start):
    width = out_ref.shape[1]
    step = width // 2 if width % (4 * LANES) else 4 * LANES
    for low in range(0, width, step):
        out_ref[:, low : low + step] = jnp.dot(
            hidden_ref[...],
            down_ref[:, start + low : start + low + step],
            preferred_element_type=jnp.float32,
        ).astype(out_ref.dtype)


def first_expert_kernel(
    expert_ref,
    rows_a,
    rows_b,
    gate_a,
    gate_b,
    up_a,
    up_b,
    down_a,
    down_b,
    out_a,
    out_b,
    gate_ref,
    up_ref,
    down_ref,
    turned,
    hidden,
    arrived,
):
    per_half = gate_a.shape[0] // UNITS
    chunks = 2 * per_half
    pairs = ((gate_a, gate_b), (up_a, up_b), (down_a, down_b))
    targets = (gate_ref, up_ref, down_ref)

    def copy_of(part, chunk):
        low = chunk % per_half * UNITS
        return pltpu.make_async_copy(
            pairs[part][chunk // per_half].at[low : low + UNITS, :],
            targets[part].at[chunk * UNITS : (chunk + 1) * UNITS, :],
            arrived.at[part, chunk],
        )

    for chunk in range(chunks):
        for part in range(2):
            copy_of(part, chunk).start()
    for chunk in range(chunks):
        copy_of(2, chunk).start()

    def ready(chunk):
        copy_of(0, chunk).wait()
        copy_of(1, chunk).wait()

    hidden_units(expert_ref, (rows_a, rows_b), gate_ref, up_ref, turned, hidden, ready)
    for chunk in range(chunks):
        copy_of(2, chunk).wait()
    down_product(hidden, down_ref, out_a, 0)
    down_product(hidden, down_ref, out_b, out_a.shape[1])


def second_expert_kernel(
    expert_ref, rows_a, rows_b, gate_ref, up_ref, down_ref, out_ref, hidden, turned
):
    hidden_units(
        expert_ref, (rows_a, rows_b), gate_ref, up_ref, turned, hidden, lambda chunk: None
    )
    down_product(hidden, down_ref, out_ref, 0)


def rest_expert_kernel(start, hidden_ref, down_ref, first_ref, sent_ref, kept_ref, value_ref):
    down_product(hidden_ref, down_ref, value_ref, start)
    half = first_ref.shape[0] // 2
    sent_ref[:half, :] = first_ref[half:, :].astype(sent_ref.dtype)
    sent_ref[half:, :] = value_ref[half:, :].astype(sent_ref.dtype)
    kept_ref[:half, :] = first_ref[:half, :]
    kept_ref[half:, :] = value_ref[:half, :]


def first_expert_rows(expert, halves, weights):
    units, model_width = weights[0].shape
    row_count = halves[0].shape[0]
    whole = pl.BlockSpec(memory_space=pltpu.VMEM)
    anywhere = pl.BlockSpec(memory_space=pltpu.HBM)
    chunks = 2 * units // UNITS
    return pl.pallas_call(
        first_expert_kernel,
        name="expert_first",
        compiler_params=pltpu.CompilerParams(vmem_limit_bytes=12 << 20),
        out_shape=(near_shape((row_count, model_width // 2), jnp.float32),) * 2
        + (near_shape((2 * units, model_width), jnp.bfloat16),) * 3,
        in_specs=[pl.BlockSpec(memory_space=pltpu.SMEM)] + [whole] * 2 + [anywhere] * 6,
        out_specs=(whole,) * 5,
        scratch_shapes=[
            pltpu.VMEM((model_width + LANES, row_count), jnp.bfloat16),
            pltpu.VMEM((row_count, 2 * units), jnp.bfloat16),
            pltpu.SemaphoreType.DMA((3, chunks)),
        ],
        cost_estimate=pl.CostEstimate(
            flops=12 * row_count * model_width * units,
            transcendentals=0,
            bytes_accessed=12 * units * model_width,
        ),
    )(expert, *[near(half) for half in halves], *[far(weight) for weight in weights])


def second_expert_rows(expert, halves, weights, totals):
    units, model_width = weights[0].shape
    row_count = halves[0].shape[0]
    width = model_width // 2
    whole = pl.BlockSpec(memory_space=pltpu.VMEM)
    first, hidden = pl.pallas_call(
        second_expert_kernel,
        name="expert_second",
        compiler_params=pltpu.CompilerParams(vmem_limit_bytes=12 << 20),
        out_shape=(
            near_shape((row_count, width), jnp.bfloat16),
            near_shape((row_count, units), jnp.bfloat16),
        ),
        in_specs=[pl.BlockSpec(memory_space=pltpu.SMEM)] + [whole] * 5,
        out_specs=(whole, whole),
        scratch_shapes=[pltpu.VMEM((model_width + LANES, row_count), jnp.bfloat16)],
    )(expert, *[near(half) for half in halves], *[near(weight) for weight in weights])
    sent, kept = pl.pallas_call(
        functools.partial(rest_expert_kernel, width),
        name="expert_rest",
        compiler_params=pltpu.CompilerParams(vmem_limit_bytes=12 << 20),
        out_shape=(
            near_shape((row_count, width), jnp.bfloat16),
            near_shape((row_count, width), jnp.float32),
        ),
        in_specs=[whole] * 3,
        out_specs=(whole, whole),
        scratch_shapes=[pltpu.VMEM((row_count, width), jnp.float32)],
    )(near(hidden), near(weights[2]), near(totals[1]))
    return [(first, totals[0]), (sent, kept)]


def attention_rows(
    queries, patch_keys, patch_values, other_keys, other_values, norm_gain, table, row_count, orders
):
    model_width = patch_values.shape[1]
    part_width = model_width // PARTS + LANES
    part_heads = HEADS // PARTS
    stages = len(orders[0])
    device_index = lax.axis_index("wide")
    masks = [
        [
            sum(
                (1 << order[stage])
                for stage in range(stages)
                if slot >> (stages - 1 - stage) & 1
            )
            for slot in range(1 << stages)
        ]
        for order in orders
    ]
    rows = row_count << stages
    whole = pl.BlockSpec(memory_space=pltpu.VMEM)

    def pair_shapes(rows):
        return (
            near_shape((rows, part_width), jnp.bfloat16),
            near_shape((rows, part_width), jnp.float32),
        )

    query_rows, *partials = pl.pallas_call(
        functools.partial(attend_own_kernel, HEADS, row_count, masks),
        name="attend_own",
        compiler_params=pltpu.CompilerParams(vmem_limit_bytes=12 << 20),
        out_shape=(near_shape((rows, queries.shape[1]), jnp.bfloat16),)
        + (near_shape((rows, part_width), jnp.float32),) * PARTS,
        in_specs=[pl.BlockSpec(memory_space=pltpu.SMEM)] + [whole] * 3,
        out_specs=(whole,) * (PARTS + 1),
    )(device_index.reshape(1), far(queries), far(patch_keys), far(patch_values))
    chains = pl.pallas_call(
        functools.partial(attend_other_kernel, HEADS),
        name="attend_other",
        compiler_params=pltpu.CompilerParams(vmem_limit_bytes=12 << 20),
        out_shape=pair_shapes(rows // 2) * PARTS,
        in_specs=[whole] * (3 + PARTS),
        out_specs=(whole,) * (2 * PARTS),
    )(
        near(query_rows),
        near(other_keys),
        near(other_values),
        *[near(partial) for partial in partials],
    )
    finished = []
    for part in range(PARTS):
        sent, kept = chains[2 * part : 2 * part + 2]
        for stage in range(stages - 1):
            came = exchange(sent, orders, stage)
            rows = kept.shape[0]
            last = stage == stages - 2
            operands = [near(kept), near(came)]
            if last and part == 0:
                operands.append(near(table))
            sent, kept = pl.pallas_call(
                functools.partial(last_merge_kernel if last else merge_kernel, part_heads),
                compiler_params=pltpu.CompilerParams(vmem_limit_bytes=6 << 20),
                out_shape=pair_shapes(rows if last else rows // 2),
                in_specs=[whole] * len(operands),
                out_specs=(whole, whole),
            )(*operands)
        came = exchange(sent, orders, stages - 1)
        finished += [near(kept), near(came)]
    rows = kept.shape[0]
    *blocks, projected = pl.pallas_call(
        functools.partial(finish_kernel, HEADS),
        name="finish",
        compiler_params=pltpu.CompilerParams(vmem_limit_bytes=6 << 20),
        out_shape=tuple(
            near_shape((rows, model_width // PARTS + (LANES if part == 0 else 0)), jnp.bfloat16)
            for part in range(PARTS)
        )
        + (near_shape((row_count, model_width), jnp.bfloat16),),
        in_specs=[whole] * (2 + 2 * PARTS),
        out_specs=(whole,) * (PARTS + 1),
    )(near(norm_gain.reshape(1, model_width)), near(table), *finished)
    return blocks, projected


def on_device(
    queries, patch_keys, patch_values, norm_gain, route_experts, route_weights, w_gate, w_up, w_down
):
    row_count = route_experts.shape[0]
    devices = lax.axis_size("wide")
    device_index = lax.axis_index("wide")
    score_table = jnp.sum(
        jnp.where(
            route_experts[:, :, None] == jnp.arange(-TABLE_LANE, LANES - TABLE_LANE, dtype=jnp.int32),
            route_weights[:, :, None],
            0,
        ),
        axis=1,
    ).astype(jnp.bfloat16)
    merge_order, gather_order, scatter_order = plan_orders(
        devices, queries.shape[0] // row_count
    )
    other_keys = partner(patch_keys, "wide", 0)
    other_values = partner(patch_values, "wide", 0)
    halves, other_keys, other_values = lax.optimization_barrier(
        ((w_gate, w_up, w_down), other_keys, other_values)
    )
    weights = []
    for own in halves:
        weights += [own, partner(own, "wide", 0)]
    blocks, projected = attention_rows(
        queries,
        patch_keys,
        patch_values,
        other_keys,
        other_values,
        norm_gain,
        score_table,
        row_count,
        merge_order,
    )
    stages = len(gather_order[0])
    came = []
    for part in range(PARTS):
        for stage in range(stages - 1):
            arrived = exchange(blocks[part], gather_order, stage)
            blocks[part] = jnp.concatenate([blocks[part], arrived], axis=0)
        came.append(exchange(blocks[part], gather_order, stages - 1))
    expert = (device_index // 2).reshape(1)
    *totals, gate, up, down = first_expert_rows(expert, blocks, weights)
    outputs = []
    for part, (sent, kept) in enumerate(
        second_expert_rows(expert, came, (gate, up, down), totals)
    ):
        for stage in range(stages + 1):
            arrived = exchange(sent, scatter_order[part], stage)
            kept = kept + arrived.astype(jnp.float32)
            half_rows = kept.shape[0] // 2
            if stage < stages:
                sent = kept[half_rows:].astype(jnp.bfloat16)
                kept = kept[:half_rows]
        outputs.append(kept)
    total = jnp.concatenate(outputs, axis=1)
    return (projected.astype(jnp.float32) + total).astype(jnp.bfloat16)


def solution(mesh):
    return mapped(mesh)


def mapped(mesh):
    return jax.shard_map(
        on_device,
        mesh=mesh,
        in_specs=(
            P("groups", None),
            P(("groups", "wide"), None),
            P(("groups", "wide"), None),
            P(),
            P(("groups", "wide"), None),
            P(("groups", "wide"), None),
            P("wide", None),
            P("wide", None),
            P("wide", None),
        ),
        out_specs=P(("groups", "wide"), None),
        check_vma=False,
    )
```

```python
import functools

import jax
import jax.numpy as jnp
from jax import lax
from jax.experimental import pallas as pl
from jax.experimental.pallas import tpu as pltpu
from jax.sharding import PartitionSpec as P


HEADS = 16
LANES = 128
TABLE_LANE = 64
UNITS = 256
PARTS = 2


def near(value):
    return pltpu.with_memory_space_constraint(value, pltpu.VMEM)


def far(value):
    return pltpu.with_memory_space_constraint(value, pltpu.HBM)


def near_shape(shape, dtype):
    return pltpu.VMEM(shape, dtype)


def partner(value, axis, stride):
    mask = 2**stride
    pairs = [(source, source ^ mask) for source in range(lax.axis_size(axis))]
    return lax.ppermute(value, axis, pairs)


def plan_orders(devices, group_size):
    near_bits = list(range(1, group_size.bit_length() - 1))
    all_bits = list(range(1, devices.bit_length() - 1))
    merge = (near_bits, near_bits[1:] + near_bits[:1])
    rest = [[bit for bit in all_bits if bit != order[-1]] for order in merge]
    gather = (rest[0][::-1], rest[1][2:][::-1] + rest[1][:2])
    scatter = [order[::-1] + kept[-1:] for order, kept in zip(gather, merge)]
    crossed = [order[1::-1] + order[2:] for order in scatter]
    return merge, gather, (scatter, crossed)


def exchange(value, orders, stage):
    pairs = [
        (source, source ^ (1 << orders[source % 2][stage]))
        for source in range(lax.axis_size("wide"))
    ]
    return lax.ppermute(value, "wide", pairs)


def lane_iota(shape):
    return lax.broadcasted_iota(jnp.int32, shape, 1)


def expand_tile(columns, tile, value_size):
    first = tile * LANES // value_size
    last = (tile * LANES + LANES - 1) // value_size
    rows = columns[0].shape[0]
    out = jnp.broadcast_to(columns[first], (rows, LANES))
    for head in range(first + 1, last + 1):
        edge = head * value_size - tile * LANES
        out = jnp.where(lane_iota((rows, LANES)) < edge, out, columns[head])
    return out


def pack_stats(peak, total, head_count):
    lane = lane_iota(peak.shape)
    high = total.astype(jnp.bfloat16).astype(jnp.float32)
    low = total - high
    packed = jnp.where(lane < head_count, peak, 0.0)
    shifted = pltpu.roll(jnp.where(lane < head_count, high, 0.0), head_count, 1)
    shifted_low = pltpu.roll(jnp.where(lane < head_count, low, 0.0), 2 * head_count, 1)
    return packed + shifted + shifted_low


def total_of(stats, head_count):
    return pltpu.roll(stats, LANES - head_count, 1) + pltpu.roll(
        stats, LANES - 2 * head_count, 1
    )


def head_windows(head, size):
    return head * size // LANES, -(-(head + 1) * size // LANES)


def head_scores(head, head_count, query_ref, keys_ref):
    key_size = query_ref.shape[1] // head_count
    low, high = [LANES * tile for tile in head_windows(head, key_size)]
    window = lane_iota((query_ref.shape[0], high - low)) + low
    inside = (window >= head * key_size) & (window < (head + 1) * key_size)
    query = jnp.where(inside, query_ref[:, low:high], jnp.zeros((), jnp.bfloat16))
    return key_size ** (-0.5) * lax.dot_general(
        query,
        keys_ref[:, low:high],
        (((1,), (1,)), ((), ())),
        preferred_element_type=jnp.float32,
    )


def rounded_peak(scores):
    peak = jnp.max(scores, axis=1, keepdims=True)
    return peak.astype(jnp.bfloat16).astype(jnp.float32)


def head_sums(head, value_size, raised, values_ref):
    low, high = head_windows(head, value_size)
    return jnp.dot(
        raised.astype(jnp.bfloat16),
        values_ref[:, low * LANES : high * LANES],
        preferred_element_type=jnp.float32,
    )


def stage_kernel(
    row_count,
    masks,
    device_ref,
    queries_ref,
    keys_ref,
    values_ref,
    query_ref,
    near_keys_ref,
    near_values_ref,
    arrived,
):
    group_size = queries_ref.shape[0] // row_count
    device = device_ref[0]
    odd = lax.rem(device, 2) == 1
    own_block = lax.rem(device, group_size)
    copies = [
        pltpu.make_async_copy(keys_ref, near_keys_ref, arrived.at[0]),
        pltpu.make_async_copy(values_ref, near_values_ref, arrived.at[1]),
    ]
    for slot, (even_mask, odd_mask) in enumerate(zip(*masks)):
        block = own_block ^ jnp.where(odd, odd_mask, even_mask)
        start = pl.multiple_of(block * row_count, row_count)
        copies.append(
            pltpu.make_async_copy(
                queries_ref.at[pl.ds(start, row_count), :],
                query_ref.at[slot * row_count : (slot + 1) * row_count, :],
                arrived.at[2 + slot],
            )
        )
    for copy in copies:
        copy.start()
    for copy in copies:
        copy.wait()


def attend_kernel(
    head_count, part, part_heads, query_ref, keys_a, keys_b, values_a, values_b, sent_ref, kept_ref
):
    rows = query_ref.shape[0]
    half = rows // 2
    value_size = values_a.shape[1] // head_count
    part_tiles = part_heads * value_size // LANES
    base = part * part_tiles
    lane = lane_iota((rows, LANES))
    peaks = jnp.zeros((rows, LANES), jnp.float32)
    totals = jnp.zeros((rows, LANES), jnp.float32)

    def put(tile, value):
        columns = slice(tile * LANES, (tile + 1) * LANES)
        kept_ref[:, columns] = value[:half]
        sent_ref[:, columns] = value[half:].astype(jnp.bfloat16)

    for at in range(part_heads):
        head = part * part_heads + at
        scores_a = head_scores(head, head_count, query_ref, keys_a)
        scores_b = head_scores(head, head_count, query_ref, keys_b)
        peak = jnp.maximum(rounded_peak(scores_a), rounded_peak(scores_b))
        raised_a = jnp.exp(scores_a - peak)
        raised_b = jnp.exp(scores_b - peak)
        total = jnp.sum(raised_a + raised_b, axis=1, keepdims=True)
        peaks = jnp.where(lane == at, peak, peaks)
        totals = jnp.where(lane == at, total, totals)
        summed = head_sums(head, value_size, raised_a, values_a) + head_sums(
            head, value_size, raised_b, values_b
        )
        low, high = head_windows(head, value_size)
        for tile in range(low, high):
            value = summed[:, (tile - low) * LANES : (tile - low + 1) * LANES]
            edge = head * value_size - tile * LANES
            if edge > 0:
                value = jnp.where(lane < edge, waiting, value)
            waiting = value
            if (tile + 1) * LANES <= (head + 1) * value_size:
                put(tile - base, value)
    put(part_tiles, pack_stats(peaks, totals, part_heads))


def merged_parts(kept_ref, came_ref, head_count, model_width):
    stats_a = kept_ref[:, model_width:]
    stats_b = came_ref[:, model_width:].astype(jnp.float32)
    peak = jnp.maximum(stats_a, stats_b)
    factor_a = jnp.exp(stats_a - peak)
    factor_b = jnp.exp(stats_b - peak)
    total = total_of(stats_a, head_count) * factor_a + total_of(stats_b, head_count) * factor_b
    return peak, total, factor_a, factor_b


def head_columns(array, head_count):
    return [array[:, head : head + 1] for head in range(head_count)]


def merge_kernel(head_count, kept_ref, came_ref, sent_ref, next_ref):
    model_width = kept_ref.shape[1] - LANES
    half = kept_ref.shape[0] // 2
    peak, total, factor_a, factor_b = merged_parts(kept_ref, came_ref, head_count, model_width)
    columns_a = head_columns(factor_a, head_count)
    columns_b = head_columns(factor_b, head_count)
    for tile in range(model_width // LANES + 1):
        columns = slice(tile * LANES, (tile + 1) * LANES)
        if tile * LANES == model_width:
            value = pack_stats(peak, total, head_count)
        else:
            value = kept_ref[:, columns] * expand_tile(
                columns_a, tile, model_width // head_count
            ) + came_ref[:, columns].astype(jnp.float32) * expand_tile(
                columns_b, tile, model_width // head_count
            )
        next_ref[:, columns] = value[:half]
        sent_ref[:, columns] = value[half:].astype(jnp.bfloat16)


def last_merge_kernel(head_count, kept_ref, came_ref, *rest):
    tables, (sent_ref, next_ref) = rest[:-2], rest[-2:]
    model_width = kept_ref.shape[1] - LANES
    half = kept_ref.shape[0] // 2
    peak, total, factor_a, factor_b = merged_parts(kept_ref, came_ref, head_count, model_width)
    columns_a = head_columns(factor_a, head_count)
    columns_b = head_columns(factor_b, head_count)
    for tile in range(model_width // LANES + 1):
        columns = slice(tile * LANES, (tile + 1) * LANES)
        if tile * LANES == model_width:
            value = pack_stats(peak, total, head_count)
            own = value[:half]
            for table_ref in tables:
                own = own + table_ref[...].astype(jnp.float32)
        else:
            value = kept_ref[:, columns] * expand_tile(
                columns_a, tile, model_width // head_count
            ) + came_ref[:, columns].astype(jnp.float32) * expand_tile(
                columns_b, tile, model_width // head_count
            )
            own = value[:half]
        next_ref[:, columns] = value
        sent_ref[:half, columns] = value[half:].astype(jnp.bfloat16)
        sent_ref[half:, columns] = own.astype(jnp.bfloat16)


def finish_kernel(head_count, gain_ref, table_ref, *rest):
    parts = (len(rest) - 1) // 3
    pairs, blocks, projected_ref = rest[: 2 * parts], rest[2 * parts : 3 * parts], rest[-1]
    part_heads = head_count // parts
    rows = pairs[0].shape[0]
    half = rows // 2
    width = pairs[0].shape[1] - LANES
    square = jnp.zeros((rows, LANES), jnp.float32)
    for part in range(parts):
        kept_ref, came_ref = pairs[2 * part : 2 * part + 2]
        _, total, factor_a, factor_b = merged_parts(kept_ref, came_ref, part_heads, width)
        columns_a = head_columns(factor_a / total, part_heads)
        columns_b = head_columns(factor_b / total, part_heads)
        for tile in range(width // LANES):
            columns = slice(tile * LANES, (tile + 1) * LANES)
            value = kept_ref[:, columns] * expand_tile(
                columns_a, tile, width // part_heads
            ) + came_ref[:, columns].astype(jnp.float32) * expand_tile(
                columns_b, tile, width // part_heads
            )
            rounded = value.astype(jnp.bfloat16)
            blocks[part][:, columns] = rounded
            low = part * width + tile * LANES
            projected_ref[:, low : low + LANES] = rounded[:half]
            residual = rounded.astype(jnp.float32)
            square = square + residual * residual
    mean = jnp.sum(square, axis=1, keepdims=True) / (parts * width)
    inverse = lax.rsqrt(mean + 1e-06)
    for part in range(parts):
        gain = gain_ref[:, part * width : (part + 1) * width]
        normed = blocks[part][:, :width].astype(jnp.float32) * inverse * gain
        blocks[part][:, :width] = normed.astype(jnp.bfloat16)
    came_table = pairs[1][half:, width:]
    lane = lane_iota(came_table.shape)
    blocks[0][:half, width:] = table_ref[...]
    blocks[0][half:, width:] = jnp.where(
        lane >= TABLE_LANE, came_table.astype(jnp.float32), 0.0
    ).astype(jnp.bfloat16)


def hidden_units(expert_ref, row_refs, gate_ref, up_ref, turned, hidden, ready):
    width = row_refs[1].shape[1]
    model_width = width * len(row_refs)
    for part, rows_ref in enumerate(row_refs):
        for low in range(0, width, LANES):
            at = part * width + low
            turned[at : at + LANES, :] = rows_ref[:, low : low + LANES].T
    turned[model_width:, :] = row_refs[0][:, width:].T
    scores = turned[model_width:, :].astype(jnp.float32)
    lane = lax.broadcasted_iota(jnp.int32, scores.shape, 0)
    chosen = jnp.where(lane == expert_ref[0] + TABLE_LANE, scores, 0.0)
    share = jnp.sum(chosen, axis=0, keepdims=True) / jnp.sum(scores, axis=0, keepdims=True)
    rows = turned[:model_width, :]
    for chunk in range(gate_ref.shape[0] // UNITS):
        ready(chunk)
        units = slice(chunk * UNITS, (chunk + 1) * UNITS)
        gate_part = jnp.dot(gate_ref[units, :], rows, preferred_element_type=jnp.float32)
        up_part = jnp.dot(up_ref[units, :], rows, preferred_element_type=jnp.float32)
        silu = gate_part / (1.0 + jnp.exp(-gate_part))
        hidden[:, units] = (silu * up_part * share).T.astype(jnp.bfloat16)


def down_product(hidden_ref, down_ref, out_ref, start):
    width = out_ref.shape[1]
    step = width // 2 if width % (4 * LANES) else 4 * LANES
    for low in range(0, width, step):
        out_ref[:, low : low + step] = jnp.dot(
            hidden_ref[...],
            down_ref[:, start + low : start + low + step],
            preferred_element_type=jnp.float32,
        ).astype(out_ref.dtype)


def first_expert_kernel(
    expert_ref,
    rows_a,
    rows_b,
    gate_a,
    gate_b,
    up_a,
    up_b,
    down_a,
    down_b,
    out_a,
    out_b,
    gate_ref,
    up_ref,
    down_ref,
    turned,
    hidden,
    arrived,
):
    per_half = gate_a.shape[0] // UNITS
    chunks = 2 * per_half
    pairs = ((gate_a, gate_b), (up_a, up_b), (down_a, down_b))
    targets = (gate_ref, up_ref, down_ref)

    def copy_of(part, chunk):
        low = chunk % per_half * UNITS
        return pltpu.make_async_copy(
            pairs[part][chunk // per_half].at[low : low + UNITS, :],
            targets[part].at[chunk * UNITS : (chunk + 1) * UNITS, :],
            arrived.at[part, chunk],
        )

    for chunk in range(chunks):
        for part in range(2):
            copy_of(part, chunk).start()
    for chunk in range(chunks):
        copy_of(2, chunk).start()

    def ready(chunk):
        copy_of(0, chunk).wait()
        copy_of(1, chunk).wait()

    hidden_units(expert_ref, (rows_a, rows_b), gate_ref, up_ref, turned, hidden, ready)
    for chunk in range(chunks):
        copy_of(2, chunk).wait()
    down_product(hidden, down_ref, out_a, 0)
    down_product(hidden, down_ref, out_b, out_a.shape[1])


def second_expert_kernel(
    expert_ref, rows_a, rows_b, gate_ref, up_ref, down_ref, out_ref, hidden, turned
):
    hidden_units(
        expert_ref, (rows_a, rows_b), gate_ref, up_ref, turned, hidden, lambda chunk: None
    )
    down_product(hidden, down_ref, out_ref, 0)


def rest_expert_kernel(start, hidden_ref, down_ref, first_ref, sent_ref, kept_ref, value_ref):
    down_product(hidden_ref, down_ref, value_ref, start)
    half = first_ref.shape[0] // 2
    sent_ref[:half, :] = first_ref[half:, :].astype(sent_ref.dtype)
    sent_ref[half:, :] = value_ref[half:, :].astype(sent_ref.dtype)
    kept_ref[:half, :] = first_ref[:half, :]
    kept_ref[half:, :] = value_ref[:half, :]


def first_expert_rows(expert, halves, weights):
    units, model_width = weights[0].shape
    row_count = halves[0].shape[0]
    whole = pl.BlockSpec(memory_space=pltpu.VMEM)
    anywhere = pl.BlockSpec(memory_space=pltpu.HBM)
    chunks = 2 * units // UNITS
    return pl.pallas_call(
        first_expert_kernel,
        name="expert_first",
        compiler_params=pltpu.CompilerParams(vmem_limit_bytes=12 << 20),
        out_shape=(near_shape((row_count, model_width // 2), jnp.float32),) * 2
        + (near_shape((2 * units, model_width), jnp.bfloat16),) * 3,
        in_specs=[pl.BlockSpec(memory_space=pltpu.SMEM)] + [whole] * 2 + [anywhere] * 6,
        out_specs=(whole,) * 5,
        scratch_shapes=[
            pltpu.VMEM((model_width + LANES, row_count), jnp.bfloat16),
            pltpu.VMEM((row_count, 2 * units), jnp.bfloat16),
            pltpu.SemaphoreType.DMA((3, chunks)),
        ],
        cost_estimate=pl.CostEstimate(
            flops=12 * row_count * model_width * units,
            transcendentals=0,
            bytes_accessed=12 * units * model_width,
        ),
    )(expert, *[near(half) for half in halves], *[far(weight) for weight in weights])


def second_expert_rows(expert, halves, weights, totals):
    units, model_width = weights[0].shape
    row_count = halves[0].shape[0]
    width = model_width // 2
    whole = pl.BlockSpec(memory_space=pltpu.VMEM)
    first, hidden = pl.pallas_call(
        second_expert_kernel,
        name="expert_second",
        compiler_params=pltpu.CompilerParams(vmem_limit_bytes=12 << 20),
        out_shape=(
            near_shape((row_count, width), jnp.bfloat16),
            near_shape((row_count, units), jnp.bfloat16),
        ),
        in_specs=[pl.BlockSpec(memory_space=pltpu.SMEM)] + [whole] * 5,
        out_specs=(whole, whole),
        scratch_shapes=[pltpu.VMEM((model_width + LANES, row_count), jnp.bfloat16)],
    )(expert, *[near(half) for half in halves], *[near(weight) for weight in weights])
    sent, kept = pl.pallas_call(
        functools.partial(rest_expert_kernel, width),
        name="expert_rest",
        compiler_params=pltpu.CompilerParams(vmem_limit_bytes=12 << 20),
        out_shape=(
            near_shape((row_count, width), jnp.bfloat16),
            near_shape((row_count, width), jnp.float32),
        ),
        in_specs=[whole] * 3,
        out_specs=(whole, whole),
        scratch_shapes=[pltpu.VMEM((row_count, width), jnp.float32)],
    )(near(hidden), near(weights[2]), near(totals[1]))
    return [(first, totals[0]), (sent, kept)]


def attention_rows(
    queries, patch_keys, patch_values, other_keys, other_values, norm_gain, table, row_count, orders
):
    model_width = patch_values.shape[1]
    part_width = model_width // PARTS + LANES
    part_heads = HEADS // PARTS
    stages = len(orders[0])
    device_index = lax.axis_index("wide")
    masks = [
        [
            sum(
                (1 << order[stage])
                for stage in range(stages)
                if slot >> (stages - 1 - stage) & 1
            )
            for slot in range(1 << stages)
        ]
        for order in orders
    ]
    rows = row_count << stages
    whole = pl.BlockSpec(memory_space=pltpu.VMEM)

    def pair_shapes(rows):
        return (
            near_shape((rows, part_width), jnp.bfloat16),
            near_shape((rows, part_width), jnp.float32),
        )

    anywhere = pl.BlockSpec(memory_space=pltpu.HBM)
    query_rows, own_keys, own_values = pl.pallas_call(
        functools.partial(stage_kernel, row_count, masks),
        name="stage_in",
        compiler_params=pltpu.CompilerParams(vmem_limit_bytes=4 << 20),
        out_shape=(
            near_shape((rows, queries.shape[1]), jnp.bfloat16),
            near_shape(patch_keys.shape, jnp.bfloat16),
            near_shape(patch_values.shape, jnp.bfloat16),
        ),
        in_specs=[pl.BlockSpec(memory_space=pltpu.SMEM)] + [anywhere] * 3,
        out_specs=(whole,) * 3,
        scratch_shapes=[pltpu.SemaphoreType.DMA((2 + (1 << stages),))],
    )(device_index.reshape(1), far(queries), far(patch_keys), far(patch_values))
    operands = (query_rows, own_keys, other_keys, own_values, other_values)
    chains = []
    for part in range(PARTS):
        chains += pl.pallas_call(
            functools.partial(attend_kernel, HEADS, part, part_heads),
            compiler_params=pltpu.CompilerParams(vmem_limit_bytes=8 << 20),
            out_shape=pair_shapes(rows // 2),
            in_specs=[whole] * 5,
            out_specs=(whole, whole),
        )(*[near(operand) for operand in operands])
    finished = []
    for part in range(PARTS):
        sent, kept = chains[2 * part : 2 * part + 2]
        for stage in range(stages - 1):
            came = exchange(sent, orders, stage)
            rows = kept.shape[0]
            last = stage == stages - 2
            operands = [near(kept), near(came)]
            if last and part == 0:
                operands.append(near(table))
            sent, kept = pl.pallas_call(
                functools.partial(last_merge_kernel if last else merge_kernel, part_heads),
                compiler_params=pltpu.CompilerParams(vmem_limit_bytes=6 << 20),
                out_shape=pair_shapes(rows if last else rows // 2),
                in_specs=[whole] * len(operands),
                out_specs=(whole, whole),
            )(*operands)
        came = exchange(sent, orders, stages - 1)
        finished += [near(kept), near(came)]
    rows = kept.shape[0]
    *blocks, projected = pl.pallas_call(
        functools.partial(finish_kernel, HEADS),
        name="finish",
        compiler_params=pltpu.CompilerParams(vmem_limit_bytes=6 << 20),
        out_shape=tuple(
            near_shape((rows, model_width // PARTS + (LANES if part == 0 else 0)), jnp.bfloat16)
            for part in range(PARTS)
        )
        + (near_shape((row_count, model_width), jnp.bfloat16),),
        in_specs=[whole] * (2 + 2 * PARTS),
        out_specs=(whole,) * (PARTS + 1),
    )(near(norm_gain.reshape(1, model_width)), near(table), *finished)
    return blocks, projected


def on_device(
    queries, patch_keys, patch_values, norm_gain, route_experts, route_weights, w_gate, w_up, w_down
):
    row_count = route_experts.shape[0]
    devices = lax.axis_size("wide")
    device_index = lax.axis_index("wide")
    score_table = jnp.sum(
        jnp.where(
            route_experts[:, :, None] == jnp.arange(-TABLE_LANE, LANES - TABLE_LANE, dtype=jnp.int32),
            route_weights[:, :, None],
            0,
        ),
        axis=1,
    ).astype(jnp.bfloat16)
    merge_order, gather_order, scatter_order = plan_orders(
        devices, queries.shape[0] // row_count
    )
    other_keys = partner(patch_keys, "wide", 0)
    other_values = partner(patch_values, "wide", 0)
    halves, other_keys, other_values = lax.optimization_barrier(
        ((w_gate, w_up, w_down), other_keys, other_values)
    )
    weights = []
    for own in halves:
        weights += [own, partner(own, "wide", 0)]
    blocks, projected = attention_rows(
        queries,
        patch_keys,
        patch_values,
        other_keys,
        other_values,
        norm_gain,
        score_table,
        row_count,
        merge_order,
    )
    stages = len(gather_order[0])
    came = []
    for part in range(PARTS):
        for stage in range(stages - 1):
            arrived = exchange(blocks[part], gather_order, stage)
            blocks[part] = jnp.concatenate([blocks[part], arrived], axis=0)
        came.append(exchange(blocks[part], gather_order, stages - 1))
    expert = (device_index // 2).reshape(1)
    *totals, gate, up, down = first_expert_rows(expert, blocks, weights)
    outputs = []
    for part, (sent, kept) in enumerate(
        second_expert_rows(expert, came, (gate, up, down), totals)
    ):
        for stage in range(stages + 1):
            arrived = exchange(sent, scatter_order[part], stage)
            kept = kept + arrived.astype(jnp.float32)
            half_rows = kept.shape[0] // 2
            if stage < stages:
                sent = kept[half_rows:].astype(jnp.bfloat16)
                kept = kept[:half_rows]
        outputs.append(kept)
    total = jnp.concatenate(outputs, axis=1)
    return (projected.astype(jnp.float32) + total).astype(jnp.bfloat16)


def solution(mesh):
    return mapped(mesh)


def mapped(mesh):
    return jax.shard_map(
        on_device,
        mesh=mesh,
        in_specs=(
            P("groups", None),
            P(("groups", "wide"), None),
            P(("groups", "wide"), None),
            P(),
            P(("groups", "wide"), None),
            P(("groups", "wide"), None),
            P("wide", None),
            P("wide", None),
            P("wide", None),
        ),
        out_specs=P(("groups", "wide"), None),
        check_vma=False,
    )
```

```python
import functools

import jax
import jax.numpy as jnp
from jax import lax
from jax.experimental import pallas as pl
from jax.experimental.pallas import tpu as pltpu
from jax.sharding import PartitionSpec as P


HEADS = 16
LANES = 128
TABLE_LANE = 64
UNITS = 256
PARTS = 2


def near(value):
    return pltpu.with_memory_space_constraint(value, pltpu.VMEM)


def far(value):
    return pltpu.with_memory_space_constraint(value, pltpu.HBM)


def near_shape(shape, dtype):
    return pltpu.VMEM(shape, dtype)


def partner(value, axis, stride):
    mask = 2**stride
    pairs = [(source, source ^ mask) for source in range(lax.axis_size(axis))]
    return lax.ppermute(value, axis, pairs)


def plan_orders(devices, group_size):
    near_bits = list(range(1, group_size.bit_length() - 1))
    all_bits = list(range(1, devices.bit_length() - 1))
    merge = (near_bits, near_bits[1:] + near_bits[:1])
    rest = [[bit for bit in all_bits if bit != order[-1]] for order in merge]
    gather = (rest[0][::-1], rest[1][2:][::-1] + rest[1][:2])
    scatter = [order[::-1] + kept[-1:] for order, kept in zip(gather, merge)]
    crossed = [order[1::-1] + order[2:] for order in scatter]
    return merge, gather, (scatter, crossed)


def exchange(value, orders, stage):
    pairs = [
        (source, source ^ (1 << orders[source % 2][stage]))
        for source in range(lax.axis_size("wide"))
    ]
    return lax.ppermute(value, "wide", pairs)


def lane_iota(shape):
    return lax.broadcasted_iota(jnp.int32, shape, 1)


def expand_tile(columns, tile, value_size):
    first = tile * LANES // value_size
    last = (tile * LANES + LANES - 1) // value_size
    rows = columns[0].shape[0]
    out = jnp.broadcast_to(columns[first], (rows, LANES))
    for head in range(first + 1, last + 1):
        edge = head * value_size - tile * LANES
        out = jnp.where(lane_iota((rows, LANES)) < edge, out, columns[head])
    return out


def pack_stats(peak, total, head_count):
    lane = lane_iota(peak.shape)
    high = total.astype(jnp.bfloat16).astype(jnp.float32)
    low = total - high
    packed = jnp.where(lane < head_count, peak, 0.0)
    shifted = pltpu.roll(jnp.where(lane < head_count, high, 0.0), head_count, 1)
    shifted_low = pltpu.roll(jnp.where(lane < head_count, low, 0.0), 2 * head_count, 1)
    return packed + shifted + shifted_low


def total_of(stats, head_count):
    return pltpu.roll(stats, LANES - head_count, 1) + pltpu.roll(
        stats, LANES - 2 * head_count, 1
    )


def head_windows(head, size):
    return head * size // LANES, -(-(head + 1) * size // LANES)


def head_scores(head, head_count, query_ref, keys_ref):
    key_size = query_ref.shape[1] // head_count
    low, high = [LANES * tile for tile in head_windows(head, key_size)]
    window = lane_iota((query_ref.shape[0], high - low)) + low
    inside = (window >= head * key_size) & (window < (head + 1) * key_size)
    query = jnp.where(inside, query_ref[:, low:high], jnp.zeros((), jnp.bfloat16))
    return key_size ** (-0.5) * lax.dot_general(
        query,
        keys_ref[:, low:high],
        (((1,), (1,)), ((), ())),
        preferred_element_type=jnp.float32,
    )


def rounded_peak(scores):
    peak = jnp.max(scores, axis=1, keepdims=True)
    return peak.astype(jnp.bfloat16).astype(jnp.float32)


def head_sums(head, value_size, raised, values_ref):
    low, high = head_windows(head, value_size)
    return jnp.dot(
        raised.astype(jnp.bfloat16),
        values_ref[:, low * LANES : high * LANES],
        preferred_element_type=jnp.float32,
    )


def stage_kernel(
    row_count,
    masks,
    device_ref,
    queries_ref,
    keys_ref,
    values_ref,
    query_ref,
    near_keys_ref,
    near_values_ref,
    arrived,
):
    group_size = queries_ref.shape[0] // row_count
    device = device_ref[0]
    odd = lax.rem(device, 2) == 1
    own_block = lax.rem(device, group_size)
    copies = [
        pltpu.make_async_copy(keys_ref, near_keys_ref, arrived.at[0]),
        pltpu.make_async_copy(values_ref, near_values_ref, arrived.at[1]),
    ]
    for slot, (even_mask, odd_mask) in enumerate(zip(*masks)):
        block = own_block ^ jnp.where(odd, odd_mask, even_mask)
        start = pl.multiple_of(block * row_count, row_count)
        copies.append(
            pltpu.make_async_copy(
                queries_ref.at[pl.ds(start, row_count), :],
                query_ref.at[slot * row_count : (slot + 1) * row_count, :],
                arrived.at[2 + slot],
            )
        )
    for copy in copies:
        copy.start()
    for copy in copies:
        copy.wait()


def attend_kernel(
    head_count, part, part_heads, query_ref, keys_a, keys_b, values_a, values_b, sent_ref, kept_ref
):
    rows = query_ref.shape[0]
    half = rows // 2
    value_size = values_a.shape[1] // head_count
    part_tiles = part_heads * value_size // LANES
    base = part * part_tiles
    lane = lane_iota((rows, LANES))
    peaks = jnp.zeros((rows, LANES), jnp.float32)
    totals = jnp.zeros((rows, LANES), jnp.float32)

    def put(tile, value):
        columns = slice(tile * LANES, (tile + 1) * LANES)
        kept_ref[:, columns] = value[:half]
        sent_ref[:, columns] = value[half:].astype(jnp.bfloat16)

    for at in range(part_heads):
        head = part * part_heads + at
        scores_a = head_scores(head, head_count, query_ref, keys_a)
        scores_b = head_scores(head, head_count, query_ref, keys_b)
        peak = jnp.maximum(rounded_peak(scores_a), rounded_peak(scores_b))
        raised_a = jnp.exp(scores_a - peak)
        raised_b = jnp.exp(scores_b - peak)
        total = jnp.sum(raised_a + raised_b, axis=1, keepdims=True)
        peaks = jnp.where(lane == at, peak, peaks)
        totals = jnp.where(lane == at, total, totals)
        summed = head_sums(head, value_size, raised_a, values_a) + head_sums(
            head, value_size, raised_b, values_b
        )
        low, high = head_windows(head, value_size)
        for tile in range(low, high):
            value = summed[:, (tile - low) * LANES : (tile - low + 1) * LANES]
            edge = head * value_size - tile * LANES
            if edge > 0:
                value = jnp.where(lane < edge, waiting, value)
            waiting = value
            if (tile + 1) * LANES <= (head + 1) * value_size:
                put(tile - base, value)
    put(part_tiles, pack_stats(peaks, totals, part_heads))


def merged_parts(kept_ref, came_ref, head_count, model_width):
    stats_a = kept_ref[:, model_width:]
    stats_b = came_ref[:, model_width:].astype(jnp.float32)
    peak = jnp.maximum(stats_a, stats_b)
    factor_a = jnp.exp(stats_a - peak)
    factor_b = jnp.exp(stats_b - peak)
    total = total_of(stats_a, head_count) * factor_a + total_of(stats_b, head_count) * factor_b
    return peak, total, factor_a, factor_b


def head_columns(array, head_count):
    return [array[:, head : head + 1] for head in range(head_count)]


def merge_kernel(head_count, kept_ref, came_ref, sent_ref, next_ref):
    model_width = kept_ref.shape[1] - LANES
    half = kept_ref.shape[0] // 2
    peak, total, factor_a, factor_b = merged_parts(kept_ref, came_ref, head_count, model_width)
    columns_a = head_columns(factor_a, head_count)
    columns_b = head_columns(factor_b, head_count)
    for tile in range(model_width // LANES + 1):
        columns = slice(tile * LANES, (tile + 1) * LANES)
        if tile * LANES == model_width:
            value = pack_stats(peak, total, head_count)
        else:
            value = kept_ref[:, columns] * expand_tile(
                columns_a, tile, model_width // head_count
            ) + came_ref[:, columns].astype(jnp.float32) * expand_tile(
                columns_b, tile, model_width // head_count
            )
        next_ref[:, columns] = value[:half]
        sent_ref[:, columns] = value[half:].astype(jnp.bfloat16)


def last_merge_kernel(head_count, kept_ref, came_ref, *rest):
    tables, (sent_ref, next_ref) = rest[:-2], rest[-2:]
    model_width = kept_ref.shape[1] - LANES
    half = kept_ref.shape[0] // 2
    peak, total, factor_a, factor_b = merged_parts(kept_ref, came_ref, head_count, model_width)
    columns_a = head_columns(factor_a, head_count)
    columns_b = head_columns(factor_b, head_count)
    for tile in range(model_width // LANES + 1):
        columns = slice(tile * LANES, (tile + 1) * LANES)
        if tile * LANES == model_width:
            value = pack_stats(peak, total, head_count)
            own = value[:half]
            for table_ref in tables:
                own = own + table_ref[...].astype(jnp.float32)
        else:
            value = kept_ref[:, columns] * expand_tile(
                columns_a, tile, model_width // head_count
            ) + came_ref[:, columns].astype(jnp.float32) * expand_tile(
                columns_b, tile, model_width // head_count
            )
            own = value[:half]
        next_ref[:, columns] = value
        sent_ref[:half, columns] = value[half:].astype(jnp.bfloat16)
        sent_ref[half:, columns] = own.astype(jnp.bfloat16)


def finish_kernel(part_heads, kept_ref, came_ref, *rest):
    tables, (block_ref, projected_ref) = rest[:-2], rest[-2:]
    half = kept_ref.shape[0] // 2
    width = kept_ref.shape[1] - LANES
    _, total, factor_a, factor_b = merged_parts(kept_ref, came_ref, part_heads, width)
    columns_a = head_columns(factor_a / total, part_heads)
    columns_b = head_columns(factor_b / total, part_heads)
    for tile in range(width // LANES):
        columns = slice(tile * LANES, (tile + 1) * LANES)
        value = kept_ref[:, columns] * expand_tile(
            columns_a, tile, width // part_heads
        ) + came_ref[:, columns].astype(jnp.float32) * expand_tile(
            columns_b, tile, width // part_heads
        )
        rounded = value.astype(jnp.bfloat16)
        block_ref[:, columns] = rounded
        projected_ref[:, columns] = rounded[:half]
    for table_ref in tables:
        came_table = came_ref[half:, width:]
        lane = lane_iota(came_table.shape)
        block_ref[:half, width:] = table_ref[...]
        block_ref[half:, width:] = jnp.where(
            lane >= TABLE_LANE, came_table.astype(jnp.float32), 0.0
        ).astype(jnp.bfloat16)


def hidden_units(expert_ref, gain_ref, row_refs, gate_ref, up_ref, turned, hidden, ready):
    width = row_refs[1].shape[1]
    model_width = width * len(row_refs)
    square = jnp.zeros((row_refs[0].shape[0], LANES), jnp.float32)
    for rows_ref in row_refs:
        for low in range(0, width, LANES):
            residual = rows_ref[:, low : low + LANES].astype(jnp.float32)
            square = square + residual * residual
    mean = jnp.sum(square, axis=1, keepdims=True) / model_width
    inverse = jnp.broadcast_to(lax.rsqrt(mean + 1e-06), square.shape)
    for part, rows_ref in enumerate(row_refs):
        for low in range(0, width, LANES):
            at = part * width + low
            residual = rows_ref[:, low : low + LANES].astype(jnp.float32)
            normed = residual * inverse * gain_ref[:, at : at + LANES]
            turned[at : at + LANES, :] = normed.astype(jnp.bfloat16).T
    turned[model_width:, :] = row_refs[0][:, width:].T
    scores = turned[model_width:, :].astype(jnp.float32)
    lane = lax.broadcasted_iota(jnp.int32, scores.shape, 0)
    chosen = jnp.where(lane == expert_ref[0] + TABLE_LANE, scores, 0.0)
    share = jnp.sum(chosen, axis=0, keepdims=True) / jnp.sum(scores, axis=0, keepdims=True)
    rows = turned[:model_width, :]
    for chunk in range(gate_ref.shape[0] // UNITS):
        ready(chunk)
        units = slice(chunk * UNITS, (chunk + 1) * UNITS)
        gate_part = jnp.dot(gate_ref[units, :], rows, preferred_element_type=jnp.float32)
        up_part = jnp.dot(up_ref[units, :], rows, preferred_element_type=jnp.float32)
        silu = gate_part / (1.0 + jnp.exp(-gate_part))
        hidden[:, units] = (silu * up_part * share).T.astype(jnp.bfloat16)


def down_product(hidden_ref, down_ref, out_ref, start):
    width = out_ref.shape[1]
    step = width // 2 if width % (4 * LANES) else 4 * LANES
    for low in range(0, width, step):
        out_ref[:, low : low + step] = jnp.dot(
            hidden_ref[...],
            down_ref[:, start + low : start + low + step],
            preferred_element_type=jnp.float32,
        ).astype(out_ref.dtype)


def first_expert_kernel(
    expert_ref,
    gain_ref,
    rows_a,
    rows_b,
    gate_a,
    gate_b,
    up_a,
    up_b,
    down_a,
    down_b,
    out_a,
    out_b,
    gate_ref,
    up_ref,
    down_ref,
    turned,
    hidden,
    arrived,
):
    per_half = gate_a.shape[0] // UNITS
    chunks = 2 * per_half
    pairs = ((gate_a, gate_b), (up_a, up_b), (down_a, down_b))
    targets = (gate_ref, up_ref, down_ref)

    def copy_of(part, chunk):
        low = chunk % per_half * UNITS
        return pltpu.make_async_copy(
            pairs[part][chunk // per_half].at[low : low + UNITS, :],
            targets[part].at[chunk * UNITS : (chunk + 1) * UNITS, :],
            arrived.at[part, chunk],
        )

    for chunk in range(chunks):
        for part in range(2):
            copy_of(part, chunk).start()
    for chunk in range(chunks):
        copy_of(2, chunk).start()

    def ready(chunk):
        copy_of(0, chunk).wait()
        copy_of(1, chunk).wait()

    hidden_units(
        expert_ref, gain_ref, (rows_a, rows_b), gate_ref, up_ref, turned, hidden, ready
    )
    for chunk in range(chunks):
        copy_of(2, chunk).wait()
    down_product(hidden, down_ref, out_a, 0)
    down_product(hidden, down_ref, out_b, out_a.shape[1])


def second_expert_kernel(
    expert_ref, gain_ref, rows_a, rows_b, gate_ref, up_ref, down_ref, out_ref, hidden, turned
):
    hidden_units(
        expert_ref,
        gain_ref,
        (rows_a, rows_b),
        gate_ref,
        up_ref,
        turned,
        hidden,
        lambda chunk: None,
    )
    down_product(hidden, down_ref, out_ref, 0)


def rest_expert_kernel(start, hidden_ref, down_ref, first_ref, sent_ref, kept_ref, value_ref):
    down_product(hidden_ref, down_ref, value_ref, start)
    half = first_ref.shape[0] // 2
    sent_ref[:half, :] = first_ref[half:, :].astype(sent_ref.dtype)
    sent_ref[half:, :] = value_ref[half:, :].astype(sent_ref.dtype)
    kept_ref[:half, :] = first_ref[:half, :]
    kept_ref[half:, :] = value_ref[:half, :]


def first_expert_rows(expert, gain, halves, weights):
    units, model_width = weights[0].shape
    row_count = halves[0].shape[0]
    whole = pl.BlockSpec(memory_space=pltpu.VMEM)
    anywhere = pl.BlockSpec(memory_space=pltpu.HBM)
    chunks = 2 * units // UNITS
    return pl.pallas_call(
        first_expert_kernel,
        name="expert_first",
        compiler_params=pltpu.CompilerParams(vmem_limit_bytes=12 << 20),
        out_shape=(near_shape((row_count, model_width // 2), jnp.float32),) * 2
        + (near_shape((2 * units, model_width), jnp.bfloat16),) * 3,
        in_specs=[pl.BlockSpec(memory_space=pltpu.SMEM)] + [whole] * 3 + [anywhere] * 6,
        out_specs=(whole,) * 5,
        scratch_shapes=[
            pltpu.VMEM((model_width + LANES, row_count), jnp.bfloat16),
            pltpu.VMEM((row_count, 2 * units), jnp.bfloat16),
            pltpu.SemaphoreType.DMA((3, chunks)),
        ],
        cost_estimate=pl.CostEstimate(
            flops=12 * row_count * model_width * units,
            transcendentals=0,
            bytes_accessed=12 * units * model_width,
        ),
    )(
        expert,
        near(gain),
        *[near(half) for half in halves],
        *[far(weight) for weight in weights],
    )


def second_expert_rows(expert, gain, halves, weights, totals):
    units, model_width = weights[0].shape
    row_count = halves[0].shape[0]
    width = model_width // 2
    whole = pl.BlockSpec(memory_space=pltpu.VMEM)
    first, hidden = pl.pallas_call(
        second_expert_kernel,
        name="expert_second",
        compiler_params=pltpu.CompilerParams(vmem_limit_bytes=12 << 20),
        out_shape=(
            near_shape((row_count, width), jnp.bfloat16),
            near_shape((row_count, units), jnp.bfloat16),
        ),
        in_specs=[pl.BlockSpec(memory_space=pltpu.SMEM)] + [whole] * 6,
        out_specs=(whole, whole),
        scratch_shapes=[pltpu.VMEM((model_width + LANES, row_count), jnp.bfloat16)],
    )(
        expert,
        near(gain),
        *[near(half) for half in halves],
        *[near(weight) for weight in weights],
    )
    sent, kept = pl.pallas_call(
        functools.partial(rest_expert_kernel, width),
        name="expert_rest",
        compiler_params=pltpu.CompilerParams(vmem_limit_bytes=12 << 20),
        out_shape=(
            near_shape((row_count, width), jnp.bfloat16),
            near_shape((row_count, width), jnp.float32),
        ),
        in_specs=[whole] * 3,
        out_specs=(whole, whole),
        scratch_shapes=[pltpu.VMEM((row_count, width), jnp.float32)],
    )(near(hidden), near(weights[2]), near(totals[1]))
    return [(first, totals[0]), (sent, kept)]


def attention_rows(
    queries, patch_keys, patch_values, other_keys, other_values, table, row_count, orders
):
    model_width = patch_values.shape[1]
    part_width = model_width // PARTS + LANES
    part_heads = HEADS // PARTS
    stages = len(orders[0])
    device_index = lax.axis_index("wide")
    masks = [
        [
            sum(
                (1 << order[stage])
                for stage in range(stages)
                if slot >> (stages - 1 - stage) & 1
            )
            for slot in range(1 << stages)
        ]
        for order in orders
    ]
    rows = row_count << stages
    whole = pl.BlockSpec(memory_space=pltpu.VMEM)

    def pair_shapes(rows):
        return (
            near_shape((rows, part_width), jnp.bfloat16),
            near_shape((rows, part_width), jnp.float32),
        )

    anywhere = pl.BlockSpec(memory_space=pltpu.HBM)
    query_rows, own_keys, own_values = pl.pallas_call(
        functools.partial(stage_kernel, row_count, masks),
        name="stage_in",
        compiler_params=pltpu.CompilerParams(vmem_limit_bytes=4 << 20),
        out_shape=(
            near_shape((rows, queries.shape[1]), jnp.bfloat16),
            near_shape(patch_keys.shape, jnp.bfloat16),
            near_shape(patch_values.shape, jnp.bfloat16),
        ),
        in_specs=[pl.BlockSpec(memory_space=pltpu.SMEM)] + [anywhere] * 3,
        out_specs=(whole,) * 3,
        scratch_shapes=[pltpu.SemaphoreType.DMA((2 + (1 << stages),))],
    )(device_index.reshape(1), far(queries), far(patch_keys), far(patch_values))
    operands = (query_rows, own_keys, other_keys, own_values, other_values)
    chains = []
    for part in range(PARTS):
        chains += pl.pallas_call(
            functools.partial(attend_kernel, HEADS, part, part_heads),
            compiler_params=pltpu.CompilerParams(vmem_limit_bytes=8 << 20),
            out_shape=pair_shapes(rows // 2),
            in_specs=[whole] * 5,
            out_specs=(whole, whole),
        )(*[near(operand) for operand in operands])
    finished = []
    for part in range(PARTS):
        sent, kept = chains[2 * part : 2 * part + 2]
        for stage in range(stages - 1):
            came = exchange(sent, orders, stage)
            rows = kept.shape[0]
            last = stage == stages - 2
            operands = [near(kept), near(came)]
            if last and part == 0:
                operands.append(near(table))
            sent, kept = pl.pallas_call(
                functools.partial(last_merge_kernel if last else merge_kernel, part_heads),
                compiler_params=pltpu.CompilerParams(vmem_limit_bytes=6 << 20),
                out_shape=pair_shapes(rows if last else rows // 2),
                in_specs=[whole] * len(operands),
                out_specs=(whole, whole),
            )(*operands)
        came = exchange(sent, orders, stages - 1)
        rows = kept.shape[0]
        width = model_width // PARTS
        operands = [near(kept), near(came)] + ([near(table)] if part == 0 else [])
        block, projected = pl.pallas_call(
            functools.partial(finish_kernel, part_heads),
            compiler_params=pltpu.CompilerParams(vmem_limit_bytes=6 << 20),
            out_shape=(
                near_shape((rows, width + (LANES if part == 0 else 0)), jnp.bfloat16),
                near_shape((row_count, width), jnp.bfloat16),
            ),
            in_specs=[whole] * len(operands),
            out_specs=(whole, whole),
        )(*operands)
        finished.append((block, projected))
    return finished


def on_device(
    queries, patch_keys, patch_values, norm_gain, route_experts, route_weights, w_gate, w_up, w_down
):
    row_count = route_experts.shape[0]
    model_width = patch_values.shape[1]
    devices = lax.axis_size("wide")
    device_index = lax.axis_index("wide")
    score_table = jnp.sum(
        jnp.where(
            route_experts[:, :, None] == jnp.arange(-TABLE_LANE, LANES - TABLE_LANE, dtype=jnp.int32),
            route_weights[:, :, None],
            0,
        ),
        axis=1,
    ).astype(jnp.bfloat16)
    merge_order, gather_order, scatter_order = plan_orders(
        devices, queries.shape[0] // row_count
    )
    other_keys = partner(patch_keys, "wide", 0)
    other_values = partner(patch_values, "wide", 0)
    halves, other_keys, other_values = lax.optimization_barrier(
        ((w_gate, w_up, w_down), other_keys, other_values)
    )
    weights = []
    for own in halves:
        weights += [own, partner(own, "wide", 0)]
    finished = attention_rows(
        queries,
        patch_keys,
        patch_values,
        other_keys,
        other_values,
        score_table,
        row_count,
        merge_order,
    )
    blocks = [block for block, _ in finished]
    gain = norm_gain.reshape(1, model_width)
    stages = len(gather_order[0])
    came = []
    for part in range(PARTS):
        for stage in range(stages - 1):
            arrived = exchange(blocks[part], gather_order, stage)
            blocks[part] = jnp.concatenate([blocks[part], arrived], axis=0)
        came.append(exchange(blocks[part], gather_order, stages - 1))
    expert = (device_index // 2).reshape(1)
    *totals, gate, up, down = first_expert_rows(expert, gain, blocks, weights)
    outputs = []
    for part, (sent, kept) in enumerate(
        second_expert_rows(expert, gain, came, (gate, up, down), totals)
    ):
        for stage in range(stages + 1):
            arrived = exchange(sent, scatter_order[part], stage)
            kept = kept + arrived.astype(jnp.float32)
            half_rows = kept.shape[0] // 2
            if stage < stages:
                sent = kept[half_rows:].astype(jnp.bfloat16)
                kept = kept[:half_rows]
        outputs.append((finished[part][1].astype(jnp.float32) + kept).astype(jnp.bfloat16))
    return jnp.concatenate(outputs, axis=1)


def solution(mesh):
    return mapped(mesh)


def mapped(mesh):
    return jax.shard_map(
        on_device,
        mesh=mesh,
        in_specs=(
            P("groups", None),
            P(("groups", "wide"), None),
            P(("groups", "wide"), None),
            P(),
            P(("groups", "wide"), None),
            P(("groups", "wide"), None),
            P("wide", None),
            P("wide", None),
            P("wide", None),
        ),
        out_specs=P(("groups", "wide"), None),
        check_vma=False,
    )
```

```python
import functools

import jax
import jax.numpy as jnp
from jax import lax
from jax.experimental import pallas as pl
from jax.experimental.pallas import tpu as pltpu
from jax.sharding import PartitionSpec as P


HEADS = 16
LANES = 128
TABLE_LANE = 64
UNITS = 256
PARTS = 2


def near(value):
    return pltpu.with_memory_space_constraint(value, pltpu.VMEM)


def far(value):
    return pltpu.with_memory_space_constraint(value, pltpu.HBM)


def near_shape(shape, dtype):
    return pltpu.VMEM(shape, dtype)


def partner(value, axis, stride):
    mask = 2**stride
    pairs = [(source, source ^ mask) for source in range(lax.axis_size(axis))]
    return lax.ppermute(value, axis, pairs)


def plan_orders(devices, group_size):
    near_bits = list(range(1, group_size.bit_length() - 1))
    all_bits = list(range(1, devices.bit_length() - 1))
    merge = (near_bits, near_bits[1:] + near_bits[:1])
    rest = [[bit for bit in all_bits if bit != order[-1]] for order in merge]
    gather = (rest[0][::-1], rest[1][2:][::-1] + rest[1][:2])
    scatter = [order[::-1] + kept[-1:] for order, kept in zip(gather, merge)]
    crossed = [order[1::-1] + order[2:] for order in scatter]
    return merge, gather, (scatter, crossed)


def exchange(value, orders, stage):
    pairs = [
        (source, source ^ (1 << orders[source % 2][stage]))
        for source in range(lax.axis_size("wide"))
    ]
    return lax.ppermute(value, "wide", pairs)


def lane_iota(shape):
    return lax.broadcasted_iota(jnp.int32, shape, 1)


def expand_tile(columns, tile, value_size):
    first = tile * LANES // value_size
    last = (tile * LANES + LANES - 1) // value_size
    rows = columns[0].shape[0]
    out = jnp.broadcast_to(columns[first], (rows, LANES))
    for head in range(first + 1, last + 1):
        edge = head * value_size - tile * LANES
        out = jnp.where(lane_iota((rows, LANES)) < edge, out, columns[head])
    return out


def pack_stats(peak, total, head_count):
    lane = lane_iota(peak.shape)
    high = total.astype(jnp.bfloat16).astype(jnp.float32)
    low = total - high
    packed = jnp.where(lane < head_count, peak, 0.0)
    shifted = pltpu.roll(jnp.where(lane < head_count, high, 0.0), head_count, 1)
    shifted_low = pltpu.roll(jnp.where(lane < head_count, low, 0.0), 2 * head_count, 1)
    return packed + shifted + shifted_low


def total_of(stats, head_count):
    return pltpu.roll(stats, LANES - head_count, 1) + pltpu.roll(
        stats, LANES - 2 * head_count, 1
    )


def head_windows(head, size):
    return head * size // LANES, -(-(head + 1) * size // LANES)


def head_scores(head, head_count, query_ref, keys_ref):
    key_size = query_ref.shape[1] // head_count
    low, high = [LANES * tile for tile in head_windows(head, key_size)]
    window = lane_iota((query_ref.shape[0], high - low)) + low
    inside = (window >= head * key_size) & (window < (head + 1) * key_size)
    query = jnp.where(inside, query_ref[:, low:high], jnp.zeros((), jnp.bfloat16))
    return key_size ** (-0.5) * lax.dot_general(
        query,
        keys_ref[:, low:high],
        (((1,), (1,)), ((), ())),
        preferred_element_type=jnp.float32,
    )


def rounded_peak(scores):
    peak = jnp.max(scores, axis=1, keepdims=True)
    return peak.astype(jnp.bfloat16).astype(jnp.float32)


def head_sums(head, value_size, raised, values_ref):
    low, high = head_windows(head, value_size)
    return jnp.dot(
        raised.astype(jnp.bfloat16),
        values_ref[:, low * LANES : high * LANES],
        preferred_element_type=jnp.float32,
    )


def stage_kernel(
    row_count,
    masks,
    device_ref,
    queries_ref,
    keys_ref,
    values_ref,
    query_ref,
    near_keys_ref,
    near_values_ref,
    arrived,
):
    group_size = queries_ref.shape[0] // row_count
    device = device_ref[0]
    odd = lax.rem(device, 2) == 1
    own_block = lax.rem(device, group_size)
    copies = [
        pltpu.make_async_copy(keys_ref, near_keys_ref, arrived.at[0]),
        pltpu.make_async_copy(values_ref, near_values_ref, arrived.at[1]),
    ]
    for slot, (even_mask, odd_mask) in enumerate(zip(*masks)):
        block = own_block ^ jnp.where(odd, odd_mask, even_mask)
        start = pl.multiple_of(block * row_count, row_count)
        copies.append(
            pltpu.make_async_copy(
                queries_ref.at[pl.ds(start, row_count), :],
                query_ref.at[slot * row_count : (slot + 1) * row_count, :],
                arrived.at[2 + slot],
            )
        )
    for copy in copies:
        copy.start()
    for copy in copies:
        copy.wait()


def attend_kernel(
    head_count, part, part_heads, query_ref, keys_a, keys_b, values_a, values_b, sent_ref, kept_ref
):
    rows = query_ref.shape[0]
    half = rows // 2
    value_size = values_a.shape[1] // head_count
    part_tiles = part_heads * value_size // LANES
    base = part * part_tiles
    lane = lane_iota((rows, LANES))
    peaks = jnp.zeros((rows, LANES), jnp.float32)
    totals = jnp.zeros((rows, LANES), jnp.float32)

    def put(tile, value):
        columns = slice(tile * LANES, (tile + 1) * LANES)
        kept_ref[:, columns] = value[:half]
        sent_ref[:, columns] = value[half:].astype(jnp.bfloat16)

    for at in range(part_heads):
        head = part * part_heads + at
        scores_a = head_scores(head, head_count, query_ref, keys_a)
        scores_b = head_scores(head, head_count, query_ref, keys_b)
        peak = jnp.maximum(rounded_peak(scores_a), rounded_peak(scores_b))
        raised_a = jnp.exp(scores_a - peak)
        raised_b = jnp.exp(scores_b - peak)
        total = jnp.sum(raised_a + raised_b, axis=1, keepdims=True)
        peaks = jnp.where(lane == at, peak, peaks)
        totals = jnp.where(lane == at, total, totals)
        summed = head_sums(head, value_size, raised_a, values_a) + head_sums(
            head, value_size, raised_b, values_b
        )
        low, high = head_windows(head, value_size)
        for tile in range(low, high):
            value = summed[:, (tile - low) * LANES : (tile - low + 1) * LANES]
            edge = head * value_size - tile * LANES
            if edge > 0:
                value = jnp.where(lane < edge, waiting, value)
            waiting = value
            if (tile + 1) * LANES <= (head + 1) * value_size:
                put(tile - base, value)
    put(part_tiles, pack_stats(peaks, totals, part_heads))


def merged_parts(kept_ref, came_ref, head_count, model_width):
    stats_a = kept_ref[:, model_width:]
    stats_b = came_ref[:, model_width:].astype(jnp.float32)
    peak = jnp.maximum(stats_a, stats_b)
    factor_a = jnp.exp(stats_a - peak)
    factor_b = jnp.exp(stats_b - peak)
    total = total_of(stats_a, head_count) * factor_a + total_of(stats_b, head_count) * factor_b
    return peak, total, factor_a, factor_b


def head_columns(array, head_count):
    return [array[:, head : head + 1] for head in range(head_count)]


def merge_kernel(head_count, kept_ref, came_ref, sent_ref, next_ref):
    model_width = kept_ref.shape[1] - LANES
    half = kept_ref.shape[0] // 2
    peak, total, factor_a, factor_b = merged_parts(kept_ref, came_ref, head_count, model_width)
    columns_a = head_columns(factor_a, head_count)
    columns_b = head_columns(factor_b, head_count)
    for tile in range(model_width // LANES + 1):
        columns = slice(tile * LANES, (tile + 1) * LANES)
        if tile * LANES == model_width:
            value = pack_stats(peak, total, head_count)
        else:
            value = kept_ref[:, columns] * expand_tile(
                columns_a, tile, model_width // head_count
            ) + came_ref[:, columns].astype(jnp.float32) * expand_tile(
                columns_b, tile, model_width // head_count
            )
        next_ref[:, columns] = value[:half]
        sent_ref[:, columns] = value[half:].astype(jnp.bfloat16)


def last_merge_kernel(head_count, kept_ref, came_ref, *rest):
    tables, (sent_ref, next_ref) = rest[:-2], rest[-2:]
    model_width = kept_ref.shape[1] - LANES
    half = kept_ref.shape[0] // 2
    peak, total, factor_a, factor_b = merged_parts(kept_ref, came_ref, head_count, model_width)
    columns_a = head_columns(factor_a, head_count)
    columns_b = head_columns(factor_b, head_count)
    for tile in range(model_width // LANES + 1):
        columns = slice(tile * LANES, (tile + 1) * LANES)
        if tile * LANES == model_width:
            value = pack_stats(peak, total, head_count)
            own = value[:half]
            for table_ref in tables:
                own = own + table_ref[...].astype(jnp.float32)
        else:
            value = kept_ref[:, columns] * expand_tile(
                columns_a, tile, model_width // head_count
            ) + came_ref[:, columns].astype(jnp.float32) * expand_tile(
                columns_b, tile, model_width // head_count
            )
            own = value[:half]
        next_ref[:, columns] = value
        sent_ref[:half, columns] = value[half:].astype(jnp.bfloat16)
        sent_ref[half:, columns] = own.astype(jnp.bfloat16)


def finish_kernel(part_heads, kept_ref, came_ref, *rest):
    tables, (block_ref, projected_ref) = rest[:-2], rest[-2:]
    half = kept_ref.shape[0] // 2
    width = kept_ref.shape[1] - LANES
    _, total, factor_a, factor_b = merged_parts(kept_ref, came_ref, part_heads, width)
    columns_a = head_columns(factor_a / total, part_heads)
    columns_b = head_columns(factor_b / total, part_heads)
    for tile in range(width // LANES):
        columns = slice(tile * LANES, (tile + 1) * LANES)
        value = kept_ref[:, columns] * expand_tile(
            columns_a, tile, width // part_heads
        ) + came_ref[:, columns].astype(jnp.float32) * expand_tile(
            columns_b, tile, width // part_heads
        )
        rounded = value.astype(jnp.bfloat16)
        block_ref[:, columns] = rounded
        projected_ref[:, columns] = rounded[:half]
    for table_ref in tables:
        came_table = came_ref[half:, width:]
        lane = lane_iota(came_table.shape)
        block_ref[:half, width:] = table_ref[...]
        block_ref[half:, width:] = jnp.where(
            lane >= TABLE_LANE, came_table.astype(jnp.float32), 0.0
        ).astype(jnp.bfloat16)


def hidden_units(expert_ref, gain_ref, row_refs, gate_ref, up_ref, turned, hidden, ready):
    width = row_refs[1].shape[1]
    model_width = width * len(row_refs)
    square = jnp.zeros((row_refs[0].shape[0], LANES), jnp.float32)
    for rows_ref in row_refs:
        for low in range(0, width, LANES):
            residual = rows_ref[:, low : low + LANES].astype(jnp.float32)
            square = square + residual * residual
    mean = jnp.sum(square, axis=1, keepdims=True) / model_width
    inverse = jnp.broadcast_to(lax.rsqrt(mean + 1e-06), square.shape)
    for part, rows_ref in enumerate(row_refs):
        for low in range(0, width, LANES):
            at = part * width + low
            residual = rows_ref[:, low : low + LANES].astype(jnp.float32)
            normed = residual * inverse * gain_ref[:, at : at + LANES]
            turned[at : at + LANES, :] = normed.astype(jnp.bfloat16).T
    turned[model_width:, :] = row_refs[0][:, width:].T
    scores = turned[model_width:, :].astype(jnp.float32)
    lane = lax.broadcasted_iota(jnp.int32, scores.shape, 0)
    chosen = jnp.where(lane == expert_ref[0] + TABLE_LANE, scores, 0.0)
    share = jnp.sum(chosen, axis=0, keepdims=True) / jnp.sum(scores, axis=0, keepdims=True)
    rows = turned[:model_width, :]
    for chunk in range(gate_ref.shape[0] // UNITS):
        ready(chunk)
        units = slice(chunk * UNITS, (chunk + 1) * UNITS)
        gate_part = jnp.dot(gate_ref[units, :], rows, preferred_element_type=jnp.float32)
        up_part = jnp.dot(up_ref[units, :], rows, preferred_element_type=jnp.float32)
        silu = gate_part / (1.0 + jnp.exp(-gate_part))
        hidden[:, units] = (silu * up_part * share).T.astype(jnp.bfloat16)


def down_product(hidden_ref, down_ref, out_ref, start):
    width = out_ref.shape[1]
    step = width // 2 if width % (4 * LANES) else 4 * LANES
    for low in range(0, width, step):
        out_ref[:, low : low + step] = jnp.dot(
            hidden_ref[...],
            down_ref[:, start + low : start + low + step],
            preferred_element_type=jnp.float32,
        ).astype(out_ref.dtype)


def first_expert_kernel(
    expert_ref,
    gain_ref,
    rows_a,
    rows_b,
    gate_a,
    gate_b,
    up_a,
    up_b,
    down_a,
    down_b,
    out_a,
    out_b,
    gate_ref,
    up_ref,
    down_ref,
    turned,
    hidden,
    arrived,
):
    per_half = gate_a.shape[0] // UNITS
    chunks = 2 * per_half
    pairs = ((gate_a, gate_b), (up_a, up_b), (down_a, down_b))
    targets = (gate_ref, up_ref, down_ref)

    def copy_of(part, chunk):
        low = chunk % per_half * UNITS
        return pltpu.make_async_copy(
            pairs[part][chunk // per_half].at[low : low + UNITS, :],
            targets[part].at[chunk * UNITS : (chunk + 1) * UNITS, :],
            arrived.at[part, chunk],
        )

    for chunk in range(chunks):
        for part in range(2):
            copy_of(part, chunk).start()
    for chunk in range(chunks):
        copy_of(2, chunk).start()

    def ready(chunk):
        copy_of(0, chunk).wait()
        copy_of(1, chunk).wait()

    hidden_units(
        expert_ref, gain_ref, (rows_a, rows_b), gate_ref, up_ref, turned, hidden, ready
    )
    for chunk in range(chunks):
        copy_of(2, chunk).wait()
    down_product(hidden, down_ref, out_a, 0)
    down_product(hidden, down_ref, out_b, out_a.shape[1])


def turned_half(rows_ref, gain_ref, start, width, turned):
    square = jnp.zeros((rows_ref.shape[0], LANES), jnp.float32)
    for low in range(0, width, LANES):
        residual = rows_ref[:, low : low + LANES].astype(jnp.float32)
        square = square + residual * residual
        gained = residual * gain_ref[:, start + low : start + low + LANES]
        turned[low : low + LANES, :] = gained.astype(jnp.bfloat16).T
    return jnp.sum(square.T, axis=0, keepdims=True)


def half_expert_kernel(
    expert_ref, gain_ref, rows_ref, gate_ref, up_ref, gates_ref, ups_ref, stats_ref, turned
):
    width = turned.shape[0]
    stats_ref[0:1, :] = turned_half(rows_ref, gain_ref, 0, width, turned)
    scores = rows_ref[:, width:].astype(jnp.float32).T
    lane = lax.broadcasted_iota(jnp.int32, scores.shape, 0)
    chosen = jnp.where(lane == expert_ref[0] + TABLE_LANE, scores, 0.0)
    stats_ref[1:2, :] = jnp.sum(chosen, axis=0, keepdims=True) / jnp.sum(
        scores, axis=0, keepdims=True
    )
    rows = turned[...]
    gates_ref[...] = jnp.dot(gate_ref[:, :width], rows, preferred_element_type=jnp.float32)
    ups_ref[...] = jnp.dot(up_ref[:, :width], rows, preferred_element_type=jnp.float32)


def second_expert_kernel(
    gain_ref,
    rows_ref,
    gates_ref,
    ups_ref,
    stats_ref,
    gate_ref,
    up_ref,
    down_ref,
    out_ref,
    hidden,
    turned,
):
    width = turned.shape[0]
    square = stats_ref[0:1, :] + turned_half(rows_ref, gain_ref, width, width, turned)
    inverse = lax.rsqrt(square / (2 * width) + 1e-06)
    share = stats_ref[1:2, :]
    rows = turned[...]
    for low in range(0, gate_ref.shape[0], UNITS):
        units = slice(low, low + UNITS)
        gate_part = inverse * (
            gates_ref[units, :]
            + jnp.dot(gate_ref[units, width:], rows, preferred_element_type=jnp.float32)
        )
        up_part = inverse * (
            ups_ref[units, :]
            + jnp.dot(up_ref[units, width:], rows, preferred_element_type=jnp.float32)
        )
        silu = gate_part / (1.0 + jnp.exp(-gate_part))
        hidden[:, units] = (silu * up_part * share).T.astype(jnp.bfloat16)
    down_product(hidden, down_ref, out_ref, 0)


def rest_expert_kernel(start, hidden_ref, down_ref, first_ref, sent_ref, kept_ref, value_ref):
    down_product(hidden_ref, down_ref, value_ref, start)
    half = first_ref.shape[0] // 2
    sent_ref[:half, :] = first_ref[half:, :].astype(sent_ref.dtype)
    sent_ref[half:, :] = value_ref[half:, :].astype(sent_ref.dtype)
    kept_ref[:half, :] = first_ref[:half, :]
    kept_ref[half:, :] = value_ref[:half, :]


def first_expert_rows(expert, gain, halves, weights):
    units, model_width = weights[0].shape
    row_count = halves[0].shape[0]
    whole = pl.BlockSpec(memory_space=pltpu.VMEM)
    anywhere = pl.BlockSpec(memory_space=pltpu.HBM)
    chunks = 2 * units // UNITS
    return pl.pallas_call(
        first_expert_kernel,
        name="expert_first",
        compiler_params=pltpu.CompilerParams(vmem_limit_bytes=12 << 20),
        out_shape=(near_shape((row_count, model_width // 2), jnp.float32),) * 2
        + (near_shape((2 * units, model_width), jnp.bfloat16),) * 3,
        in_specs=[pl.BlockSpec(memory_space=pltpu.SMEM)] + [whole] * 3 + [anywhere] * 6,
        out_specs=(whole,) * 5,
        scratch_shapes=[
            pltpu.VMEM((model_width + LANES, row_count), jnp.bfloat16),
            pltpu.VMEM((row_count, 2 * units), jnp.bfloat16),
            pltpu.SemaphoreType.DMA((3, chunks)),
        ],
        cost_estimate=pl.CostEstimate(
            flops=12 * row_count * model_width * units,
            transcendentals=0,
            bytes_accessed=12 * units * model_width,
        ),
    )(
        expert,
        near(gain),
        *[near(half) for half in halves],
        *[far(weight) for weight in weights],
    )


def second_expert_rows(expert, gain, halves, weights, totals):
    units, model_width = weights[0].shape
    row_count = halves[0].shape[0]
    width = model_width // 2
    whole = pl.BlockSpec(memory_space=pltpu.VMEM)
    gate, up, down = weights
    gates, ups, stats = pl.pallas_call(
        half_expert_kernel,
        name="expert_half",
        compiler_params=pltpu.CompilerParams(vmem_limit_bytes=12 << 20),
        out_shape=(near_shape((units, row_count), jnp.float32),) * 2
        + (near_shape((8, row_count), jnp.float32),),
        in_specs=[pl.BlockSpec(memory_space=pltpu.SMEM)] + [whole] * 4,
        out_specs=(whole,) * 3,
        scratch_shapes=[pltpu.VMEM((width, row_count), jnp.bfloat16)],
    )(expert, near(gain), near(halves[0]), near(gate), near(up))
    first, hidden = pl.pallas_call(
        second_expert_kernel,
        name="expert_second",
        compiler_params=pltpu.CompilerParams(vmem_limit_bytes=12 << 20),
        out_shape=(
            near_shape((row_count, width), jnp.bfloat16),
            near_shape((row_count, units), jnp.bfloat16),
        ),
        in_specs=[whole] * 8,
        out_specs=(whole, whole),
        scratch_shapes=[pltpu.VMEM((width, row_count), jnp.bfloat16)],
    )(near(gain), near(halves[1]), near(gates), near(ups), near(stats), near(gate), near(up), near(down))
    sent, kept = pl.pallas_call(
        functools.partial(rest_expert_kernel, width),
        name="expert_rest",
        compiler_params=pltpu.CompilerParams(vmem_limit_bytes=12 << 20),
        out_shape=(
            near_shape((row_count, width), jnp.bfloat16),
            near_shape((row_count, width), jnp.float32),
        ),
        in_specs=[whole] * 3,
        out_specs=(whole, whole),
        scratch_shapes=[pltpu.VMEM((row_count, width), jnp.float32)],
    )(near(hidden), near(weights[2]), near(totals[1]))
    return [(first, totals[0]), (sent, kept)]


def attention_rows(
    queries, patch_keys, patch_values, other_keys, other_values, table, row_count, orders
):
    model_width = patch_values.shape[1]
    part_width = model_width // PARTS + LANES
    part_heads = HEADS // PARTS
    stages = len(orders[0])
    device_index = lax.axis_index("wide")
    masks = [
        [
            sum(
                (1 << order[stage])
                for stage in range(stages)
                if slot >> (stages - 1 - stage) & 1
            )
            for slot in range(1 << stages)
        ]
        for order in orders
    ]
    rows = row_count << stages
    whole = pl.BlockSpec(memory_space=pltpu.VMEM)

    def pair_shapes(rows):
        return (
            near_shape((rows, part_width), jnp.bfloat16),
            near_shape((rows, part_width), jnp.float32),
        )

    anywhere = pl.BlockSpec(memory_space=pltpu.HBM)
    query_rows, own_keys, own_values = pl.pallas_call(
        functools.partial(stage_kernel, row_count, masks),
        name="stage_in",
        compiler_params=pltpu.CompilerParams(vmem_limit_bytes=4 << 20),
        out_shape=(
            near_shape((rows, queries.shape[1]), jnp.bfloat16),
            near_shape(patch_keys.shape, jnp.bfloat16),
            near_shape(patch_values.shape, jnp.bfloat16),
        ),
        in_specs=[pl.BlockSpec(memory_space=pltpu.SMEM)] + [anywhere] * 3,
        out_specs=(whole,) * 3,
        scratch_shapes=[pltpu.SemaphoreType.DMA((2 + (1 << stages),))],
    )(device_index.reshape(1), far(queries), far(patch_keys), far(patch_values))
    operands = (query_rows, own_keys, other_keys, own_values, other_values)
    chains = []
    for part in range(PARTS):
        chains += pl.pallas_call(
            functools.partial(attend_kernel, HEADS, part, part_heads),
            compiler_params=pltpu.CompilerParams(vmem_limit_bytes=8 << 20),
            out_shape=pair_shapes(rows // 2),
            in_specs=[whole] * 5,
            out_specs=(whole, whole),
        )(*[near(operand) for operand in operands])
    finished = []
    for part in range(PARTS):
        sent, kept = chains[2 * part : 2 * part + 2]
        for stage in range(stages - 1):
            came = exchange(sent, orders, stage)
            rows = kept.shape[0]
            last = stage == stages - 2
            operands = [near(kept), near(came)]
            if last and part == 0:
                operands.append(near(table))
            sent, kept = pl.pallas_call(
                functools.partial(last_merge_kernel if last else merge_kernel, part_heads),
                compiler_params=pltpu.CompilerParams(vmem_limit_bytes=6 << 20),
                out_shape=pair_shapes(rows if last else rows // 2),
                in_specs=[whole] * len(operands),
                out_specs=(whole, whole),
            )(*operands)
        came = exchange(sent, orders, stages - 1)
        rows = kept.shape[0]
        width = model_width // PARTS
        operands = [near(kept), near(came)] + ([near(table)] if part == 0 else [])
        block, projected = pl.pallas_call(
            functools.partial(finish_kernel, part_heads),
            compiler_params=pltpu.CompilerParams(vmem_limit_bytes=6 << 20),
            out_shape=(
                near_shape((rows, width + (LANES if part == 0 else 0)), jnp.bfloat16),
                near_shape((row_count, width), jnp.bfloat16),
            ),
            in_specs=[whole] * len(operands),
            out_specs=(whole, whole),
        )(*operands)
        finished.append((block, projected))
    return finished


def on_device(
    queries, patch_keys, patch_values, norm_gain, route_experts, route_weights, w_gate, w_up, w_down
):
    row_count = route_experts.shape[0]
    model_width = patch_values.shape[1]
    devices = lax.axis_size("wide")
    device_index = lax.axis_index("wide")
    score_table = jnp.sum(
        jnp.where(
            route_experts[:, :, None] == jnp.arange(-TABLE_LANE, LANES - TABLE_LANE, dtype=jnp.int32),
            route_weights[:, :, None],
            0,
        ),
        axis=1,
    ).astype(jnp.bfloat16)
    merge_order, gather_order, scatter_order = plan_orders(
        devices, queries.shape[0] // row_count
    )
    other_keys = partner(patch_keys, "wide", 0)
    other_values = partner(patch_values, "wide", 0)
    halves, other_keys, other_values = lax.optimization_barrier(
        ((w_gate, w_up, w_down), other_keys, other_values)
    )
    weights = []
    for own in halves:
        weights += [own, partner(own, "wide", 0)]
    finished = attention_rows(
        queries,
        patch_keys,
        patch_values,
        other_keys,
        other_values,
        score_table,
        row_count,
        merge_order,
    )
    blocks = [block for block, _ in finished]
    gain = norm_gain.reshape(1, model_width)
    stages = len(gather_order[0])
    came = []
    for part in range(PARTS):
        for stage in range(stages - 1):
            arrived = exchange(blocks[part], gather_order, stage)
            blocks[part] = jnp.concatenate([blocks[part], arrived], axis=0)
        came.append(exchange(blocks[part], gather_order, stages - 1))
    expert = (device_index // 2).reshape(1)
    *totals, gate, up, down = first_expert_rows(expert, gain, blocks, weights)
    outputs = []
    for part, (sent, kept) in enumerate(
        second_expert_rows(expert, gain, came, (gate, up, down), totals)
    ):
        for stage in range(stages + 1):
            arrived = exchange(sent, scatter_order[part], stage)
            kept = kept + arrived.astype(jnp.float32)
            half_rows = kept.shape[0] // 2
            if stage < stages:
                sent = kept[half_rows:].astype(jnp.bfloat16)
                kept = kept[:half_rows]
        outputs.append((finished[part][1].astype(jnp.float32) + kept).astype(jnp.bfloat16))
    return jnp.concatenate(outputs, axis=1)


def solution(mesh):
    return mapped(mesh)


def mapped(mesh):
    return jax.shard_map(
        on_device,
        mesh=mesh,
        in_specs=(
            P("groups", None),
            P(("groups", "wide"), None),
            P(("groups", "wide"), None),
            P(),
            P(("groups", "wide"), None),
            P(("groups", "wide"), None),
            P("wide", None),
            P("wide", None),
            P("wide", None),
        ),
        out_specs=P(("groups", "wide"), None),
        check_vma=False,
    )
```

```python
import functools

import jax
import jax.numpy as jnp
from jax import lax
from jax.experimental import pallas as pl
from jax.experimental.pallas import tpu as pltpu
from jax.sharding import PartitionSpec as P


HEADS = 16
LANES = 128
TABLE_LANE = 64
UNITS = 256
PARTS = 2


def near(value):
    return pltpu.with_memory_space_constraint(value, pltpu.VMEM)


def far(value):
    return pltpu.with_memory_space_constraint(value, pltpu.HBM)


def near_shape(shape, dtype):
    return pltpu.VMEM(shape, dtype)


def partner(value, axis, stride):
    mask = 2**stride
    pairs = [(source, source ^ mask) for source in range(lax.axis_size(axis))]
    return lax.ppermute(value, axis, pairs)


def plan_orders(devices, group_size):
    near_bits = list(range(1, group_size.bit_length() - 1))
    all_bits = list(range(1, devices.bit_length() - 1))
    merge = (near_bits, near_bits[1:] + near_bits[:1])
    rest = [[bit for bit in all_bits if bit != order[-1]] for order in merge]
    gather = (rest[0][::-1], rest[1][2:][::-1] + rest[1][:2])
    scatter = [order[::-1] + kept[-1:] for order, kept in zip(gather, merge)]
    crossed = [order[1::-1] + order[2:] for order in scatter]
    return merge, gather, (scatter, crossed)


def exchange(value, orders, stage):
    pairs = [
        (source, source ^ (1 << orders[source % 2][stage]))
        for source in range(lax.axis_size("wide"))
    ]
    return lax.ppermute(value, "wide", pairs)


def lane_iota(shape):
    return lax.broadcasted_iota(jnp.int32, shape, 1)


def expand_tile(columns, tile, value_size):
    first = tile * LANES // value_size
    last = (tile * LANES + LANES - 1) // value_size
    rows = columns[0].shape[0]
    out = jnp.broadcast_to(columns[first], (rows, LANES))
    for head in range(first + 1, last + 1):
        edge = head * value_size - tile * LANES
        out = jnp.where(lane_iota((rows, LANES)) < edge, out, columns[head])
    return out


def pack_stats(peak, total, head_count):
    lane = lane_iota(peak.shape)
    high = total.astype(jnp.bfloat16).astype(jnp.float32)
    low = total - high
    packed = jnp.where(lane < head_count, peak, 0.0)
    shifted = pltpu.roll(jnp.where(lane < head_count, high, 0.0), head_count, 1)
    shifted_low = pltpu.roll(jnp.where(lane < head_count, low, 0.0), 2 * head_count, 1)
    return packed + shifted + shifted_low


def total_of(stats, head_count):
    return pltpu.roll(stats, LANES - head_count, 1) + pltpu.roll(
        stats, LANES - 2 * head_count, 1
    )


def head_windows(head, size):
    return head * size // LANES, -(-(head + 1) * size // LANES)


def head_scores(head, head_count, query_ref, keys_ref):
    key_size = query_ref.shape[1] // head_count
    low, high = [LANES * tile for tile in head_windows(head, key_size)]
    window = lane_iota((query_ref.shape[0], high - low)) + low
    inside = (window >= head * key_size) & (window < (head + 1) * key_size)
    query = jnp.where(inside, query_ref[:, low:high], jnp.zeros((), jnp.bfloat16))
    return key_size ** (-0.5) * lax.dot_general(
        query,
        keys_ref[:, low:high],
        (((1,), (1,)), ((), ())),
        preferred_element_type=jnp.float32,
    )


def rounded_peak(scores):
    peak = jnp.max(scores, axis=1, keepdims=True)
    return peak.astype(jnp.bfloat16).astype(jnp.float32)


def head_sums(head, value_size, raised, values_ref):
    low, high = head_windows(head, value_size)
    return jnp.dot(
        raised.astype(jnp.bfloat16),
        values_ref[:, low * LANES : high * LANES],
        preferred_element_type=jnp.float32,
    )


def stage_kernel(
    row_count,
    masks,
    device_ref,
    queries_ref,
    keys_ref,
    values_ref,
    gain_ref,
    query_ref,
    near_keys_ref,
    near_values_ref,
    near_gain_ref,
    arrived,
):
    group_size = queries_ref.shape[0] // row_count
    device = device_ref[0]
    odd = lax.rem(device, 2) == 1
    own_block = lax.rem(device, group_size)
    copies = [
        pltpu.make_async_copy(keys_ref, near_keys_ref, arrived.at[0]),
        pltpu.make_async_copy(values_ref, near_values_ref, arrived.at[1]),
        pltpu.make_async_copy(gain_ref, near_gain_ref, arrived.at[2]),
    ]
    for slot, (even_mask, odd_mask) in enumerate(zip(*masks)):
        block = own_block ^ jnp.where(odd, odd_mask, even_mask)
        start = pl.multiple_of(block * row_count, row_count)
        copies.append(
            pltpu.make_async_copy(
                queries_ref.at[pl.ds(start, row_count), :],
                query_ref.at[slot * row_count : (slot + 1) * row_count, :],
                arrived.at[3 + slot],
            )
        )
    for copy in copies:
        copy.start()
    for copy in copies:
        copy.wait()


def attend_kernel(
    head_count, part, part_heads, query_ref, keys_a, keys_b, values_a, values_b, sent_ref, kept_ref
):
    rows = query_ref.shape[0]
    half = rows // 2
    value_size = values_a.shape[1] // head_count
    part_tiles = part_heads * value_size // LANES
    base = part * part_tiles
    lane = lane_iota((rows, LANES))
    peaks = jnp.zeros((rows, LANES), jnp.float32)
    totals = jnp.zeros((rows, LANES), jnp.float32)

    def put(tile, value):
        columns = slice(tile * LANES, (tile + 1) * LANES)
        kept_ref[:, columns] = value[:half]
        sent_ref[:, columns] = value[half:].astype(jnp.bfloat16)

    for at in range(part_heads):
        head = part * part_heads + at
        scores_a = head_scores(head, head_count, query_ref, keys_a)
        scores_b = head_scores(head, head_count, query_ref, keys_b)
        peak = jnp.maximum(rounded_peak(scores_a), rounded_peak(scores_b))
        raised_a = jnp.exp(scores_a - peak)
        raised_b = jnp.exp(scores_b - peak)
        total = jnp.sum(raised_a + raised_b, axis=1, keepdims=True)
        peaks = jnp.where(lane == at, peak, peaks)
        totals = jnp.where(lane == at, total, totals)
        summed = head_sums(head, value_size, raised_a, values_a) + head_sums(
            head, value_size, raised_b, values_b
        )
        low, high = head_windows(head, value_size)
        for tile in range(low, high):
            value = summed[:, (tile - low) * LANES : (tile - low + 1) * LANES]
            edge = head * value_size - tile * LANES
            if edge > 0:
                value = jnp.where(lane < edge, waiting, value)
            waiting = value
            if (tile + 1) * LANES <= (head + 1) * value_size:
                put(tile - base, value)
    put(part_tiles, pack_stats(peaks, totals, part_heads))


def merged_parts(kept_ref, came_ref, head_count, model_width):
    stats_a = kept_ref[:, model_width:]
    stats_b = came_ref[:, model_width:].astype(jnp.float32)
    peak = jnp.maximum(stats_a, stats_b)
    factor_a = jnp.exp(stats_a - peak)
    factor_b = jnp.exp(stats_b - peak)
    total = total_of(stats_a, head_count) * factor_a + total_of(stats_b, head_count) * factor_b
    return peak, total, factor_a, factor_b


def head_columns(array, head_count):
    return [array[:, head : head + 1] for head in range(head_count)]


def merge_kernel(head_count, kept_ref, came_ref, sent_ref, next_ref):
    model_width = kept_ref.shape[1] - LANES
    half = kept_ref.shape[0] // 2
    peak, total, factor_a, factor_b = merged_parts(kept_ref, came_ref, head_count, model_width)
    columns_a = head_columns(factor_a, head_count)
    columns_b = head_columns(factor_b, head_count)
    for tile in range(model_width // LANES + 1):
        columns = slice(tile * LANES, (tile + 1) * LANES)
        if tile * LANES == model_width:
            value = pack_stats(peak, total, head_count)
        else:
            value = kept_ref[:, columns] * expand_tile(
                columns_a, tile, model_width // head_count
            ) + came_ref[:, columns].astype(jnp.float32) * expand_tile(
                columns_b, tile, model_width // head_count
            )
        next_ref[:, columns] = value[:half]
        sent_ref[:, columns] = value[half:].astype(jnp.bfloat16)


def last_merge_kernel(head_count, kept_ref, came_ref, *rest):
    tables, (sent_ref, next_ref) = rest[:-2], rest[-2:]
    model_width = kept_ref.shape[1] - LANES
    half = kept_ref.shape[0] // 2
    peak, total, factor_a, factor_b = merged_parts(kept_ref, came_ref, head_count, model_width)
    columns_a = head_columns(factor_a, head_count)
    columns_b = head_columns(factor_b, head_count)
    for tile in range(model_width // LANES + 1):
        columns = slice(tile * LANES, (tile + 1) * LANES)
        if tile * LANES == model_width:
            value = pack_stats(peak, total, head_count)
            own = value[:half]
            for table_ref in tables:
                own = own + table_ref[...].astype(jnp.float32)
        else:
            value = kept_ref[:, columns] * expand_tile(
                columns_a, tile, model_width // head_count
            ) + came_ref[:, columns].astype(jnp.float32) * expand_tile(
                columns_b, tile, model_width // head_count
            )
            own = value[:half]
        next_ref[:, columns] = value
        sent_ref[:half, columns] = value[half:].astype(jnp.bfloat16)
        sent_ref[half:, columns] = own.astype(jnp.bfloat16)


def finish_kernel(part_heads, kept_ref, came_ref, *rest):
    tables, (block_ref, projected_ref) = rest[:-2], rest[-2:]
    half = kept_ref.shape[0] // 2
    width = kept_ref.shape[1] - LANES
    _, total, factor_a, factor_b = merged_parts(kept_ref, came_ref, part_heads, width)
    columns_a = head_columns(factor_a / total, part_heads)
    columns_b = head_columns(factor_b / total, part_heads)
    for tile in range(width // LANES):
        columns = slice(tile * LANES, (tile + 1) * LANES)
        value = kept_ref[:, columns] * expand_tile(
            columns_a, tile, width // part_heads
        ) + came_ref[:, columns].astype(jnp.float32) * expand_tile(
            columns_b, tile, width // part_heads
        )
        rounded = value.astype(jnp.bfloat16)
        block_ref[:, columns] = rounded
        projected_ref[:, columns] = rounded[:half]
    for table_ref in tables:
        came_table = came_ref[half:, width:]
        lane = lane_iota(came_table.shape)
        block_ref[:half, width:] = table_ref[...]
        block_ref[half:, width:] = jnp.where(
            lane >= TABLE_LANE, came_table.astype(jnp.float32), 0.0
        ).astype(jnp.bfloat16)


def normed_rows(device_ref, gain_ref, row_refs, turned):
    width = row_refs[1].shape[1]
    model_width = width * len(row_refs)
    square = jnp.zeros((row_refs[0].shape[0], LANES), jnp.float32)
    for rows_ref in row_refs:
        for low in range(0, width, LANES):
            residual = rows_ref[:, low : low + LANES].astype(jnp.float32)
            square = square + residual * residual
    mean = jnp.sum(square, axis=1, keepdims=True) / model_width
    inverse = jnp.broadcast_to(lax.rsqrt(mean + 1e-06), square.shape)
    for part, rows_ref in enumerate(row_refs):
        for low in range(0, width, LANES):
            at = part * width + low
            residual = rows_ref[:, low : low + LANES].astype(jnp.float32)
            normed = residual * inverse * gain_ref[:, at : at + LANES]
            turned[at : at + LANES, :] = normed.astype(jnp.bfloat16).T
    turned[model_width:, :] = row_refs[0][:, width:].T
    scores = turned[model_width:, :].astype(jnp.float32)
    lane = lax.broadcasted_iota(jnp.int32, scores.shape, 0)
    chosen = jnp.where(lane == lax.div(device_ref[0], 2) + TABLE_LANE, scores, 0.0)
    return jnp.sum(chosen, axis=0, keepdims=True) / jnp.sum(scores, axis=0, keepdims=True)


def down_product(hidden_ref, down_refs, out_ref, start):
    width = out_ref.shape[1]
    units = down_refs[0].shape[0]
    step = width // 2 if width % (4 * LANES) else 4 * LANES
    for low in range(0, width, step):
        columns = slice(start + low, start + low + step)
        out_ref[:, low : low + step] = sum(
            jnp.dot(
                hidden_ref[:, half * units : (half + 1) * units],
                down_ref[:, columns],
                preferred_element_type=jnp.float32,
            )
            for half, down_ref in enumerate(down_refs)
        ).astype(out_ref.dtype)


def fetch_kernel(*refs):
    count = (len(refs) - 1) // 2
    arrived = refs[-1]
    copies = [
        pltpu.make_async_copy(refs[i], refs[count + i], arrived.at[i]) for i in range(count)
    ]
    for copy in copies:
        copy.start()
    for copy in copies:
        copy.wait()


def fetched(arrays):
    return pl.pallas_call(
        fetch_kernel,
        compiler_params=pltpu.CompilerParams(vmem_limit_bytes=1 << 20),
        out_shape=tuple(near_shape(array.shape, array.dtype) for array in arrays),
        in_specs=[pl.BlockSpec(memory_space=pltpu.HBM)] * len(arrays),
        out_specs=(pl.BlockSpec(memory_space=pltpu.VMEM),) * len(arrays),
        scratch_shapes=[pltpu.SemaphoreType.DMA((len(arrays),))],
    )(*[far(array) for array in arrays])


def joined_kernel(own_ref, came_ref, *refs):
    out_ref = refs[len(refs) // 2]
    half = own_ref.shape[0]
    out_ref[:half, :] = own_ref[...]
    out_ref[half:, :] = came_ref[...]


def joined(own, came, passed=()):
    rows, width = own.shape
    whole = pl.BlockSpec(memory_space=pltpu.VMEM)
    out, *passed = pl.pallas_call(
        joined_kernel,
        compiler_params=pltpu.CompilerParams(vmem_limit_bytes=12 << 20),
        out_shape=(near_shape((2 * rows, width), own.dtype),)
        + tuple(near_shape(array.shape, array.dtype) for array in passed),
        in_specs=[whole] * (2 + len(passed)),
        out_specs=(whole,) * (1 + len(passed)),
        input_output_aliases={2 + i: 1 + i for i in range(len(passed))},
    )(near(own), near(came), *[near(array) for array in passed])
    return out, passed


def first_expert_kernel(
    device_ref,
    gain_ref,
    rows_a,
    rows_b,
    gate_a,
    up_a,
    down_a,
    gate_b,
    up_b,
    down_b,
    out_a,
    out_b,
    turned,
    hidden,
):
    units = gate_a.shape[0]
    share = normed_rows(device_ref, gain_ref, (rows_a, rows_b), turned)
    model_width = gain_ref.shape[1]
    rows = turned[:model_width, :]
    for half, (gate_ref, up_ref) in enumerate(((gate_a, up_a), (gate_b, up_b))):
        for low in range(0, units, UNITS):
            chunk = slice(low, low + UNITS)
            gate_part = jnp.dot(gate_ref[chunk, :], rows, preferred_element_type=jnp.float32)
            up_part = jnp.dot(up_ref[chunk, :], rows, preferred_element_type=jnp.float32)
            silu = gate_part / (1.0 + jnp.exp(-gate_part))
            hidden[:, half * units + low : half * units + low + UNITS] = (
                (silu * up_part * share).T.astype(jnp.bfloat16)
            )
    down_product(hidden, (down_a, down_b), out_a, 0)
    down_product(hidden, (down_a, down_b), out_b, out_a.shape[1])


def turned_half(rows_ref, gain_ref, start, width, turned):
    square = jnp.zeros((rows_ref.shape[0], LANES), jnp.float32)
    for low in range(0, width, LANES):
        residual = rows_ref[:, low : low + LANES].astype(jnp.float32)
        square = square + residual * residual
        gained = residual * gain_ref[:, start + low : start + low + LANES]
        turned[low : low + LANES, :] = gained.astype(jnp.bfloat16).T
    return jnp.sum(square.T, axis=0, keepdims=True)


def half_expert_kernel(
    device_ref,
    gain_ref,
    rows_ref,
    gate_a,
    gate_b,
    up_a,
    up_b,
    gates_ref,
    ups_ref,
    stats_ref,
    turned,
):
    width = turned.shape[0]
    stats_ref[0:1, :] = turned_half(rows_ref, gain_ref, 0, width, turned)
    scores = rows_ref[:, width:].astype(jnp.float32).T
    lane = lax.broadcasted_iota(jnp.int32, scores.shape, 0)
    chosen = jnp.where(lane == lax.div(device_ref[0], 2) + TABLE_LANE, scores, 0.0)
    stats_ref[1:2, :] = jnp.sum(chosen, axis=0, keepdims=True) / jnp.sum(
        scores, axis=0, keepdims=True
    )
    rows = turned[...]
    units = gate_a.shape[0]
    for weight_ref, low, out_ref in (
        (gate_a, 0, gates_ref),
        (gate_b, units, gates_ref),
        (up_a, 0, ups_ref),
        (up_b, units, ups_ref),
    ):
        out_ref[low : low + units, :] = jnp.dot(
            weight_ref[:, :width], rows, preferred_element_type=jnp.float32
        )


def second_expert_kernel(
    gain_ref,
    rows_ref,
    gates_ref,
    ups_ref,
    stats_ref,
    gate_a,
    gate_b,
    up_a,
    up_b,
    down_a,
    down_b,
    out_ref,
    hidden,
    turned,
):
    width = turned.shape[0]
    square = stats_ref[0:1, :] + turned_half(rows_ref, gain_ref, width, width, turned)
    inverse = lax.rsqrt(square / (2 * width) + 1e-06)
    share = stats_ref[1:2, :]
    rows = turned[...]
    units = gate_a.shape[0]
    for half, (gate_ref, up_ref) in enumerate(((gate_a, up_a), (gate_b, up_b))):
        for low in range(0, units, UNITS):
            chunk = slice(low, low + UNITS)
            at = slice(half * units + low, half * units + low + UNITS)
            gate_part = inverse * (
                gates_ref[at, :]
                + jnp.dot(gate_ref[chunk, width:], rows, preferred_element_type=jnp.float32)
            )
            up_part = inverse * (
                ups_ref[at, :]
                + jnp.dot(up_ref[chunk, width:], rows, preferred_element_type=jnp.float32)
            )
            silu = gate_part / (1.0 + jnp.exp(-gate_part))
            hidden[:, at] = (silu * up_part * share).T.astype(jnp.bfloat16)
    down_product(hidden, (down_a, down_b), out_ref, 0)


def rest_expert_kernel(
    start, hidden_ref, down_a, down_b, first_ref, sent_ref, kept_ref, value_ref
):
    down_product(hidden_ref, (down_a, down_b), value_ref, start)
    half = first_ref.shape[0] // 2
    sent_ref[:half, :] = first_ref[half:, :].astype(sent_ref.dtype)
    sent_ref[half:, :] = value_ref[half:, :].astype(sent_ref.dtype)
    kept_ref[:half, :] = first_ref[:half, :]
    kept_ref[half:, :] = value_ref[:half, :]


def first_expert_rows(device, gain, halves, weights):
    units, model_width = weights[0].shape
    row_count = halves[0].shape[0]
    whole = pl.BlockSpec(memory_space=pltpu.VMEM)
    return pl.pallas_call(
        first_expert_kernel,
        name="expert_first",
        compiler_params=pltpu.CompilerParams(vmem_limit_bytes=12 << 20),
        out_shape=(near_shape((row_count, model_width // 2), jnp.float32),) * 2,
        in_specs=[pl.BlockSpec(memory_space=pltpu.SMEM)] + [whole] * 9,
        out_specs=(whole,) * 2,
        scratch_shapes=[
            pltpu.VMEM((model_width + LANES, row_count), jnp.bfloat16),
            pltpu.VMEM((row_count, 2 * units), jnp.bfloat16),
        ],
        cost_estimate=pl.CostEstimate(
            flops=12 * row_count * model_width * units,
            transcendentals=0,
            bytes_accessed=12 * units * model_width,
        ),
    )(
        device,
        near(gain),
        *[near(part) for part in (*halves, *weights)],
    )


def second_expert_rows(device, gain, halves, gates, ups, downs, totals):
    units, model_width = gates[0].shape
    units = 2 * units
    row_count = halves[0].shape[0]
    width = model_width // 2
    whole = pl.BlockSpec(memory_space=pltpu.VMEM)
    gates, ups, downs = [[near(half) for half in pair] for pair in (gates, ups, downs)]
    gate_parts, up_parts, stats = pl.pallas_call(
        half_expert_kernel,
        name="expert_half",
        compiler_params=pltpu.CompilerParams(vmem_limit_bytes=12 << 20),
        out_shape=(near_shape((units, row_count), jnp.float32),) * 2
        + (near_shape((8, row_count), jnp.float32),),
        in_specs=[pl.BlockSpec(memory_space=pltpu.SMEM)] + [whole] * 6,
        out_specs=(whole,) * 3,
        scratch_shapes=[pltpu.VMEM((width, row_count), jnp.bfloat16)],
    )(device, near(gain), near(halves[0]), *gates, *ups)
    first, hidden = pl.pallas_call(
        second_expert_kernel,
        name="expert_second",
        compiler_params=pltpu.CompilerParams(vmem_limit_bytes=12 << 20),
        out_shape=(
            near_shape((row_count, width), jnp.bfloat16),
            near_shape((row_count, units), jnp.bfloat16),
        ),
        in_specs=[whole] * 11,
        out_specs=(whole, whole),
        scratch_shapes=[pltpu.VMEM((width, row_count), jnp.bfloat16)],
    )(
        near(gain),
        near(halves[1]),
        near(gate_parts),
        near(up_parts),
        near(stats),
        *gates,
        *ups,
        *downs,
    )
    sent, kept = pl.pallas_call(
        functools.partial(rest_expert_kernel, width),
        name="expert_rest",
        compiler_params=pltpu.CompilerParams(vmem_limit_bytes=12 << 20),
        out_shape=(
            near_shape((row_count, width), jnp.bfloat16),
            near_shape((row_count, width), jnp.float32),
        ),
        in_specs=[whole] * 4,
        out_specs=(whole, whole),
        scratch_shapes=[pltpu.VMEM((row_count, width), jnp.float32)],
    )(near(hidden), *downs, near(totals[1]))
    return [(first, totals[0]), (sent, kept)]


def attention_rows(
    queries, patch_keys, patch_values, other_keys, other_values, gain, table, row_count, orders
):
    model_width = patch_values.shape[1]
    part_width = model_width // PARTS + LANES
    part_heads = HEADS // PARTS
    stages = len(orders[0])
    device_index = lax.axis_index("wide")
    masks = [
        [
            sum(
                (1 << order[stage])
                for stage in range(stages)
                if slot >> (stages - 1 - stage) & 1
            )
            for slot in range(1 << stages)
        ]
        for order in orders
    ]
    rows = row_count << stages
    whole = pl.BlockSpec(memory_space=pltpu.VMEM)

    def pair_shapes(rows):
        return (
            near_shape((rows, part_width), jnp.bfloat16),
            near_shape((rows, part_width), jnp.float32),
        )

    anywhere = pl.BlockSpec(memory_space=pltpu.HBM)
    query_rows, own_keys, own_values, gain = pl.pallas_call(
        functools.partial(stage_kernel, row_count, masks),
        name="stage_in",
        compiler_params=pltpu.CompilerParams(vmem_limit_bytes=4 << 20),
        out_shape=(
            near_shape((rows, queries.shape[1]), jnp.bfloat16),
            near_shape(patch_keys.shape, jnp.bfloat16),
            near_shape(patch_values.shape, jnp.bfloat16),
            near_shape(gain.shape, jnp.float32),
        ),
        in_specs=[pl.BlockSpec(memory_space=pltpu.SMEM)] + [anywhere] * 4,
        out_specs=(whole,) * 4,
        scratch_shapes=[pltpu.SemaphoreType.DMA((3 + (1 << stages),))],
    )(device_index.reshape(1), far(queries), far(patch_keys), far(patch_values), far(gain))
    operands = (query_rows, own_keys, other_keys, own_values, other_values)
    chains = []
    for part in range(PARTS):
        chains += pl.pallas_call(
            functools.partial(attend_kernel, HEADS, part, part_heads),
            compiler_params=pltpu.CompilerParams(vmem_limit_bytes=8 << 20),
            out_shape=pair_shapes(rows // 2),
            in_specs=[whole] * 5,
            out_specs=(whole, whole),
        )(*[near(operand) for operand in operands])
    finished = []
    for part in range(PARTS):
        sent, kept = chains[2 * part : 2 * part + 2]
        for stage in range(stages - 1):
            came = exchange(sent, orders, stage)
            rows = kept.shape[0]
            last = stage == stages - 2
            operands = [near(kept), near(came)]
            if last and part == 0:
                operands.append(near(table))
            sent, kept = pl.pallas_call(
                functools.partial(last_merge_kernel if last else merge_kernel, part_heads),
                compiler_params=pltpu.CompilerParams(vmem_limit_bytes=6 << 20),
                out_shape=pair_shapes(rows if last else rows // 2),
                in_specs=[whole] * len(operands),
                out_specs=(whole, whole),
            )(*operands)
        came = exchange(sent, orders, stages - 1)
        rows = kept.shape[0]
        width = model_width // PARTS
        operands = [near(kept), near(came)] + ([near(table)] if part == 0 else [])
        block, projected = pl.pallas_call(
            functools.partial(finish_kernel, part_heads),
            compiler_params=pltpu.CompilerParams(vmem_limit_bytes=6 << 20),
            out_shape=(
                near_shape((rows, width + (LANES if part == 0 else 0)), jnp.bfloat16),
                near_shape((row_count, width), jnp.bfloat16),
            ),
            in_specs=[whole] * len(operands),
            out_specs=(whole, whole),
        )(*operands)
        finished.append((block, projected))
    return finished, gain


def on_device(
    queries, patch_keys, patch_values, norm_gain, route_experts, route_weights, w_gate, w_up, w_down
):
    row_count = route_experts.shape[0]
    model_width = patch_values.shape[1]
    devices = lax.axis_size("wide")
    device_index = lax.axis_index("wide")
    score_table = jnp.sum(
        jnp.where(
            route_experts[:, :, None] == jnp.arange(-TABLE_LANE, LANES - TABLE_LANE, dtype=jnp.int32),
            route_weights[:, :, None],
            0,
        ),
        axis=1,
    ).astype(jnp.bfloat16)
    merge_order, gather_order, scatter_order = plan_orders(
        devices, queries.shape[0] // row_count
    )
    other_keys = partner(patch_keys, "wide", 0)
    other_values = partner(patch_values, "wide", 0)
    halves, other_keys, other_values = lax.optimization_barrier(
        ((w_gate, w_up, w_down), other_keys, other_values)
    )
    weights = []
    for own in halves:
        weights += [own, partner(own, "wide", 0)]
    gain = norm_gain.reshape(1, model_width)
    finished, gain = attention_rows(
        queries,
        patch_keys,
        patch_values,
        other_keys,
        other_values,
        gain,
        score_table,
        row_count,
        merge_order,
    )
    blocks = [block for block, _ in finished]
    stages = len(gather_order[0])
    own_weights = fetched(weights[::2])
    arrived = {}
    for stage in range(stages):
        for part in range(PARTS):
            arrived[part] = exchange(blocks[part], gather_order, stage)
            if stage < stages - 1:
                last = stage == stages - 2
                blocks[part], passed = joined(
                    blocks[part], arrived[part], own_weights if last else ()
                )
                own_weights = passed if last else own_weights
    came = [arrived[part] for part in range(PARTS)]
    device = device_index.reshape(1)
    gate_a, up_a, down_a = own_weights
    gate_b, up_b, down_b = weights[1::2]
    totals = first_expert_rows(
        device, gain, blocks, (*own_weights, gate_b, up_b, down_b)
    )
    gates = (gate_a, gate_b)
    outputs = []
    for part, (sent, kept) in enumerate(
        second_expert_rows(
            device, gain, came, gates, (up_a, up_b), (down_a, down_b), totals
        )
    ):
        for stage in range(stages + 1):
            arrived = exchange(sent, scatter_order[part], stage)
            kept = kept + arrived.astype(jnp.float32)
            half_rows = kept.shape[0] // 2
            if stage < stages:
                sent = kept[half_rows:].astype(jnp.bfloat16)
                kept = kept[:half_rows]
        outputs.append((finished[part][1].astype(jnp.float32) + kept).astype(jnp.bfloat16))
    return jnp.concatenate(outputs, axis=1)


def solution(mesh):
    return mapped(mesh)


def mapped(mesh):
    return jax.shard_map(
        on_device,
        mesh=mesh,
        in_specs=(
            P("groups", None),
            P(("groups", "wide"), None),
            P(("groups", "wide"), None),
            P(),
            P(("groups", "wide"), None),
            P(("groups", "wide"), None),
            P("wide", None),
            P("wide", None),
            P("wide", None),
        ),
        out_specs=P(("groups", "wide"), None),
        check_vma=False,
    )
```

```python
import functools

import jax
import jax.numpy as jnp
from jax import lax
from jax.experimental import pallas as pl
from jax.experimental.pallas import tpu as pltpu
from jax.sharding import PartitionSpec as P


HEADS = 16
LANES = 128
TABLE_LANE = 64
UNITS = 256
PARTS = 2


def near(value):
    return pltpu.with_memory_space_constraint(value, pltpu.VMEM)


def far(value):
    return pltpu.with_memory_space_constraint(value, pltpu.HBM)


def near_shape(shape, dtype):
    return pltpu.VMEM(shape, dtype)


def partner(value, axis, stride):
    mask = 2**stride
    pairs = [(source, source ^ mask) for source in range(lax.axis_size(axis))]
    return lax.ppermute(value, axis, pairs)


def plan_orders(devices, group_size):
    near_bits = list(range(1, group_size.bit_length() - 1))
    all_bits = list(range(1, devices.bit_length() - 1))
    merge = (near_bits, near_bits[1:] + near_bits[:1])
    rest = [[bit for bit in all_bits if bit != order[-1]] for order in merge]
    gather = (rest[0][::-1], rest[1][2:][::-1] + rest[1][:2])
    scatter = [order[::-1] + kept[-1:] for order, kept in zip(gather, merge)]
    crossed = [order[1::-1] + order[2:] for order in scatter]
    return merge, gather, (scatter, crossed)


def exchange(value, orders, stage):
    pairs = [
        (source, source ^ (1 << orders[source % 2][stage]))
        for source in range(lax.axis_size("wide"))
    ]
    return lax.ppermute(value, "wide", pairs)


def lane_iota(shape):
    return lax.broadcasted_iota(jnp.int32, shape, 1)


def expand_tile(columns, tile, value_size):
    first = tile * LANES // value_size
    last = (tile * LANES + LANES - 1) // value_size
    rows = columns[0].shape[0]
    out = jnp.broadcast_to(columns[first], (rows, LANES))
    for head in range(first + 1, last + 1):
        edge = head * value_size - tile * LANES
        out = jnp.where(lane_iota((rows, LANES)) < edge, out, columns[head])
    return out


def pack_stats(peak, total, head_count):
    lane = lane_iota(peak.shape)
    high = total.astype(jnp.bfloat16).astype(jnp.float32)
    low = total - high
    packed = jnp.where(lane < head_count, peak, 0.0)
    shifted = pltpu.roll(jnp.where(lane < head_count, high, 0.0), head_count, 1)
    shifted_low = pltpu.roll(jnp.where(lane < head_count, low, 0.0), 2 * head_count, 1)
    return packed + shifted + shifted_low


def total_of(stats, head_count):
    return pltpu.roll(stats, LANES - head_count, 1) + pltpu.roll(
        stats, LANES - 2 * head_count, 1
    )


def head_windows(head, size):
    return head * size // LANES, -(-(head + 1) * size // LANES)


def head_scores(head, head_count, query_ref, keys_ref):
    key_size = query_ref.shape[1] // head_count
    low, high = [LANES * tile for tile in head_windows(head, key_size)]
    window = lane_iota((query_ref.shape[0], high - low)) + low
    inside = (window >= head * key_size) & (window < (head + 1) * key_size)
    query = jnp.where(inside, query_ref[:, low:high], jnp.zeros((), jnp.bfloat16))
    return key_size ** (-0.5) * lax.dot_general(
        query,
        keys_ref[:, low:high],
        (((1,), (1,)), ((), ())),
        preferred_element_type=jnp.float32,
    )


def rounded_peak(scores):
    peak = jnp.max(scores, axis=1, keepdims=True)
    return peak.astype(jnp.bfloat16).astype(jnp.float32)


def head_sums(head, value_size, raised, values_ref):
    low, high = head_windows(head, value_size)
    return jnp.dot(
        raised.astype(jnp.bfloat16),
        values_ref[:, low * LANES : high * LANES],
        preferred_element_type=jnp.float32,
    )


def stage_kernel(
    row_count,
    masks,
    device_ref,
    queries_ref,
    keys_ref,
    values_ref,
    query_ref,
    near_keys_ref,
    near_values_ref,
    arrived,
):
    group_size = queries_ref.shape[0] // row_count
    device = device_ref[0]
    odd = lax.rem(device, 2) == 1
    own_block = lax.rem(device, group_size)
    copies = [
        pltpu.make_async_copy(keys_ref, near_keys_ref, arrived.at[0]),
        pltpu.make_async_copy(values_ref, near_values_ref, arrived.at[1]),
    ]
    for slot, (even_mask, odd_mask) in enumerate(zip(*masks)):
        block = own_block ^ jnp.where(odd, odd_mask, even_mask)
        start = pl.multiple_of(block * row_count, row_count)
        copies.append(
            pltpu.make_async_copy(
                queries_ref.at[pl.ds(start, row_count), :],
                query_ref.at[slot * row_count : (slot + 1) * row_count, :],
                arrived.at[2 + slot],
            )
        )
    for copy in copies:
        copy.start()
    for copy in copies:
        copy.wait()


def attend_kernel(
    head_count, part, part_heads, query_ref, keys_a, keys_b, values_a, values_b, sent_ref, kept_ref
):
    rows = query_ref.shape[0]
    half = rows // 2
    value_size = values_a.shape[1] // head_count
    part_tiles = part_heads * value_size // LANES
    base = part * part_tiles
    lane = lane_iota((rows, LANES))
    peaks = jnp.zeros((rows, LANES), jnp.float32)
    totals = jnp.zeros((rows, LANES), jnp.float32)

    def put(tile, value):
        columns = slice(tile * LANES, (tile + 1) * LANES)
        kept_ref[:, columns] = value[:half]
        sent_ref[:, columns] = value[half:].astype(jnp.bfloat16)

    for at in range(part_heads):
        head = part * part_heads + at
        scores_a = head_scores(head, head_count, query_ref, keys_a)
        scores_b = head_scores(head, head_count, query_ref, keys_b)
        peak = jnp.maximum(rounded_peak(scores_a), rounded_peak(scores_b))
        raised_a = jnp.exp(scores_a - peak)
        raised_b = jnp.exp(scores_b - peak)
        total = jnp.sum(raised_a + raised_b, axis=1, keepdims=True)
        peaks = jnp.where(lane == at, peak, peaks)
        totals = jnp.where(lane == at, total, totals)
        summed = head_sums(head, value_size, raised_a, values_a) + head_sums(
            head, value_size, raised_b, values_b
        )
        low, high = head_windows(head, value_size)
        for tile in range(low, high):
            value = summed[:, (tile - low) * LANES : (tile - low + 1) * LANES]
            edge = head * value_size - tile * LANES
            if edge > 0:
                value = jnp.where(lane < edge, waiting, value)
            waiting = value
            if (tile + 1) * LANES <= (head + 1) * value_size:
                put(tile - base, value)
    put(part_tiles, pack_stats(peaks, totals, part_heads))


def merged_parts(kept_ref, came_ref, head_count, model_width):
    stats_a = kept_ref[:, model_width:]
    stats_b = came_ref[:, model_width:].astype(jnp.float32)
    peak = jnp.maximum(stats_a, stats_b)
    factor_a = jnp.exp(stats_a - peak)
    factor_b = jnp.exp(stats_b - peak)
    total = total_of(stats_a, head_count) * factor_a + total_of(stats_b, head_count) * factor_b
    return peak, total, factor_a, factor_b


def head_columns(array, head_count):
    return [array[:, head : head + 1] for head in range(head_count)]


def merge_kernel(head_count, kept_ref, came_ref, sent_ref, next_ref):
    model_width = kept_ref.shape[1] - LANES
    half = kept_ref.shape[0] // 2
    peak, total, factor_a, factor_b = merged_parts(kept_ref, came_ref, head_count, model_width)
    columns_a = head_columns(factor_a, head_count)
    columns_b = head_columns(factor_b, head_count)
    for tile in range(model_width // LANES + 1):
        columns = slice(tile * LANES, (tile + 1) * LANES)
        if tile * LANES == model_width:
            value = pack_stats(peak, total, head_count)
        else:
            value = kept_ref[:, columns] * expand_tile(
                columns_a, tile, model_width // head_count
            ) + came_ref[:, columns].astype(jnp.float32) * expand_tile(
                columns_b, tile, model_width // head_count
            )
        next_ref[:, columns] = value[:half]
        sent_ref[:, columns] = value[half:].astype(jnp.bfloat16)


def last_merge_kernel(head_count, kept_ref, came_ref, *rest):
    tables, (sent_ref, next_ref) = rest[:-2], rest[-2:]
    model_width = kept_ref.shape[1] - LANES
    half = kept_ref.shape[0] // 2
    peak, total, factor_a, factor_b = merged_parts(kept_ref, came_ref, head_count, model_width)
    columns_a = head_columns(factor_a, head_count)
    columns_b = head_columns(factor_b, head_count)
    for tile in range(model_width // LANES + 1):
        columns = slice(tile * LANES, (tile + 1) * LANES)
        if tile * LANES == model_width:
            value = pack_stats(peak, total, head_count)
            own = value[:half]
            for table_ref in tables:
                own = own + table_ref[...].astype(jnp.float32)
        else:
            value = kept_ref[:, columns] * expand_tile(
                columns_a, tile, model_width // head_count
            ) + came_ref[:, columns].astype(jnp.float32) * expand_tile(
                columns_b, tile, model_width // head_count
            )
            own = value[:half]
        next_ref[:, columns] = value
        sent_ref[:half, columns] = value[half:].astype(jnp.bfloat16)
        sent_ref[half:, columns] = own.astype(jnp.bfloat16)


def finish_kernel(part_heads, kept_ref, came_ref, *rest):
    tables, (block_ref, projected_ref) = rest[:-2], rest[-2:]
    half = kept_ref.shape[0] // 2
    width = kept_ref.shape[1] - LANES
    _, total, factor_a, factor_b = merged_parts(kept_ref, came_ref, part_heads, width)
    columns_a = head_columns(factor_a / total, part_heads)
    columns_b = head_columns(factor_b / total, part_heads)
    for tile in range(width // LANES):
        columns = slice(tile * LANES, (tile + 1) * LANES)
        value = kept_ref[:, columns] * expand_tile(
            columns_a, tile, width // part_heads
        ) + came_ref[:, columns].astype(jnp.float32) * expand_tile(
            columns_b, tile, width // part_heads
        )
        rounded = value.astype(jnp.bfloat16)
        block_ref[:, columns] = rounded
        projected_ref[:, columns] = rounded[:half]
    for table_ref in tables:
        came_table = came_ref[half:, width:]
        lane = lane_iota(came_table.shape)
        block_ref[:half, width:] = table_ref[...]
        block_ref[half:, width:] = jnp.where(
            lane >= TABLE_LANE, came_table.astype(jnp.float32), 0.0
        ).astype(jnp.bfloat16)


def normed_rows(device_ref, gain_ref, row_refs, turned):
    width = row_refs[1].shape[1]
    model_width = width * len(row_refs)
    square = jnp.zeros((row_refs[0].shape[0], LANES), jnp.float32)
    for rows_ref in row_refs:
        for low in range(0, width, LANES):
            residual = rows_ref[:, low : low + LANES].astype(jnp.float32)
            square = square + residual * residual
    mean = jnp.sum(square, axis=1, keepdims=True) / model_width
    inverse = jnp.broadcast_to(lax.rsqrt(mean + 1e-06), square.shape)
    for part, rows_ref in enumerate(row_refs):
        for low in range(0, width, LANES):
            at = part * width + low
            residual = rows_ref[:, low : low + LANES].astype(jnp.float32)
            normed = residual * inverse * gain_ref[:, at : at + LANES]
            turned[at : at + LANES, :] = normed.astype(jnp.bfloat16).T
    turned[model_width:, :] = row_refs[0][:, width:].T
    scores = turned[model_width:, :].astype(jnp.float32)
    lane = lax.broadcasted_iota(jnp.int32, scores.shape, 0)
    chosen = jnp.where(lane == lax.div(device_ref[0], 2) + TABLE_LANE, scores, 0.0)
    return jnp.sum(chosen, axis=0, keepdims=True) / jnp.sum(scores, axis=0, keepdims=True)


def down_product(hidden_ref, down_refs, out_ref, start):
    width = out_ref.shape[1]
    units = down_refs[0].shape[0]
    step = width // 2 if width % (4 * LANES) else 4 * LANES
    for low in range(0, width, step):
        columns = slice(start + low, start + low + step)
        out_ref[:, low : low + step] = sum(
            jnp.dot(
                hidden_ref[:, half * units : (half + 1) * units],
                down_ref[:, columns],
                preferred_element_type=jnp.float32,
            )
            for half, down_ref in enumerate(down_refs)
        ).astype(out_ref.dtype)


def fetch_kernel(*refs):
    count = (len(refs) - 1) // 2
    arrived = refs[-1]
    copies = [
        pltpu.make_async_copy(refs[i], refs[count + i], arrived.at[i]) for i in range(count)
    ]
    for copy in copies:
        copy.start()
    for copy in copies:
        copy.wait()


def fetched(arrays):
    return pl.pallas_call(
        fetch_kernel,
        compiler_params=pltpu.CompilerParams(vmem_limit_bytes=1 << 20),
        out_shape=tuple(near_shape(array.shape, array.dtype) for array in arrays),
        in_specs=[pl.BlockSpec(memory_space=pltpu.HBM)] * len(arrays),
        out_specs=(pl.BlockSpec(memory_space=pltpu.VMEM),) * len(arrays),
        scratch_shapes=[pltpu.SemaphoreType.DMA((len(arrays),))],
    )(*[far(array) for array in arrays])


def joined_kernel(own_ref, came_ref, *refs):
    out_ref = refs[len(refs) // 2]
    half = own_ref.shape[0]
    out_ref[:half, :] = own_ref[...]
    out_ref[half:, :] = came_ref[...]


def joined(own, came, passed=()):
    rows, width = own.shape
    whole = pl.BlockSpec(memory_space=pltpu.VMEM)
    out, *passed = pl.pallas_call(
        joined_kernel,
        compiler_params=pltpu.CompilerParams(vmem_limit_bytes=12 << 20),
        out_shape=(near_shape((2 * rows, width), own.dtype),)
        + tuple(near_shape(array.shape, array.dtype) for array in passed),
        in_specs=[whole] * (2 + len(passed)),
        out_specs=(whole,) * (1 + len(passed)),
        input_output_aliases={2 + i: 1 + i for i in range(len(passed))},
    )(near(own), near(came), *[near(array) for array in passed])
    return out, passed


def first_expert_kernel(
    device_ref,
    gain_ref,
    rows_a,
    rows_b,
    gate_a,
    up_a,
    down_a,
    gate_b,
    up_b,
    down_b,
    out_a,
    out_b,
    turned,
    hidden,
):
    units = gate_a.shape[0]
    share = normed_rows(device_ref, gain_ref, (rows_a, rows_b), turned)
    model_width = gain_ref.shape[1]
    rows = turned[:model_width, :]
    for half, (gate_ref, up_ref) in enumerate(((gate_a, up_a), (gate_b, up_b))):
        for low in range(0, units, UNITS):
            chunk = slice(low, low + UNITS)
            gate_part = jnp.dot(gate_ref[chunk, :], rows, preferred_element_type=jnp.float32)
            up_part = jnp.dot(up_ref[chunk, :], rows, preferred_element_type=jnp.float32)
            silu = gate_part / (1.0 + jnp.exp(-gate_part))
            hidden[:, half * units + low : half * units + low + UNITS] = (
                (silu * up_part * share).T.astype(jnp.bfloat16)
            )
    down_product(hidden, (down_a, down_b), out_a, 0)
    down_product(hidden, (down_a, down_b), out_b, out_a.shape[1])


def turned_half(rows_ref, gain_ref, start, width, turned):
    square = jnp.zeros((rows_ref.shape[0], LANES), jnp.float32)
    for low in range(0, width, LANES):
        residual = rows_ref[:, low : low + LANES].astype(jnp.float32)
        square = square + residual * residual
        gained = residual * gain_ref[:, start + low : start + low + LANES]
        turned[low : low + LANES, :] = gained.astype(jnp.bfloat16).T
    return jnp.sum(square.T, axis=0, keepdims=True)


def half_expert_kernel(
    device_ref,
    gain_ref,
    rows_ref,
    gate_a,
    gate_b,
    up_a,
    up_b,
    gates_ref,
    ups_ref,
    stats_ref,
    turned,
):
    width = turned.shape[0]
    stats_ref[0:1, :] = turned_half(rows_ref, gain_ref, 0, width, turned)
    scores = rows_ref[:, width:].astype(jnp.float32).T
    lane = lax.broadcasted_iota(jnp.int32, scores.shape, 0)
    chosen = jnp.where(lane == lax.div(device_ref[0], 2) + TABLE_LANE, scores, 0.0)
    stats_ref[1:2, :] = jnp.sum(chosen, axis=0, keepdims=True) / jnp.sum(
        scores, axis=0, keepdims=True
    )
    rows = turned[...]
    units = gate_a.shape[0]
    for weight_ref, low, out_ref in (
        (gate_a, 0, gates_ref),
        (gate_b, units, gates_ref),
        (up_a, 0, ups_ref),
        (up_b, units, ups_ref),
    ):
        out_ref[low : low + units, :] = jnp.dot(
            weight_ref[:, :width], rows, preferred_element_type=jnp.float32
        )


def second_expert_kernel(
    gain_ref,
    rows_ref,
    gates_ref,
    ups_ref,
    stats_ref,
    gate_a,
    gate_b,
    up_a,
    up_b,
    down_a,
    down_b,
    out_ref,
    hidden,
    turned,
):
    width = turned.shape[0]
    square = stats_ref[0:1, :] + turned_half(rows_ref, gain_ref, width, width, turned)
    inverse = lax.rsqrt(square / (2 * width) + 1e-06)
    share = stats_ref[1:2, :]
    rows = turned[...]
    units = gate_a.shape[0]
    for half, (gate_ref, up_ref) in enumerate(((gate_a, up_a), (gate_b, up_b))):
        for low in range(0, units, UNITS):
            chunk = slice(low, low + UNITS)
            at = slice(half * units + low, half * units + low + UNITS)
            gate_part = inverse * (
                gates_ref[at, :]
                + jnp.dot(gate_ref[chunk, width:], rows, preferred_element_type=jnp.float32)
            )
            up_part = inverse * (
                ups_ref[at, :]
                + jnp.dot(up_ref[chunk, width:], rows, preferred_element_type=jnp.float32)
            )
            silu = gate_part / (1.0 + jnp.exp(-gate_part))
            hidden[:, at] = (silu * up_part * share).T.astype(jnp.bfloat16)
    down_product(hidden, (down_a, down_b), out_ref, 0)


def rest_expert_kernel(
    start, hidden_ref, down_a, down_b, first_ref, sent_ref, kept_ref, value_ref
):
    down_product(hidden_ref, (down_a, down_b), value_ref, start)
    half = first_ref.shape[0] // 2
    sent_ref[:half, :] = first_ref[half:, :].astype(sent_ref.dtype)
    sent_ref[half:, :] = value_ref[half:, :].astype(sent_ref.dtype)
    kept_ref[:half, :] = first_ref[:half, :]
    kept_ref[half:, :] = value_ref[:half, :]


def first_expert_rows(device, gain, halves, weights):
    units, model_width = weights[0].shape
    row_count = halves[0].shape[0]
    whole = pl.BlockSpec(memory_space=pltpu.VMEM)
    return pl.pallas_call(
        first_expert_kernel,
        name="expert_first",
        compiler_params=pltpu.CompilerParams(vmem_limit_bytes=12 << 20),
        out_shape=(near_shape((row_count, model_width // 2), jnp.float32),) * 2,
        in_specs=[pl.BlockSpec(memory_space=pltpu.SMEM)] + [whole] * 9,
        out_specs=(whole,) * 2,
        scratch_shapes=[
            pltpu.VMEM((model_width + LANES, row_count), jnp.bfloat16),
            pltpu.VMEM((row_count, 2 * units), jnp.bfloat16),
        ],
        cost_estimate=pl.CostEstimate(
            flops=12 * row_count * model_width * units,
            transcendentals=0,
            bytes_accessed=12 * units * model_width,
        ),
    )(
        device,
        near(gain),
        *[near(part) for part in (*halves, *weights)],
    )


def second_expert_rows(device, gain, halves, gates, ups, downs, totals):
    units, model_width = gates[0].shape
    units = 2 * units
    row_count = halves[0].shape[0]
    width = model_width // 2
    whole = pl.BlockSpec(memory_space=pltpu.VMEM)
    gates, ups, downs = [[near(half) for half in pair] for pair in (gates, ups, downs)]
    gate_parts, up_parts, stats = pl.pallas_call(
        half_expert_kernel,
        name="expert_half",
        compiler_params=pltpu.CompilerParams(vmem_limit_bytes=12 << 20),
        out_shape=(near_shape((units, row_count), jnp.float32),) * 2
        + (near_shape((8, row_count), jnp.float32),),
        in_specs=[pl.BlockSpec(memory_space=pltpu.SMEM)] + [whole] * 6,
        out_specs=(whole,) * 3,
        scratch_shapes=[pltpu.VMEM((width, row_count), jnp.bfloat16)],
    )(device, near(gain), near(halves[0]), *gates, *ups)
    first, hidden = pl.pallas_call(
        second_expert_kernel,
        name="expert_second",
        compiler_params=pltpu.CompilerParams(vmem_limit_bytes=12 << 20),
        out_shape=(
            near_shape((row_count, width), jnp.bfloat16),
            near_shape((row_count, units), jnp.bfloat16),
        ),
        in_specs=[whole] * 11,
        out_specs=(whole, whole),
        scratch_shapes=[pltpu.VMEM((width, row_count), jnp.bfloat16)],
    )(
        near(gain),
        near(halves[1]),
        near(gate_parts),
        near(up_parts),
        near(stats),
        *gates,
        *ups,
        *downs,
    )
    sent, kept = pl.pallas_call(
        functools.partial(rest_expert_kernel, width),
        name="expert_rest",
        compiler_params=pltpu.CompilerParams(vmem_limit_bytes=12 << 20),
        out_shape=(
            near_shape((row_count, width), jnp.bfloat16),
            near_shape((row_count, width), jnp.float32),
        ),
        in_specs=[whole] * 4,
        out_specs=(whole, whole),
        scratch_shapes=[pltpu.VMEM((row_count, width), jnp.float32)],
    )(near(hidden), *downs, near(totals[1]))
    return [(first, totals[0]), (sent, kept)]


def attention_rows(
    queries, patch_keys, patch_values, other_keys, other_values, table, row_count, orders
):
    model_width = patch_values.shape[1]
    part_width = model_width // PARTS + LANES
    part_heads = HEADS // PARTS
    stages = len(orders[0])
    device_index = lax.axis_index("wide")
    masks = [
        [
            sum(
                (1 << order[stage])
                for stage in range(stages)
                if slot >> (stages - 1 - stage) & 1
            )
            for slot in range(1 << stages)
        ]
        for order in orders
    ]
    rows = row_count << stages
    whole = pl.BlockSpec(memory_space=pltpu.VMEM)

    def pair_shapes(rows):
        return (
            near_shape((rows, part_width), jnp.bfloat16),
            near_shape((rows, part_width), jnp.float32),
        )

    anywhere = pl.BlockSpec(memory_space=pltpu.HBM)
    query_rows, own_keys, own_values = pl.pallas_call(
        functools.partial(stage_kernel, row_count, masks),
        name="stage_in",
        compiler_params=pltpu.CompilerParams(vmem_limit_bytes=4 << 20),
        out_shape=(
            near_shape((rows, queries.shape[1]), jnp.bfloat16),
            near_shape(patch_keys.shape, jnp.bfloat16),
            near_shape(patch_values.shape, jnp.bfloat16),
        ),
        in_specs=[pl.BlockSpec(memory_space=pltpu.SMEM)] + [anywhere] * 3,
        out_specs=(whole,) * 3,
        scratch_shapes=[pltpu.SemaphoreType.DMA((2 + (1 << stages),))],
    )(device_index.reshape(1), far(queries), far(patch_keys), far(patch_values))
    operands = (query_rows, own_keys, other_keys, own_values, other_values)
    chains = []
    for part in range(PARTS):
        chains += pl.pallas_call(
            functools.partial(attend_kernel, HEADS, part, part_heads),
            compiler_params=pltpu.CompilerParams(vmem_limit_bytes=8 << 20),
            out_shape=pair_shapes(rows // 2),
            in_specs=[whole] * 5,
            out_specs=(whole, whole),
        )(*[near(operand) for operand in operands])
    finished = []
    for part in range(PARTS):
        sent, kept = chains[2 * part : 2 * part + 2]
        for stage in range(stages - 1):
            came = exchange(sent, orders, stage)
            rows = kept.shape[0]
            last = stage == stages - 2
            operands = [near(kept), near(came)]
            if last and part == 0:
                operands.append(near(table))
            sent, kept = pl.pallas_call(
                functools.partial(last_merge_kernel if last else merge_kernel, part_heads),
                compiler_params=pltpu.CompilerParams(vmem_limit_bytes=6 << 20),
                out_shape=pair_shapes(rows if last else rows // 2),
                in_specs=[whole] * len(operands),
                out_specs=(whole, whole),
            )(*operands)
        came = exchange(sent, orders, stages - 1)
        rows = kept.shape[0]
        width = model_width // PARTS
        operands = [near(kept), near(came)] + ([near(table)] if part == 0 else [])
        block, projected = pl.pallas_call(
            functools.partial(finish_kernel, part_heads),
            compiler_params=pltpu.CompilerParams(vmem_limit_bytes=6 << 20),
            out_shape=(
                near_shape((rows, width + (LANES if part == 0 else 0)), jnp.bfloat16),
                near_shape((row_count, width), jnp.bfloat16),
            ),
            in_specs=[whole] * len(operands),
            out_specs=(whole, whole),
        )(*operands)
        finished.append((block, projected))
    return finished


def on_device(
    queries, patch_keys, patch_values, norm_gain, route_experts, route_weights, w_gate, w_up, w_down
):
    row_count = route_experts.shape[0]
    model_width = patch_values.shape[1]
    devices = lax.axis_size("wide")
    device_index = lax.axis_index("wide")
    score_table = jnp.sum(
        jnp.where(
            route_experts[:, :, None] == jnp.arange(-TABLE_LANE, LANES - TABLE_LANE, dtype=jnp.int32),
            route_weights[:, :, None],
            0,
        ),
        axis=1,
    ).astype(jnp.bfloat16)
    merge_order, gather_order, scatter_order = plan_orders(
        devices, queries.shape[0] // row_count
    )
    other_keys = partner(patch_keys, "wide", 0)
    other_values = partner(patch_values, "wide", 0)
    halves, other_keys, other_values = lax.optimization_barrier(
        ((w_gate, w_up, w_down), other_keys, other_values)
    )
    weights = []
    for own in halves:
        weights += [own, partner(own, "wide", 0)]
    gain = norm_gain.reshape(1, model_width)
    finished = attention_rows(
        queries,
        patch_keys,
        patch_values,
        other_keys,
        other_values,
        score_table,
        row_count,
        merge_order,
    )
    blocks = [block for block, _ in finished]
    stages = len(gather_order[0])
    own_weights = fetched(weights[::2])
    arrived = {}
    for stage in range(stages):
        for part in range(PARTS):
            arrived[part] = exchange(blocks[part], gather_order, stage)
            if stage < stages - 1:
                last = stage == stages - 2
                blocks[part], passed = joined(
                    blocks[part], arrived[part], own_weights if last else ()
                )
                own_weights = passed if last else own_weights
    came = [arrived[part] for part in range(PARTS)]
    device = device_index.reshape(1)
    gate_a, up_a, down_a = own_weights
    gate_b, up_b, down_b = weights[1::2]
    totals = first_expert_rows(
        device, gain, blocks, (*own_weights, gate_b, up_b, down_b)
    )
    gates = (gate_a, gate_b)
    outputs = []
    for part, (sent, kept) in enumerate(
        second_expert_rows(
            device, gain, came, gates, (up_a, up_b), (down_a, down_b), totals
        )
    ):
        for stage in range(stages + 1):
            arrived = exchange(sent, scatter_order[part], stage)
            kept = kept + arrived.astype(jnp.float32)
            half_rows = kept.shape[0] // 2
            if stage < stages:
                sent = kept[half_rows:].astype(jnp.bfloat16)
                kept = kept[:half_rows]
        outputs.append((finished[part][1].astype(jnp.float32) + kept).astype(jnp.bfloat16))
    return jnp.concatenate(outputs, axis=1)


def solution(mesh):
    return mapped(mesh)


def mapped(mesh):
    return jax.shard_map(
        on_device,
        mesh=mesh,
        in_specs=(
            P("groups", None),
            P(("groups", "wide"), None),
            P(("groups", "wide"), None),
            P(),
            P(("groups", "wide"), None),
            P(("groups", "wide"), None),
            P("wide", None),
            P("wide", None),
            P("wide", None),
        ),
        out_specs=P(("groups", "wide"), None),
        check_vma=False,
    )
```

```python
import functools

import jax
import jax.numpy as jnp
from jax import lax
from jax.experimental import pallas as pl
from jax.experimental.pallas import tpu as pltpu
from jax.sharding import PartitionSpec as P


HEADS = 16
LANES = 128
TABLE_LANE = 64
UNITS = 256
PARTS = 2


def near(value):
    return pltpu.with_memory_space_constraint(value, pltpu.VMEM)


def far(value):
    return pltpu.with_memory_space_constraint(value, pltpu.HBM)


def near_shape(shape, dtype):
    return pltpu.VMEM(shape, dtype)


def partner(value, axis, stride):
    mask = 2**stride
    pairs = [(source, source ^ mask) for source in range(lax.axis_size(axis))]
    return lax.ppermute(value, axis, pairs)


def plan_orders(devices, group_size):
    near_bits = list(range(1, group_size.bit_length() - 1))
    all_bits = list(range(1, devices.bit_length() - 1))
    merge = (near_bits, near_bits[1:] + near_bits[:1])
    rest = [[bit for bit in all_bits if bit != order[-1]] for order in merge]
    gather = (rest[0][::-1], rest[1][2:][::-1] + rest[1][:2])
    crossed = [order[:-2] + order[-2:][::-1] for order in gather]
    scatter = [
        [order[::-1] + kept[-1:] for order, kept in zip(orders, merge)]
        for orders in (gather, crossed)
    ]
    return merge, (gather, crossed), scatter


def exchange(value, orders, stage):
    pairs = [
        (source, source ^ (1 << orders[source % 2][stage]))
        for source in range(lax.axis_size("wide"))
    ]
    return lax.ppermute(value, "wide", pairs)


def lane_iota(shape):
    return lax.broadcasted_iota(jnp.int32, shape, 1)


def expand_tile(columns, tile, value_size):
    first = tile * LANES // value_size
    last = (tile * LANES + LANES - 1) // value_size
    rows = columns[0].shape[0]
    out = jnp.broadcast_to(columns[first], (rows, LANES))
    for head in range(first + 1, last + 1):
        edge = head * value_size - tile * LANES
        out = jnp.where(lane_iota((rows, LANES)) < edge, out, columns[head])
    return out


def pack_stats(peak, total, head_count):
    lane = lane_iota(peak.shape)
    high = total.astype(jnp.bfloat16).astype(jnp.float32)
    low = total - high
    packed = jnp.where(lane < head_count, peak, 0.0)
    shifted = pltpu.roll(jnp.where(lane < head_count, high, 0.0), head_count, 1)
    shifted_low = pltpu.roll(jnp.where(lane < head_count, low, 0.0), 2 * head_count, 1)
    return packed + shifted + shifted_low


def total_of(stats, head_count):
    return pltpu.roll(stats, LANES - head_count, 1) + pltpu.roll(
        stats, LANES - 2 * head_count, 1
    )


def head_windows(head, size):
    return head * size // LANES, -(-(head + 1) * size // LANES)


def head_scores(head, head_count, query_ref, keys_ref):
    key_size = query_ref.shape[1] // head_count
    low, high = [LANES * tile for tile in head_windows(head, key_size)]
    window = lane_iota((query_ref.shape[0], high - low)) + low
    inside = (window >= head * key_size) & (window < (head + 1) * key_size)
    query = jnp.where(inside, query_ref[:, low:high], jnp.zeros((), jnp.bfloat16))
    return key_size ** (-0.5) * lax.dot_general(
        query,
        keys_ref[:, low:high],
        (((1,), (1,)), ((), ())),
        preferred_element_type=jnp.float32,
    )


def rounded_peak(scores):
    peak = jnp.max(scores, axis=1, keepdims=True)
    return peak.astype(jnp.bfloat16).astype(jnp.float32)


def head_sums(head, value_size, raised, values_ref):
    low, high = head_windows(head, value_size)
    return jnp.dot(
        raised.astype(jnp.bfloat16),
        values_ref[:, low * LANES : high * LANES],
        preferred_element_type=jnp.float32,
    )


def stage_kernel(
    row_count,
    masks,
    device_ref,
    queries_ref,
    keys_ref,
    values_ref,
    query_ref,
    near_keys_ref,
    near_values_ref,
    arrived,
):
    group_size = queries_ref.shape[0] // row_count
    device = device_ref[0]
    odd = lax.rem(device, 2) == 1
    own_block = lax.rem(device, group_size)
    copies = [
        pltpu.make_async_copy(keys_ref, near_keys_ref, arrived.at[0]),
        pltpu.make_async_copy(values_ref, near_values_ref, arrived.at[1]),
    ]
    for slot, (even_mask, odd_mask) in enumerate(zip(*masks)):
        block = own_block ^ jnp.where(odd, odd_mask, even_mask)
        start = pl.multiple_of(block * row_count, row_count)
        copies.append(
            pltpu.make_async_copy(
                queries_ref.at[pl.ds(start, row_count), :],
                query_ref.at[slot * row_count : (slot + 1) * row_count, :],
                arrived.at[2 + slot],
            )
        )
    for copy in copies:
        copy.start()
    for copy in copies:
        copy.wait()


def attend_kernel(
    head_count, part, part_heads, query_ref, keys_a, keys_b, values_a, values_b, sent_ref, kept_ref
):
    rows = query_ref.shape[0]
    half = rows // 2
    value_size = values_a.shape[1] // head_count
    part_tiles = part_heads * value_size // LANES
    base = part * part_tiles
    lane = lane_iota((rows, LANES))
    peaks = jnp.zeros((rows, LANES), jnp.float32)
    totals = jnp.zeros((rows, LANES), jnp.float32)

    def put(tile, value):
        columns = slice(tile * LANES, (tile + 1) * LANES)
        kept_ref[:, columns] = value[:half]
        sent_ref[:, columns] = value[half:].astype(jnp.bfloat16)

    for at in range(part_heads):
        head = part * part_heads + at
        scores_a = head_scores(head, head_count, query_ref, keys_a)
        scores_b = head_scores(head, head_count, query_ref, keys_b)
        peak = jnp.maximum(rounded_peak(scores_a), rounded_peak(scores_b))
        raised_a = jnp.exp(scores_a - peak)
        raised_b = jnp.exp(scores_b - peak)
        total = jnp.sum(raised_a + raised_b, axis=1, keepdims=True)
        peaks = jnp.where(lane == at, peak, peaks)
        totals = jnp.where(lane == at, total, totals)
        summed = head_sums(head, value_size, raised_a, values_a) + head_sums(
            head, value_size, raised_b, values_b
        )
        low, high = head_windows(head, value_size)
        for tile in range(low, high):
            value = summed[:, (tile - low) * LANES : (tile - low + 1) * LANES]
            edge = head * value_size - tile * LANES
            if edge > 0:
                value = jnp.where(lane < edge, waiting, value)
            waiting = value
            if (tile + 1) * LANES <= (head + 1) * value_size:
                put(tile - base, value)
    put(part_tiles, pack_stats(peaks, totals, part_heads))


def merged_parts(kept_ref, came_ref, head_count, model_width):
    stats_a = kept_ref[:, model_width:]
    stats_b = came_ref[:, model_width:].astype(jnp.float32)
    peak = jnp.maximum(stats_a, stats_b)
    factor_a = jnp.exp(stats_a - peak)
    factor_b = jnp.exp(stats_b - peak)
    total = total_of(stats_a, head_count) * factor_a + total_of(stats_b, head_count) * factor_b
    return peak, total, factor_a, factor_b


def head_columns(array, head_count):
    return [array[:, head : head + 1] for head in range(head_count)]


def merge_kernel(head_count, kept_ref, came_ref, sent_ref, next_ref):
    model_width = kept_ref.shape[1] - LANES
    half = kept_ref.shape[0] // 2
    peak, total, factor_a, factor_b = merged_parts(kept_ref, came_ref, head_count, model_width)
    columns_a = head_columns(factor_a, head_count)
    columns_b = head_columns(factor_b, head_count)
    for tile in range(model_width // LANES + 1):
        columns = slice(tile * LANES, (tile + 1) * LANES)
        if tile * LANES == model_width:
            value = pack_stats(peak, total, head_count)
        else:
            value = kept_ref[:, columns] * expand_tile(
                columns_a, tile, model_width // head_count
            ) + came_ref[:, columns].astype(jnp.float32) * expand_tile(
                columns_b, tile, model_width // head_count
            )
        next_ref[:, columns] = value[:half]
        sent_ref[:, columns] = value[half:].astype(jnp.bfloat16)


def last_merge_kernel(head_count, kept_ref, came_ref, *rest):
    tables, (sent_ref, next_ref) = rest[:-2], rest[-2:]
    model_width = kept_ref.shape[1] - LANES
    half = kept_ref.shape[0] // 2
    peak, total, factor_a, factor_b = merged_parts(kept_ref, came_ref, head_count, model_width)
    columns_a = head_columns(factor_a, head_count)
    columns_b = head_columns(factor_b, head_count)
    for tile in range(model_width // LANES + 1):
        columns = slice(tile * LANES, (tile + 1) * LANES)
        if tile * LANES == model_width:
            value = pack_stats(peak, total, head_count)
            own = value[:half]
            for table_ref in tables:
                own = own + table_ref[...].astype(jnp.float32)
        else:
            value = kept_ref[:, columns] * expand_tile(
                columns_a, tile, model_width // head_count
            ) + came_ref[:, columns].astype(jnp.float32) * expand_tile(
                columns_b, tile, model_width // head_count
            )
            own = value[:half]
        next_ref[:, columns] = value
        sent_ref[:half, columns] = value[half:].astype(jnp.bfloat16)
        sent_ref[half:, columns] = own.astype(jnp.bfloat16)


def finish_kernel(part_heads, kept_ref, came_ref, *rest):
    tables, (block_ref, projected_ref) = rest[:-2], rest[-2:]
    half = kept_ref.shape[0] // 2
    width = kept_ref.shape[1] - LANES
    _, total, factor_a, factor_b = merged_parts(kept_ref, came_ref, part_heads, width)
    columns_a = head_columns(factor_a / total, part_heads)
    columns_b = head_columns(factor_b / total, part_heads)
    for tile in range(width // LANES):
        columns = slice(tile * LANES, (tile + 1) * LANES)
        value = kept_ref[:, columns] * expand_tile(
            columns_a, tile, width // part_heads
        ) + came_ref[:, columns].astype(jnp.float32) * expand_tile(
            columns_b, tile, width // part_heads
        )
        rounded = value.astype(jnp.bfloat16)
        block_ref[:, columns] = rounded
        projected_ref[:, columns] = rounded[:half]
    for table_ref in tables:
        came_table = came_ref[half:, width:]
        lane = lane_iota(came_table.shape)
        block_ref[:half, width:] = table_ref[...]
        block_ref[half:, width:] = jnp.where(
            lane >= TABLE_LANE, came_table.astype(jnp.float32), 0.0
        ).astype(jnp.bfloat16)


def down_product(hidden_ref, down_refs, out_ref, start):
    width = out_ref.shape[1]
    units = down_refs[0].shape[0]
    step = width // 2 if width % (4 * LANES) else 4 * LANES
    for low in range(0, width, step):
        columns = slice(start + low, start + low + step)
        out_ref[:, low : low + step] = sum(
            jnp.dot(
                hidden_ref[:, half * units : (half + 1) * units],
                down_ref[:, columns],
                preferred_element_type=jnp.float32,
            )
            for half, down_ref in enumerate(down_refs)
        ).astype(out_ref.dtype)


def fetch_kernel(*refs):
    count = (len(refs) - 1) // 2
    arrived = refs[-1]
    copies = [
        pltpu.make_async_copy(refs[i], refs[count + i], arrived.at[i]) for i in range(count)
    ]
    for copy in copies:
        copy.start()
    for copy in copies:
        copy.wait()


def fetched(arrays):
    return pl.pallas_call(
        fetch_kernel,
        compiler_params=pltpu.CompilerParams(vmem_limit_bytes=1 << 20),
        out_shape=tuple(near_shape(array.shape, array.dtype) for array in arrays),
        in_specs=[pl.BlockSpec(memory_space=pltpu.HBM)] * len(arrays),
        out_specs=(pl.BlockSpec(memory_space=pltpu.VMEM),) * len(arrays),
        scratch_shapes=[pltpu.SemaphoreType.DMA((len(arrays),))],
    )(*[far(array) for array in arrays])


def joined_kernel(own_ref, came_ref, *refs):
    out_ref = refs[len(refs) // 2]
    half = own_ref.shape[0]
    out_ref[:half, :] = own_ref[...]
    out_ref[half:, :] = came_ref[...]


def joined(own, came, passed=()):
    rows, width = own.shape
    whole = pl.BlockSpec(memory_space=pltpu.VMEM)
    out, *passed = pl.pallas_call(
        joined_kernel,
        compiler_params=pltpu.CompilerParams(vmem_limit_bytes=12 << 20),
        out_shape=(near_shape((2 * rows, width), own.dtype),)
        + tuple(near_shape(array.shape, array.dtype) for array in passed),
        in_specs=[whole] * (2 + len(passed)),
        out_specs=(whole,) * (1 + len(passed)),
        input_output_aliases={2 + i: 1 + i for i in range(len(passed))},
    )(near(own), near(came), *[near(array) for array in passed])
    return out, passed


def turned_half(rows_ref, gain_ref, start, width, turned):
    square = jnp.zeros((rows_ref.shape[0], LANES), jnp.float32)
    for low in range(0, width, LANES):
        residual = rows_ref[:, low : low + LANES].astype(jnp.float32)
        square = square + residual * residual
        gained = residual * gain_ref[:, start + low : start + low + LANES]
        turned[low : low + LANES, :] = gained.astype(jnp.bfloat16).T
    return jnp.sum(square.T, axis=0, keepdims=True)


def part_expert_kernel(
    part,
    device_ref,
    gain_ref,
    rows_ref,
    gate_a,
    gate_b,
    up_a,
    up_b,
    gates_ref,
    ups_ref,
    stats_ref,
    turned,
):
    width = turned.shape[0]
    stats_ref[0:1, :] = turned_half(rows_ref, gain_ref, part * width, width, turned)
    if rows_ref.shape[1] > width:
        scores = rows_ref[:, width:].astype(jnp.float32).T
        lane = lax.broadcasted_iota(jnp.int32, scores.shape, 0)
        chosen = jnp.where(lane == lax.div(device_ref[0], 2) + TABLE_LANE, scores, 0.0)
        stats_ref[1:2, :] = jnp.sum(chosen, axis=0, keepdims=True) / jnp.sum(
            scores, axis=0, keepdims=True
        )
    rows = turned[...]
    units = gate_a.shape[0]
    for weight_ref, low, out_ref in (
        (gate_a, 0, gates_ref),
        (gate_b, units, gates_ref),
        (up_a, 0, ups_ref),
        (up_b, units, ups_ref),
    ):
        out_ref[low : low + units, :] = jnp.dot(
            weight_ref[:, part * width : (part + 1) * width],
            rows,
            preferred_element_type=jnp.float32,
        )


def lower_pair(early, late):
    half = early.shape[1] // 2
    return jnp.where(lane_iota(early.shape) < half, early, pltpu.roll(late, half, 1))


def upper_pair(early, late):
    half = early.shape[1] // 2
    return jnp.where(lane_iota(early.shape) < half, pltpu.roll(early, half, 1), late)


def hidden_of(gate_part, up_part, inverse, share):
    gate_part = inverse * gate_part
    silu = gate_part / (1.0 + jnp.exp(-gate_part))
    return (silu * (inverse * up_part) * share).T.astype(jnp.bfloat16)


def second_expert_kernel(
    gain_ref,
    rows_ref,
    gates_ref,
    ups_ref,
    stats_ref,
    early_gates,
    early_ups,
    early_stats,
    gate_a,
    gate_b,
    up_a,
    up_b,
    down_a,
    down_b,
    out_ref,
    hidden,
    late_gates,
    late_ups,
    late_stats,
    turned,
):
    width = turned.shape[0]
    square = turned_half(rows_ref, gain_ref, width, width, turned)
    late_stats[0:1, :] = square
    row = (8, square.shape[1])
    other = upper_pair(
        jnp.broadcast_to(early_stats[0:1, :], row), jnp.broadcast_to(square, row)
    )[0:1, :]
    inverse = lax.rsqrt((stats_ref[0:1, :] + other) / (2 * width) + 1e-06)
    share = stats_ref[1:2, :]
    rows = turned[...]
    units = gate_a.shape[0]
    for half, (gate_ref, up_ref) in enumerate(((gate_a, up_a), (gate_b, up_b))):
        for low in range(0, units, UNITS):
            chunk = slice(low, low + UNITS)
            at = slice(half * units + low, half * units + low + UNITS)
            gate_part = jnp.dot(
                gate_ref[chunk, width:], rows, preferred_element_type=jnp.float32
            )
            up_part = jnp.dot(up_ref[chunk, width:], rows, preferred_element_type=jnp.float32)
            late_gates[at, :] = gate_part
            late_ups[at, :] = up_part
            hidden[:, at] = hidden_of(
                gates_ref[at, :] + upper_pair(early_gates[at, :], gate_part),
                ups_ref[at, :] + upper_pair(early_ups[at, :], up_part),
                inverse,
                share,
            )
    down_product(hidden, (down_a, down_b), out_ref, 0)


def rest_expert_kernel(
    hidden_ref,
    gates_ref,
    ups_ref,
    stats_ref,
    early_gates,
    early_ups,
    early_stats,
    late_gates,
    late_ups,
    late_stats,
    down_a,
    down_b,
    sent_ref,
    kept_ref,
    hidden,
    early_value,
    late_value,
):
    width = sent_ref.shape[1]
    row = (8, stats_ref.shape[1])
    other = lower_pair(
        jnp.broadcast_to(early_stats[0:1, :], row), jnp.broadcast_to(late_stats[0:1, :], row)
    )[0:1, :]
    inverse = lax.rsqrt((stats_ref[0:1, :] + other) / (2 * width) + 1e-06)
    for low in range(0, gates_ref.shape[0], UNITS):
        at = slice(low, low + UNITS)
        hidden[:, at] = hidden_of(
            gates_ref[at, :] + lower_pair(early_gates[at, :], late_gates[at, :]),
            ups_ref[at, :] + lower_pair(early_ups[at, :], late_ups[at, :]),
            inverse,
            stats_ref[1:2, :],
        )
    down_product(hidden, (down_a, down_b), early_value, width)
    down_product(hidden_ref, (down_a, down_b), late_value, width)
    half = early_value.shape[0] // 2
    sent_ref[:half, :] = early_value[half:, :].astype(sent_ref.dtype)
    sent_ref[half:, :] = late_value[half:, :].astype(sent_ref.dtype)
    kept_ref[:half, :] = early_value[:half, :]
    kept_ref[half:, :] = late_value[:half, :]


def kept_expert_kernel(hidden_ref, down_a, down_b, kept_ref):
    down_product(hidden_ref, (down_a, down_b), kept_ref, 0)


def part_expert_rows(part, device, gain, rows, gates, ups):
    units, model_width = gates[0].shape
    row_count = rows.shape[0]
    whole = pl.BlockSpec(memory_space=pltpu.VMEM)
    return pl.pallas_call(
        functools.partial(part_expert_kernel, part),
        compiler_params=pltpu.CompilerParams(vmem_limit_bytes=12 << 20),
        out_shape=(near_shape((2 * units, row_count), jnp.float32),) * 2
        + (near_shape((8, row_count), jnp.float32),),
        in_specs=[pl.BlockSpec(memory_space=pltpu.SMEM)] + [whole] * 6,
        out_specs=(whole,) * 3,
        scratch_shapes=[pltpu.VMEM((model_width // PARTS, row_count), jnp.bfloat16)],
    )(device, near(gain), near(rows), *[near(half) for half in (*gates, *ups)])


def expert_rows(device, gain, early, late, gates, ups, downs):
    units, model_width = gates[0].shape
    row_count = early[0].shape[0]
    width = model_width // PARTS
    whole = pl.BlockSpec(memory_space=pltpu.VMEM)
    first = [part_expert_rows(part, device, gain, early[part], gates, ups) for part in range(PARTS)]
    half = part_expert_rows(0, device, gain, late[0], gates, ups)
    products = (near_shape((2 * units, row_count), jnp.float32),) * 2 + (
        near_shape((8, row_count), jnp.float32),
    )
    hidden_shape = near_shape((row_count, 2 * units), jnp.bfloat16)
    operands = [gain, late[1], *half, *first[1], *gates, *ups, *downs]
    sent_first, hidden, *rest = pl.pallas_call(
        second_expert_kernel,
        name="expert_second",
        compiler_params=pltpu.CompilerParams(vmem_limit_bytes=12 << 20),
        out_shape=(near_shape((row_count, width), jnp.bfloat16), hidden_shape) + products,
        in_specs=[whole] * len(operands),
        out_specs=(whole,) * 5,
        scratch_shapes=[pltpu.VMEM((width, row_count), jnp.bfloat16)],
    )(*[near(operand) for operand in operands])
    operands = [hidden, *first[0], *first[1], *rest, *downs]
    sent, kept, hidden = pl.pallas_call(
        rest_expert_kernel,
        name="expert_rest",
        compiler_params=pltpu.CompilerParams(vmem_limit_bytes=12 << 20),
        out_shape=(
            near_shape((row_count, width), jnp.bfloat16),
            near_shape((row_count, width), jnp.float32),
            hidden_shape,
        ),
        in_specs=[whole] * len(operands),
        out_specs=(whole,) * 3,
        scratch_shapes=[pltpu.VMEM((row_count, width), jnp.float32)] * 2,
    )(*[near(operand) for operand in operands])
    kept_first = pl.pallas_call(
        kept_expert_kernel,
        name="expert_kept",
        compiler_params=pltpu.CompilerParams(vmem_limit_bytes=12 << 20),
        out_shape=near_shape((row_count, width), jnp.float32),
        in_specs=[whole] * 3,
        out_specs=whole,
    )(*[near(operand) for operand in (hidden, *downs)])
    return [(sent_first, kept_first), (sent, kept)]


def attention_rows(
    queries, patch_keys, patch_values, other_keys, other_values, table, row_count, orders
):
    model_width = patch_values.shape[1]
    part_width = model_width // PARTS + LANES
    part_heads = HEADS // PARTS
    stages = len(orders[0])
    device_index = lax.axis_index("wide")
    masks = [
        [
            sum(
                (1 << order[stage])
                for stage in range(stages)
                if slot >> (stages - 1 - stage) & 1
            )
            for slot in range(1 << stages)
        ]
        for order in orders
    ]
    rows = row_count << stages
    whole = pl.BlockSpec(memory_space=pltpu.VMEM)

    def pair_shapes(rows):
        return (
            near_shape((rows, part_width), jnp.bfloat16),
            near_shape((rows, part_width), jnp.float32),
        )

    anywhere = pl.BlockSpec(memory_space=pltpu.HBM)
    query_rows, own_keys, own_values = pl.pallas_call(
        functools.partial(stage_kernel, row_count, masks),
        name="stage_in",
        compiler_params=pltpu.CompilerParams(vmem_limit_bytes=4 << 20),
        out_shape=(
            near_shape((rows, queries.shape[1]), jnp.bfloat16),
            near_shape(patch_keys.shape, jnp.bfloat16),
            near_shape(patch_values.shape, jnp.bfloat16),
        ),
        in_specs=[pl.BlockSpec(memory_space=pltpu.SMEM)] + [anywhere] * 3,
        out_specs=(whole,) * 3,
        scratch_shapes=[pltpu.SemaphoreType.DMA((2 + (1 << stages),))],
    )(device_index.reshape(1), far(queries), far(patch_keys), far(patch_values))
    operands = (query_rows, own_keys, other_keys, own_values, other_values)
    chains = []
    for part in range(PARTS):
        chains += pl.pallas_call(
            functools.partial(attend_kernel, HEADS, part, part_heads),
            compiler_params=pltpu.CompilerParams(vmem_limit_bytes=8 << 20),
            out_shape=pair_shapes(rows // 2),
            in_specs=[whole] * 5,
            out_specs=(whole, whole),
        )(*[near(operand) for operand in operands])
    finished = []
    for part in range(PARTS):
        sent, kept = chains[2 * part : 2 * part + 2]
        for stage in range(stages - 1):
            came = exchange(sent, orders, stage)
            rows = kept.shape[0]
            last = stage == stages - 2
            operands = [near(kept), near(came)]
            if last and part == 0:
                operands.append(near(table))
            sent, kept = pl.pallas_call(
                functools.partial(last_merge_kernel if last else merge_kernel, part_heads),
                compiler_params=pltpu.CompilerParams(vmem_limit_bytes=6 << 20),
                out_shape=pair_shapes(rows if last else rows // 2),
                in_specs=[whole] * len(operands),
                out_specs=(whole, whole),
            )(*operands)
        came = exchange(sent, orders, stages - 1)
        rows = kept.shape[0]
        width = model_width // PARTS
        operands = [near(kept), near(came)] + ([near(table)] if part == 0 else [])
        block, projected = pl.pallas_call(
            functools.partial(finish_kernel, part_heads),
            compiler_params=pltpu.CompilerParams(vmem_limit_bytes=6 << 20),
            out_shape=(
                near_shape((rows, width + (LANES if part == 0 else 0)), jnp.bfloat16),
                near_shape((row_count, width), jnp.bfloat16),
            ),
            in_specs=[whole] * len(operands),
            out_specs=(whole, whole),
        )(*operands)
        finished.append((block, projected))
    return finished


def on_device(
    queries, patch_keys, patch_values, norm_gain, route_experts, route_weights, w_gate, w_up, w_down
):
    row_count = route_experts.shape[0]
    model_width = patch_values.shape[1]
    devices = lax.axis_size("wide")
    device_index = lax.axis_index("wide")
    score_table = jnp.sum(
        jnp.where(
            route_experts[:, :, None] == jnp.arange(-TABLE_LANE, LANES - TABLE_LANE, dtype=jnp.int32),
            route_weights[:, :, None],
            0,
        ),
        axis=1,
    ).astype(jnp.bfloat16)
    merge_order, gather_order, scatter_order = plan_orders(
        devices, queries.shape[0] // row_count
    )
    other_keys = partner(patch_keys, "wide", 0)
    other_values = partner(patch_values, "wide", 0)
    halves, other_keys, other_values = lax.optimization_barrier(
        ((w_gate, w_up, w_down), other_keys, other_values)
    )
    weights = []
    for own in halves:
        weights += [own, partner(own, "wide", 0)]
    gain = norm_gain.reshape(1, model_width)
    finished = attention_rows(
        queries,
        patch_keys,
        patch_values,
        other_keys,
        other_values,
        score_table,
        row_count,
        merge_order,
    )
    blocks = [block for block, _ in finished]
    stages = len(gather_order[0][0])
    own_weights = fetched(weights[::2])
    arrived = {}
    for stage in range(stages):
        for part in range(PARTS):
            arrived[part] = exchange(blocks[part], gather_order[part], stage)
            if stage < stages - 1:
                last = stage == stages - 2
                blocks[part], passed = joined(
                    blocks[part], arrived[part], own_weights if last else ()
                )
                own_weights = passed if last else own_weights
    came = [arrived[part] for part in range(PARTS)]
    device = device_index.reshape(1)
    gate_a, up_a, down_a = own_weights
    gate_b, up_b, down_b = weights[1::2]
    gates, ups, downs = (gate_a, gate_b), (up_a, up_b), (down_a, down_b)
    outputs = []
    for part, (sent, kept) in enumerate(
        expert_rows(device, gain, blocks, came, gates, ups, downs)
    ):
        for stage in range(stages + 1):
            arrived = exchange(sent, scatter_order[part], stage)
            kept = kept + arrived.astype(jnp.float32)
            half_rows = kept.shape[0] // 2
            if stage < stages:
                sent = kept[half_rows:].astype(jnp.bfloat16)
                kept = kept[:half_rows]
        outputs.append((finished[part][1].astype(jnp.float32) + kept).astype(jnp.bfloat16))
    return jnp.concatenate(outputs, axis=1)


def solution(mesh):
    return mapped(mesh)


def mapped(mesh):
    return jax.shard_map(
        on_device,
        mesh=mesh,
        in_specs=(
            P("groups", None),
            P(("groups", "wide"), None),
            P(("groups", "wide"), None),
            P(),
            P(("groups", "wide"), None),
            P(("groups", "wide"), None),
            P("wide", None),
            P("wide", None),
            P("wide", None),
        ),
        out_specs=P(("groups", "wide"), None),
        check_vma=False,
    )
```

```python
import functools

import jax
import jax.numpy as jnp
from jax import lax
from jax.experimental import pallas as pl
from jax.experimental.pallas import tpu as pltpu
from jax.sharding import PartitionSpec as P


HEADS = 16
LANES = 128
TABLE_LANE = 64
UNITS = 256
PARTS = 2


def near(value):
    return pltpu.with_memory_space_constraint(value, pltpu.VMEM)


def far(value):
    return pltpu.with_memory_space_constraint(value, pltpu.HBM)


def near_shape(shape, dtype):
    return pltpu.VMEM(shape, dtype)


def partner(value, axis, stride):
    mask = 2**stride
    pairs = [(source, source ^ mask) for source in range(lax.axis_size(axis))]
    return lax.ppermute(value, axis, pairs)


def plan_orders(devices, group_size):
    near_bits = list(range(1, group_size.bit_length() - 1))
    all_bits = list(range(1, devices.bit_length() - 1))
    merge = (near_bits, near_bits[1:] + near_bits[:1])
    rest = [[bit for bit in all_bits if bit != order[-1]] for order in merge]
    gather = (rest[0][::-1], rest[1][2:][::-1] + rest[1][:2])
    crossed = [order[:-2] + order[-2:][::-1] for order in gather]
    scatter = [
        [order[::-1] + kept[-1:] for order, kept in zip(orders, merge)]
        for orders in (gather, crossed)
    ]
    return merge, (gather, crossed), scatter


def exchange(value, orders, stage):
    pairs = [
        (source, source ^ (1 << orders[source % 2][stage]))
        for source in range(lax.axis_size("wide"))
    ]
    return lax.ppermute(value, "wide", pairs)


def lane_iota(shape):
    return lax.broadcasted_iota(jnp.int32, shape, 1)


def expand_tile(columns, tile, value_size):
    first = tile * LANES // value_size
    last = (tile * LANES + LANES - 1) // value_size
    rows = columns[0].shape[0]
    out = jnp.broadcast_to(columns[first], (rows, LANES))
    for head in range(first + 1, last + 1):
        edge = head * value_size - tile * LANES
        out = jnp.where(lane_iota((rows, LANES)) < edge, out, columns[head])
    return out


def pack_stats(peak, total, head_count):
    lane = lane_iota(peak.shape)
    high = total.astype(jnp.bfloat16).astype(jnp.float32)
    low = total - high
    packed = jnp.where(lane < head_count, peak, 0.0)
    shifted = pltpu.roll(jnp.where(lane < head_count, high, 0.0), head_count, 1)
    shifted_low = pltpu.roll(jnp.where(lane < head_count, low, 0.0), 2 * head_count, 1)
    return packed + shifted + shifted_low


def total_of(stats, head_count):
    return pltpu.roll(stats, LANES - head_count, 1) + pltpu.roll(
        stats, LANES - 2 * head_count, 1
    )


def head_windows(head, size):
    return head * size // LANES, -(-(head + 1) * size // LANES)


def head_scores(head, head_count, query_ref, keys_ref):
    key_size = query_ref.shape[1] // head_count
    low, high = [LANES * tile for tile in head_windows(head, key_size)]
    window = lane_iota((query_ref.shape[0], high - low)) + low
    inside = (window >= head * key_size) & (window < (head + 1) * key_size)
    query = jnp.where(inside, query_ref[:, low:high], jnp.zeros((), jnp.bfloat16))
    return key_size ** (-0.5) * lax.dot_general(
        query,
        keys_ref[:, low:high],
        (((1,), (1,)), ((), ())),
        preferred_element_type=jnp.float32,
    )


def rounded_peak(scores):
    peak = jnp.max(scores, axis=1, keepdims=True)
    return peak.astype(jnp.bfloat16).astype(jnp.float32)


def head_sums(head, value_size, raised, values_ref):
    low, high = head_windows(head, value_size)
    return jnp.dot(
        raised.astype(jnp.bfloat16),
        values_ref[:, low * LANES : high * LANES],
        preferred_element_type=jnp.float32,
    )


def stage_kernel(
    row_count,
    masks,
    device_ref,
    queries_ref,
    keys_ref,
    values_ref,
    query_ref,
    near_keys_ref,
    near_values_ref,
    arrived,
):
    group_size = queries_ref.shape[0] // row_count
    device = device_ref[0]
    odd = lax.rem(device, 2) == 1
    own_block = lax.rem(device, group_size)
    copies = [
        pltpu.make_async_copy(keys_ref, near_keys_ref, arrived.at[0]),
        pltpu.make_async_copy(values_ref, near_values_ref, arrived.at[1]),
    ]
    for slot, (even_mask, odd_mask) in enumerate(zip(*masks)):
        block = own_block ^ jnp.where(odd, odd_mask, even_mask)
        start = pl.multiple_of(block * row_count, row_count)
        copies.append(
            pltpu.make_async_copy(
                queries_ref.at[pl.ds(start, row_count), :],
                query_ref.at[slot * row_count : (slot + 1) * row_count, :],
                arrived.at[2 + slot],
            )
        )
    for copy in copies:
        copy.start()
    for copy in copies:
        copy.wait()


def attend_kernel(
    head_count, part, part_heads, query_ref, keys_a, keys_b, values_a, values_b, sent_ref, kept_ref
):
    rows = query_ref.shape[0]
    half = rows // 2
    value_size = values_a.shape[1] // head_count
    part_tiles = part_heads * value_size // LANES
    base = part * part_tiles
    lane = lane_iota((rows, LANES))
    peaks = jnp.zeros((rows, LANES), jnp.float32)
    totals = jnp.zeros((rows, LANES), jnp.float32)

    def put(tile, value):
        columns = slice(tile * LANES, (tile + 1) * LANES)
        kept_ref[:, columns] = value[:half]
        sent_ref[:, columns] = value[half:].astype(jnp.bfloat16)

    for at in range(part_heads):
        head = part * part_heads + at
        scores_a = head_scores(head, head_count, query_ref, keys_a)
        scores_b = head_scores(head, head_count, query_ref, keys_b)
        peak = jnp.maximum(rounded_peak(scores_a), rounded_peak(scores_b))
        raised_a = jnp.exp(scores_a - peak)
        raised_b = jnp.exp(scores_b - peak)
        total = jnp.sum(raised_a + raised_b, axis=1, keepdims=True)
        peaks = jnp.where(lane == at, peak, peaks)
        totals = jnp.where(lane == at, total, totals)
        summed = head_sums(head, value_size, raised_a, values_a) + head_sums(
            head, value_size, raised_b, values_b
        )
        low, high = head_windows(head, value_size)
        for tile in range(low, high):
            value = summed[:, (tile - low) * LANES : (tile - low + 1) * LANES]
            edge = head * value_size - tile * LANES
            if edge > 0:
                value = jnp.where(lane < edge, waiting, value)
            waiting = value
            if (tile + 1) * LANES <= (head + 1) * value_size:
                put(tile - base, value)
    put(part_tiles, pack_stats(peaks, totals, part_heads))


def merged_parts(kept_ref, came_ref, head_count, model_width):
    stats_a = kept_ref[:, model_width:]
    stats_b = came_ref[:, model_width:].astype(jnp.float32)
    peak = jnp.maximum(stats_a, stats_b)
    factor_a = jnp.exp(stats_a - peak)
    factor_b = jnp.exp(stats_b - peak)
    total = total_of(stats_a, head_count) * factor_a + total_of(stats_b, head_count) * factor_b
    return peak, total, factor_a, factor_b


def head_columns(array, head_count):
    return [array[:, head : head + 1] for head in range(head_count)]


def merge_kernel(head_count, kept_ref, came_ref, sent_ref, next_ref):
    model_width = kept_ref.shape[1] - LANES
    half = kept_ref.shape[0] // 2
    peak, total, factor_a, factor_b = merged_parts(kept_ref, came_ref, head_count, model_width)
    columns_a = head_columns(factor_a, head_count)
    columns_b = head_columns(factor_b, head_count)
    for tile in range(model_width // LANES + 1):
        columns = slice(tile * LANES, (tile + 1) * LANES)
        if tile * LANES == model_width:
            value = pack_stats(peak, total, head_count)
        else:
            value = kept_ref[:, columns] * expand_tile(
                columns_a, tile, model_width // head_count
            ) + came_ref[:, columns].astype(jnp.float32) * expand_tile(
                columns_b, tile, model_width // head_count
            )
        next_ref[:, columns] = value[:half]
        sent_ref[:, columns] = value[half:].astype(jnp.bfloat16)


def last_merge_kernel(head_count, kept_ref, came_ref, *rest):
    tables, (sent_ref, next_ref) = rest[:-2], rest[-2:]
    model_width = kept_ref.shape[1] - LANES
    half = kept_ref.shape[0] // 2
    peak, total, factor_a, factor_b = merged_parts(kept_ref, came_ref, head_count, model_width)
    columns_a = head_columns(factor_a, head_count)
    columns_b = head_columns(factor_b, head_count)
    for tile in range(model_width // LANES + 1):
        columns = slice(tile * LANES, (tile + 1) * LANES)
        if tile * LANES == model_width:
            value = pack_stats(peak, total, head_count)
            own = value[:half]
            for table_ref in tables:
                own = own + table_ref[...].astype(jnp.float32)
        else:
            value = kept_ref[:, columns] * expand_tile(
                columns_a, tile, model_width // head_count
            ) + came_ref[:, columns].astype(jnp.float32) * expand_tile(
                columns_b, tile, model_width // head_count
            )
            own = value[:half]
        next_ref[:, columns] = value
        sent_ref[:half, columns] = value[half:].astype(jnp.bfloat16)
        sent_ref[half:, columns] = own.astype(jnp.bfloat16)


def finish_kernel(part_heads, kept_ref, came_ref, *rest):
    tables, (block_ref, projected_ref) = rest[:-2], rest[-2:]
    half = kept_ref.shape[0] // 2
    width = kept_ref.shape[1] - LANES
    _, total, factor_a, factor_b = merged_parts(kept_ref, came_ref, part_heads, width)
    columns_a = head_columns(factor_a / total, part_heads)
    columns_b = head_columns(factor_b / total, part_heads)
    for tile in range(width // LANES):
        columns = slice(tile * LANES, (tile + 1) * LANES)
        value = kept_ref[:, columns] * expand_tile(
            columns_a, tile, width // part_heads
        ) + came_ref[:, columns].astype(jnp.float32) * expand_tile(
            columns_b, tile, width // part_heads
        )
        rounded = value.astype(jnp.bfloat16)
        block_ref[:, columns] = rounded
        projected_ref[:, columns] = rounded[:half]
    for table_ref in tables:
        came_table = came_ref[half:, width:]
        lane = lane_iota(came_table.shape)
        block_ref[:half, width:] = table_ref[...]
        block_ref[half:, width:] = jnp.where(
            lane >= TABLE_LANE, came_table.astype(jnp.float32), 0.0
        ).astype(jnp.bfloat16)


def down_product(hidden_ref, down_refs, out_ref, start):
    width = out_ref.shape[1]
    units = down_refs[0].shape[0]
    step = width // 2 if width % (4 * LANES) else 4 * LANES
    for low in range(0, width, step):
        columns = slice(start + low, start + low + step)
        out_ref[:, low : low + step] = sum(
            jnp.dot(
                hidden_ref[:, half * units : (half + 1) * units],
                down_ref[:, columns],
                preferred_element_type=jnp.float32,
            )
            for half, down_ref in enumerate(down_refs)
        ).astype(out_ref.dtype)


def joined_kernel(own_ref, came_ref, out_ref):
    half = own_ref.shape[0]
    out_ref[:half, :] = own_ref[...]
    out_ref[half:, :] = came_ref[...]


def joined(own, came):
    rows, width = own.shape
    whole = pl.BlockSpec(memory_space=pltpu.VMEM)
    return pl.pallas_call(
        joined_kernel,
        compiler_params=pltpu.CompilerParams(vmem_limit_bytes=12 << 20),
        out_shape=near_shape((2 * rows, width), own.dtype),
        in_specs=[whole] * 2,
        out_specs=whole,
    )(near(own), near(came))


def turned_half(rows_ref, gain_ref, start, width, turned):
    square = jnp.zeros((rows_ref.shape[0], LANES), jnp.float32)
    for low in range(0, width, LANES):
        residual = rows_ref[:, low : low + LANES].astype(jnp.float32)
        square = square + residual * residual
        gained = residual * gain_ref[:, start + low : start + low + LANES]
        turned[low : low + LANES, :] = gained.astype(jnp.bfloat16).T
    return jnp.sum(square.T, axis=0, keepdims=True)


def part_expert_kernel(
    part,
    device_ref,
    gain_ref,
    rows_ref,
    gate_a,
    gate_b,
    up_a,
    up_b,
    gates_ref,
    ups_ref,
    stats_ref,
    turned,
):
    width = turned.shape[0]
    stats_ref[0:1, :] = turned_half(rows_ref, gain_ref, part * width, width, turned)
    if rows_ref.shape[1] > width:
        scores = rows_ref[:, width:].astype(jnp.float32).T
        lane = lax.broadcasted_iota(jnp.int32, scores.shape, 0)
        chosen = jnp.where(lane == lax.div(device_ref[0], 2) + TABLE_LANE, scores, 0.0)
        stats_ref[1:2, :] = jnp.sum(chosen, axis=0, keepdims=True) / jnp.sum(
            scores, axis=0, keepdims=True
        )
    rows = turned[...]
    units = gate_a.shape[0]
    for weight_ref, low, out_ref in (
        (gate_a, 0, gates_ref),
        (gate_b, units, gates_ref),
        (up_a, 0, ups_ref),
        (up_b, units, ups_ref),
    ):
        out_ref[low : low + units, :] = jnp.dot(
            weight_ref[:, part * width : (part + 1) * width],
            rows,
            preferred_element_type=jnp.float32,
        )


def lower_pair(early, late):
    half = early.shape[1] // 2
    return jnp.where(lane_iota(early.shape) < half, early, pltpu.roll(late, half, 1))


def upper_pair(early, late):
    half = early.shape[1] // 2
    return jnp.where(lane_iota(early.shape) < half, pltpu.roll(early, half, 1), late)


def hidden_of(gate_part, up_part, inverse, share):
    gate_part = inverse * gate_part
    silu = gate_part / (1.0 + jnp.exp(-gate_part))
    return (silu * (inverse * up_part) * share).T.astype(jnp.bfloat16)


def second_expert_kernel(
    gain_ref,
    rows_ref,
    gates_ref,
    ups_ref,
    stats_ref,
    early_gates,
    early_ups,
    early_stats,
    gate_a,
    gate_b,
    up_a,
    up_b,
    down_a,
    down_b,
    out_ref,
    hidden,
    late_gates,
    late_ups,
    late_stats,
    turned,
):
    width = turned.shape[0]
    square = turned_half(rows_ref, gain_ref, width, width, turned)
    late_stats[0:1, :] = square
    row = (8, square.shape[1])
    other = upper_pair(
        jnp.broadcast_to(early_stats[0:1, :], row), jnp.broadcast_to(square, row)
    )[0:1, :]
    inverse = lax.rsqrt((stats_ref[0:1, :] + other) / (2 * width) + 1e-06)
    share = stats_ref[1:2, :]
    rows = turned[...]
    units = gate_a.shape[0]
    for half, (gate_ref, up_ref) in enumerate(((gate_a, up_a), (gate_b, up_b))):
        for low in range(0, units, UNITS):
            chunk = slice(low, low + UNITS)
            at = slice(half * units + low, half * units + low + UNITS)
            gate_part = jnp.dot(
                gate_ref[chunk, width:], rows, preferred_element_type=jnp.float32
            )
            up_part = jnp.dot(up_ref[chunk, width:], rows, preferred_element_type=jnp.float32)
            late_gates[at, :] = gate_part
            late_ups[at, :] = up_part
            hidden[:, at] = hidden_of(
                gates_ref[at, :] + upper_pair(early_gates[at, :], gate_part),
                ups_ref[at, :] + upper_pair(early_ups[at, :], up_part),
                inverse,
                share,
            )
    down_product(hidden, (down_a, down_b), out_ref, 0)


def rest_expert_kernel(
    hidden_ref,
    gates_ref,
    ups_ref,
    stats_ref,
    early_gates,
    early_ups,
    early_stats,
    late_gates,
    late_ups,
    late_stats,
    down_a,
    down_b,
    sent_ref,
    kept_ref,
    hidden,
    early_value,
    late_value,
):
    width = sent_ref.shape[1]
    row = (8, stats_ref.shape[1])
    other = lower_pair(
        jnp.broadcast_to(early_stats[0:1, :], row), jnp.broadcast_to(late_stats[0:1, :], row)
    )[0:1, :]
    inverse = lax.rsqrt((stats_ref[0:1, :] + other) / (2 * width) + 1e-06)
    for low in range(0, gates_ref.shape[0], UNITS):
        at = slice(low, low + UNITS)
        hidden[:, at] = hidden_of(
            gates_ref[at, :] + lower_pair(early_gates[at, :], late_gates[at, :]),
            ups_ref[at, :] + lower_pair(early_ups[at, :], late_ups[at, :]),
            inverse,
            stats_ref[1:2, :],
        )
    down_product(hidden, (down_a, down_b), early_value, width)
    down_product(hidden_ref, (down_a, down_b), late_value, width)
    half = early_value.shape[0] // 2
    sent_ref[:half, :] = early_value[half:, :].astype(sent_ref.dtype)
    sent_ref[half:, :] = late_value[half:, :].astype(sent_ref.dtype)
    kept_ref[:half, :] = early_value[:half, :]
    kept_ref[half:, :] = late_value[:half, :]


def kept_expert_kernel(hidden_ref, down_a, down_b, kept_ref):
    down_product(hidden_ref, (down_a, down_b), kept_ref, 0)


def part_expert_rows(part, device, gain, rows, gates, ups):
    units, model_width = gates[0].shape
    row_count = rows.shape[0]
    whole = pl.BlockSpec(memory_space=pltpu.VMEM)
    return pl.pallas_call(
        functools.partial(part_expert_kernel, part),
        compiler_params=pltpu.CompilerParams(vmem_limit_bytes=12 << 20),
        out_shape=(near_shape((2 * units, row_count), jnp.float32),) * 2
        + (near_shape((8, row_count), jnp.float32),),
        in_specs=[pl.BlockSpec(memory_space=pltpu.SMEM)] + [whole] * 6,
        out_specs=(whole,) * 3,
        scratch_shapes=[pltpu.VMEM((model_width // PARTS, row_count), jnp.bfloat16)],
    )(device, near(gain), near(rows), *[near(half) for half in (*gates, *ups)])


def expert_rows(device, gain, early, late, gates, ups, downs):
    units, model_width = gates[0].shape
    row_count = early[0].shape[0]
    width = model_width // PARTS
    whole = pl.BlockSpec(memory_space=pltpu.VMEM)
    first = [part_expert_rows(part, device, gain, early[part], gates, ups) for part in range(PARTS)]
    half = part_expert_rows(0, device, gain, late[0], gates, ups)
    products = (near_shape((2 * units, row_count), jnp.float32),) * 2 + (
        near_shape((8, row_count), jnp.float32),
    )
    hidden_shape = near_shape((row_count, 2 * units), jnp.bfloat16)
    operands = [gain, late[1], *half, *first[1], *gates, *ups, *downs]
    sent_first, hidden, *rest = pl.pallas_call(
        second_expert_kernel,
        name="expert_second",
        compiler_params=pltpu.CompilerParams(vmem_limit_bytes=12 << 20),
        out_shape=(near_shape((row_count, width), jnp.bfloat16), hidden_shape) + products,
        in_specs=[whole] * len(operands),
        out_specs=(whole,) * 5,
        scratch_shapes=[pltpu.VMEM((width, row_count), jnp.bfloat16)],
    )(*[near(operand) for operand in operands])
    operands = [hidden, *first[0], *first[1], *rest, *downs]
    sent, kept, hidden = pl.pallas_call(
        rest_expert_kernel,
        name="expert_rest",
        compiler_params=pltpu.CompilerParams(vmem_limit_bytes=12 << 20),
        out_shape=(
            near_shape((row_count, width), jnp.bfloat16),
            near_shape((row_count, width), jnp.float32),
            hidden_shape,
        ),
        in_specs=[whole] * len(operands),
        out_specs=(whole,) * 3,
        scratch_shapes=[pltpu.VMEM((row_count, width), jnp.float32)] * 2,
    )(*[near(operand) for operand in operands])
    kept_first = pl.pallas_call(
        kept_expert_kernel,
        name="expert_kept",
        compiler_params=pltpu.CompilerParams(vmem_limit_bytes=12 << 20),
        out_shape=near_shape((row_count, width), jnp.float32),
        in_specs=[whole] * 3,
        out_specs=whole,
    )(*[near(operand) for operand in (hidden, *downs)])
    return [(sent_first, kept_first), (sent, kept)]


def attention_rows(
    queries, patch_keys, patch_values, other_keys, other_values, table, row_count, orders
):
    model_width = patch_values.shape[1]
    part_width = model_width // PARTS + LANES
    part_heads = HEADS // PARTS
    stages = len(orders[0])
    device_index = lax.axis_index("wide")
    masks = [
        [
            sum(
                (1 << order[stage])
                for stage in range(stages)
                if slot >> (stages - 1 - stage) & 1
            )
            for slot in range(1 << stages)
        ]
        for order in orders
    ]
    rows = row_count << stages
    whole = pl.BlockSpec(memory_space=pltpu.VMEM)

    def pair_shapes(rows):
        return (
            near_shape((rows, part_width), jnp.bfloat16),
            near_shape((rows, part_width), jnp.float32),
        )

    anywhere = pl.BlockSpec(memory_space=pltpu.HBM)
    query_rows, own_keys, own_values = pl.pallas_call(
        functools.partial(stage_kernel, row_count, masks),
        name="stage_in",
        compiler_params=pltpu.CompilerParams(vmem_limit_bytes=4 << 20),
        out_shape=(
            near_shape((rows, queries.shape[1]), jnp.bfloat16),
            near_shape(patch_keys.shape, jnp.bfloat16),
            near_shape(patch_values.shape, jnp.bfloat16),
        ),
        in_specs=[pl.BlockSpec(memory_space=pltpu.SMEM)] + [anywhere] * 3,
        out_specs=(whole,) * 3,
        scratch_shapes=[pltpu.SemaphoreType.DMA((2 + (1 << stages),))],
    )(device_index.reshape(1), far(queries), far(patch_keys), far(patch_values))
    operands = (query_rows, own_keys, other_keys, own_values, other_values)
    chains = []
    for part in range(PARTS):
        chains += pl.pallas_call(
            functools.partial(attend_kernel, HEADS, part, part_heads),
            compiler_params=pltpu.CompilerParams(vmem_limit_bytes=8 << 20),
            out_shape=pair_shapes(rows // 2),
            in_specs=[whole] * 5,
            out_specs=(whole, whole),
        )(*[near(operand) for operand in operands])
    finished = []
    for part in range(PARTS):
        sent, kept = chains[2 * part : 2 * part + 2]
        for stage in range(stages - 1):
            came = exchange(sent, orders, stage)
            rows = kept.shape[0]
            last = stage == stages - 2
            operands = [near(kept), near(came)]
            if last and part == 0:
                operands.append(near(table))
            sent, kept = pl.pallas_call(
                functools.partial(last_merge_kernel if last else merge_kernel, part_heads),
                compiler_params=pltpu.CompilerParams(vmem_limit_bytes=6 << 20),
                out_shape=pair_shapes(rows if last else rows // 2),
                in_specs=[whole] * len(operands),
                out_specs=(whole, whole),
            )(*operands)
        came = exchange(sent, orders, stages - 1)
        rows = kept.shape[0]
        width = model_width // PARTS
        operands = [near(kept), near(came)] + ([near(table)] if part == 0 else [])
        block, projected = pl.pallas_call(
            functools.partial(finish_kernel, part_heads),
            compiler_params=pltpu.CompilerParams(vmem_limit_bytes=6 << 20),
            out_shape=(
                near_shape((rows, width + (LANES if part == 0 else 0)), jnp.bfloat16),
                near_shape((row_count, width), jnp.bfloat16),
            ),
            in_specs=[whole] * len(operands),
            out_specs=(whole, whole),
        )(*operands)
        finished.append((block, projected))
    return finished


def on_device(
    queries, patch_keys, patch_values, norm_gain, route_experts, route_weights, w_gate, w_up, w_down
):
    row_count = route_experts.shape[0]
    model_width = patch_values.shape[1]
    devices = lax.axis_size("wide")
    device_index = lax.axis_index("wide")
    score_table = jnp.sum(
        jnp.where(
            route_experts[:, :, None] == jnp.arange(-TABLE_LANE, LANES - TABLE_LANE, dtype=jnp.int32),
            route_weights[:, :, None],
            0,
        ),
        axis=1,
    ).astype(jnp.bfloat16)
    merge_order, gather_order, scatter_order = plan_orders(
        devices, queries.shape[0] // row_count
    )
    other_keys = partner(patch_keys, "wide", 0)
    other_values = partner(patch_values, "wide", 0)
    halves, other_keys, other_values = lax.optimization_barrier(
        ((w_gate, w_up, w_down), other_keys, other_values)
    )
    weights = []
    for own in halves:
        weights += [own, partner(own, "wide", 0)]
    gain = norm_gain.reshape(1, model_width)
    finished = attention_rows(
        queries,
        patch_keys,
        patch_values,
        other_keys,
        other_values,
        score_table,
        row_count,
        merge_order,
    )
    blocks = [block for block, _ in finished]
    stages = len(gather_order[0][0])
    own_weights = weights[::2]
    arrived = {}
    for stage in range(stages):
        for part in range(PARTS):
            arrived[part] = exchange(blocks[part], gather_order[part], stage)
            if stage < stages - 1:
                blocks[part] = joined(blocks[part], arrived[part])
    came = [arrived[part] for part in range(PARTS)]
    device = device_index.reshape(1)
    gate_a, up_a, down_a = own_weights
    gate_b, up_b, down_b = weights[1::2]
    gates, ups, downs = (gate_a, gate_b), (up_a, up_b), (down_a, down_b)
    outputs = []
    for part, (sent, kept) in enumerate(
        expert_rows(device, gain, blocks, came, gates, ups, downs)
    ):
        for stage in range(stages + 1):
            arrived = exchange(sent, scatter_order[part], stage)
            kept = kept + arrived.astype(jnp.float32)
            half_rows = kept.shape[0] // 2
            if stage < stages:
                sent = kept[half_rows:].astype(jnp.bfloat16)
                kept = kept[:half_rows]
        outputs.append((finished[part][1].astype(jnp.float32) + kept).astype(jnp.bfloat16))
    return jnp.concatenate(outputs, axis=1)


def solution(mesh):
    return mapped(mesh)


def mapped(mesh):
    return jax.shard_map(
        on_device,
        mesh=mesh,
        in_specs=(
            P("groups", None),
            P(("groups", "wide"), None),
            P(("groups", "wide"), None),
            P(),
            P(("groups", "wide"), None),
            P(("groups", "wide"), None),
            P("wide", None),
            P("wide", None),
            P("wide", None),
        ),
        out_specs=P(("groups", "wide"), None),
        check_vma=False,
    )
```

```python
import functools

import jax
import jax.numpy as jnp
from jax import lax
from jax.experimental import pallas as pl
from jax.experimental.pallas import tpu as pltpu
from jax.sharding import PartitionSpec as P


HEADS = 16
LANES = 128
TABLE_LANE = 64
UNITS = 256
PARTS = 2


def near(value):
    return pltpu.with_memory_space_constraint(value, pltpu.VMEM)


def far(value):
    return pltpu.with_memory_space_constraint(value, pltpu.HBM)


def near_shape(shape, dtype):
    return pltpu.VMEM(shape, dtype)


def partner(value, axis, stride):
    mask = 2**stride
    pairs = [(source, source ^ mask) for source in range(lax.axis_size(axis))]
    return lax.ppermute(value, axis, pairs)


def plan_orders(devices, group_size):
    near_bits = list(range(1, group_size.bit_length() - 1))
    all_bits = list(range(1, devices.bit_length() - 1))
    merge = (near_bits, near_bits[1:] + near_bits[:1])
    rest = [[bit for bit in all_bits if bit != order[-1]] for order in merge]
    gather = (rest[0][::-1], rest[1][2:][::-1] + rest[1][:2])
    crossed = [order[:-2] + order[-2:][::-1] for order in gather]
    scatter = [
        [order[::-1] + kept[-1:] for order, kept in zip(orders, merge)]
        for orders in (gather, crossed)
    ]
    scatter[0] = [order[:-2] + order[-2:][::-1] for order in scatter[0]]
    return merge, (gather, crossed), scatter


def exchange(value, orders, stage):
    pairs = [
        (source, source ^ (1 << orders[source % 2][stage]))
        for source in range(lax.axis_size("wide"))
    ]
    return lax.ppermute(value, "wide", pairs)


def lane_iota(shape):
    return lax.broadcasted_iota(jnp.int32, shape, 1)


def expand_tile(columns, tile, value_size):
    first = tile * LANES // value_size
    last = (tile * LANES + LANES - 1) // value_size
    rows = columns[0].shape[0]
    out = jnp.broadcast_to(columns[first], (rows, LANES))
    for head in range(first + 1, last + 1):
        edge = head * value_size - tile * LANES
        out = jnp.where(lane_iota((rows, LANES)) < edge, out, columns[head])
    return out


def pack_stats(peak, total, head_count):
    lane = lane_iota(peak.shape)
    high = total.astype(jnp.bfloat16).astype(jnp.float32)
    low = total - high
    packed = jnp.where(lane < head_count, peak, 0.0)
    shifted = pltpu.roll(jnp.where(lane < head_count, high, 0.0), head_count, 1)
    shifted_low = pltpu.roll(jnp.where(lane < head_count, low, 0.0), 2 * head_count, 1)
    return packed + shifted + shifted_low


def total_of(stats, head_count):
    return pltpu.roll(stats, LANES - head_count, 1) + pltpu.roll(
        stats, LANES - 2 * head_count, 1
    )


def head_windows(head, size):
    return head * size // LANES, -(-(head + 1) * size // LANES)


def head_scores(head, head_count, query_ref, keys_ref):
    key_size = query_ref.shape[1] // head_count
    low, high = [LANES * tile for tile in head_windows(head, key_size)]
    window = lane_iota((query_ref.shape[0], high - low)) + low
    inside = (window >= head * key_size) & (window < (head + 1) * key_size)
    query = jnp.where(inside, query_ref[:, low:high], jnp.zeros((), jnp.bfloat16))
    return key_size ** (-0.5) * lax.dot_general(
        query,
        keys_ref[:, low:high],
        (((1,), (1,)), ((), ())),
        preferred_element_type=jnp.float32,
    )


def rounded_peak(scores):
    peak = jnp.max(scores, axis=1, keepdims=True)
    return peak.astype(jnp.bfloat16).astype(jnp.float32)


def head_sums(head, value_size, raised, values_ref):
    low, high = head_windows(head, value_size)
    return jnp.dot(
        raised.astype(jnp.bfloat16),
        values_ref[:, low * LANES : high * LANES],
        preferred_element_type=jnp.float32,
    )


def stage_kernel(
    row_count,
    masks,
    device_ref,
    queries_ref,
    keys_ref,
    values_ref,
    query_ref,
    near_keys_ref,
    near_values_ref,
    arrived,
):
    group_size = queries_ref.shape[0] // row_count
    device = device_ref[0]
    odd = lax.rem(device, 2) == 1
    own_block = lax.rem(device, group_size)
    copies = [
        pltpu.make_async_copy(keys_ref, near_keys_ref, arrived.at[0]),
        pltpu.make_async_copy(values_ref, near_values_ref, arrived.at[1]),
    ]
    for slot, (even_mask, odd_mask) in enumerate(zip(*masks)):
        block = own_block ^ jnp.where(odd, odd_mask, even_mask)
        start = pl.multiple_of(block * row_count, row_count)
        copies.append(
            pltpu.make_async_copy(
                queries_ref.at[pl.ds(start, row_count), :],
                query_ref.at[slot * row_count : (slot + 1) * row_count, :],
                arrived.at[2 + slot],
            )
        )
    for copy in copies:
        copy.start()
    for copy in copies:
        copy.wait()


def attend_kernel(
    head_count, part, part_heads, query_ref, keys_a, keys_b, values_a, values_b, sent_ref, kept_ref
):
    rows = query_ref.shape[0]
    half = rows // 2
    value_size = values_a.shape[1] // head_count
    part_tiles = part_heads * value_size // LANES
    base = part * part_tiles
    lane = lane_iota((rows, LANES))
    peaks = jnp.zeros((rows, LANES), jnp.float32)
    totals = jnp.zeros((rows, LANES), jnp.float32)

    def put(tile, value):
        columns = slice(tile * LANES, (tile + 1) * LANES)
        kept_ref[:, columns] = value[:half]
        sent_ref[:, columns] = value[half:].astype(jnp.bfloat16)

    for at in range(part_heads):
        head = part * part_heads + at
        scores_a = head_scores(head, head_count, query_ref, keys_a)
        scores_b = head_scores(head, head_count, query_ref, keys_b)
        peak = jnp.maximum(rounded_peak(scores_a), rounded_peak(scores_b))
        raised_a = jnp.exp(scores_a - peak)
        raised_b = jnp.exp(scores_b - peak)
        total = jnp.sum(raised_a + raised_b, axis=1, keepdims=True)
        peaks = jnp.where(lane == at, peak, peaks)
        totals = jnp.where(lane == at, total, totals)
        summed = head_sums(head, value_size, raised_a, values_a) + head_sums(
            head, value_size, raised_b, values_b
        )
        low, high = head_windows(head, value_size)
        for tile in range(low, high):
            value = summed[:, (tile - low) * LANES : (tile - low + 1) * LANES]
            edge = head * value_size - tile * LANES
            if edge > 0:
                value = jnp.where(lane < edge, waiting, value)
            waiting = value
            if (tile + 1) * LANES <= (head + 1) * value_size:
                put(tile - base, value)
    put(part_tiles, pack_stats(peaks, totals, part_heads))


def merged_parts(kept_ref, came_ref, head_count, model_width):
    stats_a = kept_ref[:, model_width:]
    stats_b = came_ref[:, model_width:].astype(jnp.float32)
    peak = jnp.maximum(stats_a, stats_b)
    factor_a = jnp.exp(stats_a - peak)
    factor_b = jnp.exp(stats_b - peak)
    total = total_of(stats_a, head_count) * factor_a + total_of(stats_b, head_count) * factor_b
    return peak, total, factor_a, factor_b


def head_columns(array, head_count):
    return [array[:, head : head + 1] for head in range(head_count)]


def merge_kernel(head_count, kept_ref, came_ref, sent_ref, next_ref):
    model_width = kept_ref.shape[1] - LANES
    half = kept_ref.shape[0] // 2
    peak, total, factor_a, factor_b = merged_parts(kept_ref, came_ref, head_count, model_width)
    columns_a = head_columns(factor_a, head_count)
    columns_b = head_columns(factor_b, head_count)
    for tile in range(model_width // LANES + 1):
        columns = slice(tile * LANES, (tile + 1) * LANES)
        if tile * LANES == model_width:
            value = pack_stats(peak, total, head_count)
        else:
            value = kept_ref[:, columns] * expand_tile(
                columns_a, tile, model_width // head_count
            ) + came_ref[:, columns].astype(jnp.float32) * expand_tile(
                columns_b, tile, model_width // head_count
            )
        next_ref[:, columns] = value[:half]
        sent_ref[:, columns] = value[half:].astype(jnp.bfloat16)


def last_merge_kernel(head_count, kept_ref, came_ref, *rest):
    tables, (sent_ref, next_ref) = rest[:-2], rest[-2:]
    model_width = kept_ref.shape[1] - LANES
    half = kept_ref.shape[0] // 2
    peak, total, factor_a, factor_b = merged_parts(kept_ref, came_ref, head_count, model_width)
    columns_a = head_columns(factor_a, head_count)
    columns_b = head_columns(factor_b, head_count)
    for tile in range(model_width // LANES + 1):
        columns = slice(tile * LANES, (tile + 1) * LANES)
        if tile * LANES == model_width:
            value = pack_stats(peak, total, head_count)
            own = value[:half]
            for table_ref in tables:
                own = own + table_ref[...].astype(jnp.float32)
        else:
            value = kept_ref[:, columns] * expand_tile(
                columns_a, tile, model_width // head_count
            ) + came_ref[:, columns].astype(jnp.float32) * expand_tile(
                columns_b, tile, model_width // head_count
            )
            own = value[:half]
        next_ref[:, columns] = value
        sent_ref[:half, columns] = value[half:].astype(jnp.bfloat16)
        sent_ref[half:, columns] = own.astype(jnp.bfloat16)


def finish_kernel(part_heads, kept_ref, came_ref, *rest):
    tables, (block_ref, projected_ref) = rest[:-2], rest[-2:]
    half = kept_ref.shape[0] // 2
    width = kept_ref.shape[1] - LANES
    _, total, factor_a, factor_b = merged_parts(kept_ref, came_ref, part_heads, width)
    columns_a = head_columns(factor_a / total, part_heads)
    columns_b = head_columns(factor_b / total, part_heads)
    for tile in range(width // LANES):
        columns = slice(tile * LANES, (tile + 1) * LANES)
        value = kept_ref[:, columns] * expand_tile(
            columns_a, tile, width // part_heads
        ) + came_ref[:, columns].astype(jnp.float32) * expand_tile(
            columns_b, tile, width // part_heads
        )
        rounded = value.astype(jnp.bfloat16)
        block_ref[:, columns] = rounded
        projected_ref[:, columns] = rounded[:half]
    for table_ref in tables:
        came_table = came_ref[half:, width:]
        lane = lane_iota(came_table.shape)
        block_ref[:half, width:] = table_ref[...]
        block_ref[half:, width:] = jnp.where(
            lane >= TABLE_LANE, came_table.astype(jnp.float32), 0.0
        ).astype(jnp.bfloat16)


def down_product(hidden_ref, down_refs, out_ref, start):
    width = out_ref.shape[1]
    units = down_refs[0].shape[0]
    step = width // 2 if width % (4 * LANES) else 4 * LANES
    for low in range(0, width, step):
        columns = slice(start + low, start + low + step)
        out_ref[:, low : low + step] = sum(
            jnp.dot(
                hidden_ref[:, half * units : (half + 1) * units],
                down_ref[:, columns],
                preferred_element_type=jnp.float32,
            )
            for half, down_ref in enumerate(down_refs)
        ).astype(out_ref.dtype)


def joined_kernel(own_ref, came_ref, out_ref):
    half = own_ref.shape[0]
    out_ref[:half, :] = own_ref[...]
    out_ref[half:, :] = came_ref[...]


def joined(own, came):
    rows, width = own.shape
    whole = pl.BlockSpec(memory_space=pltpu.VMEM)
    return pl.pallas_call(
        joined_kernel,
        compiler_params=pltpu.CompilerParams(vmem_limit_bytes=12 << 20),
        out_shape=near_shape((2 * rows, width), own.dtype),
        in_specs=[whole] * 2,
        out_specs=whole,
    )(near(own), near(came))


def turned_half(rows_ref, gain_ref, start, width, turned):
    square = jnp.zeros((rows_ref.shape[0], LANES), jnp.float32)
    for low in range(0, width, LANES):
        residual = rows_ref[:, low : low + LANES].astype(jnp.float32)
        square = square + residual * residual
        gained = residual * gain_ref[:, start + low : start + low + LANES]
        turned[low : low + LANES, :] = gained.astype(jnp.bfloat16).T
    return jnp.sum(square.T, axis=0, keepdims=True)


def part_expert_kernel(
    part,
    device_ref,
    gain_ref,
    rows_ref,
    gate_a,
    gate_b,
    up_a,
    up_b,
    gates_ref,
    ups_ref,
    stats_ref,
    turned,
):
    width = turned.shape[0]
    stats_ref[0:1, :] = turned_half(rows_ref, gain_ref, part * width, width, turned)
    if rows_ref.shape[1] > width:
        scores = rows_ref[:, width:].astype(jnp.float32).T
        lane = lax.broadcasted_iota(jnp.int32, scores.shape, 0)
        chosen = jnp.where(lane == lax.div(device_ref[0], 2) + TABLE_LANE, scores, 0.0)
        stats_ref[1:2, :] = jnp.sum(chosen, axis=0, keepdims=True) / jnp.sum(
            scores, axis=0, keepdims=True
        )
    rows = turned[...]
    units = gate_a.shape[0]
    for weight_ref, low, out_ref in (
        (gate_a, 0, gates_ref),
        (gate_b, units, gates_ref),
        (up_a, 0, ups_ref),
        (up_b, units, ups_ref),
    ):
        out_ref[low : low + units, :] = jnp.dot(
            weight_ref[:, part * width : (part + 1) * width],
            rows,
            preferred_element_type=jnp.float32,
        )


def lower_pair(early, late):
    half = early.shape[1] // 2
    return jnp.where(lane_iota(early.shape) < half, early, pltpu.roll(late, half, 1))


def upper_pair(early, late):
    half = early.shape[1] // 2
    return jnp.where(lane_iota(early.shape) < half, pltpu.roll(early, half, 1), late)


def hidden_of(gate_part, up_part, inverse, share):
    gate_part = inverse * gate_part
    silu = gate_part / (1.0 + jnp.exp(-gate_part))
    return (silu * (inverse * up_part) * share).T.astype(jnp.bfloat16)


def second_expert_kernel(
    gain_ref,
    rows_ref,
    gates_ref,
    ups_ref,
    stats_ref,
    early_gates,
    early_ups,
    early_stats,
    gate_a,
    gate_b,
    up_a,
    up_b,
    down_a,
    down_b,
    out_ref,
    hidden,
    late_gates,
    late_ups,
    late_stats,
    turned,
):
    width = turned.shape[0]
    square = turned_half(rows_ref, gain_ref, width, width, turned)
    late_stats[0:1, :] = square
    row = (8, square.shape[1])
    other = upper_pair(
        jnp.broadcast_to(early_stats[0:1, :], row), jnp.broadcast_to(square, row)
    )[0:1, :]
    inverse = lax.rsqrt((stats_ref[0:1, :] + other) / (2 * width) + 1e-06)
    share = stats_ref[1:2, :]
    rows = turned[...]
    units = gate_a.shape[0]
    for half, (gate_ref, up_ref) in enumerate(((gate_a, up_a), (gate_b, up_b))):
        for low in range(0, units, UNITS):
            chunk = slice(low, low + UNITS)
            at = slice(half * units + low, half * units + low + UNITS)
            gate_part = jnp.dot(
                gate_ref[chunk, width:], rows, preferred_element_type=jnp.float32
            )
            up_part = jnp.dot(up_ref[chunk, width:], rows, preferred_element_type=jnp.float32)
            late_gates[at, :] = gate_part
            late_ups[at, :] = up_part
            hidden[:, at] = hidden_of(
                gates_ref[at, :] + upper_pair(early_gates[at, :], gate_part),
                ups_ref[at, :] + upper_pair(early_ups[at, :], up_part),
                inverse,
                share,
            )
    down_product(hidden, (down_a, down_b), out_ref, 0)


def rest_expert_kernel(
    hidden_ref,
    gates_ref,
    ups_ref,
    stats_ref,
    early_gates,
    early_ups,
    early_stats,
    late_gates,
    late_ups,
    late_stats,
    down_a,
    down_b,
    sent_ref,
    kept_ref,
    hidden,
    early_value,
    late_value,
):
    width = sent_ref.shape[1]
    row = (8, stats_ref.shape[1])
    other = lower_pair(
        jnp.broadcast_to(early_stats[0:1, :], row), jnp.broadcast_to(late_stats[0:1, :], row)
    )[0:1, :]
    inverse = lax.rsqrt((stats_ref[0:1, :] + other) / (2 * width) + 1e-06)
    for low in range(0, gates_ref.shape[0], UNITS):
        at = slice(low, low + UNITS)
        hidden[:, at] = hidden_of(
            gates_ref[at, :] + lower_pair(early_gates[at, :], late_gates[at, :]),
            ups_ref[at, :] + lower_pair(early_ups[at, :], late_ups[at, :]),
            inverse,
            stats_ref[1:2, :],
        )
    down_product(hidden, (down_a, down_b), early_value, width)
    down_product(hidden_ref, (down_a, down_b), late_value, width)
    half = early_value.shape[0] // 2
    sent_ref[:half, :] = early_value[half:, :].astype(sent_ref.dtype)
    sent_ref[half:, :] = late_value[half:, :].astype(sent_ref.dtype)
    kept_ref[:half, :] = early_value[:half, :]
    kept_ref[half:, :] = late_value[:half, :]


def kept_expert_kernel(hidden_ref, down_a, down_b, kept_ref):
    down_product(hidden_ref, (down_a, down_b), kept_ref, 0)


def part_expert_rows(part, device, gain, rows, gates, ups):
    units, model_width = gates[0].shape
    row_count = rows.shape[0]
    whole = pl.BlockSpec(memory_space=pltpu.VMEM)
    return pl.pallas_call(
        functools.partial(part_expert_kernel, part),
        compiler_params=pltpu.CompilerParams(vmem_limit_bytes=12 << 20),
        out_shape=(near_shape((2 * units, row_count), jnp.float32),) * 2
        + (near_shape((8, row_count), jnp.float32),),
        in_specs=[pl.BlockSpec(memory_space=pltpu.SMEM)] + [whole] * 6,
        out_specs=(whole,) * 3,
        scratch_shapes=[pltpu.VMEM((model_width // PARTS, row_count), jnp.bfloat16)],
    )(device, near(gain), near(rows), *[near(half) for half in (*gates, *ups)])


def expert_rows(device, gain, early, late, gates, ups, downs):
    units, model_width = gates[0].shape
    row_count = early[0].shape[0]
    width = model_width // PARTS
    whole = pl.BlockSpec(memory_space=pltpu.VMEM)
    first = [part_expert_rows(part, device, gain, early[part], gates, ups) for part in range(PARTS)]
    half = part_expert_rows(0, device, gain, late[0], gates, ups)
    products = (near_shape((2 * units, row_count), jnp.float32),) * 2 + (
        near_shape((8, row_count), jnp.float32),
    )
    hidden_shape = near_shape((row_count, 2 * units), jnp.bfloat16)
    operands = [gain, late[1], *half, *first[1], *gates, *ups, *downs]
    sent_first, hidden, *rest = pl.pallas_call(
        second_expert_kernel,
        name="expert_second",
        compiler_params=pltpu.CompilerParams(vmem_limit_bytes=12 << 20),
        out_shape=(near_shape((row_count, width), jnp.bfloat16), hidden_shape) + products,
        in_specs=[whole] * len(operands),
        out_specs=(whole,) * 5,
        scratch_shapes=[pltpu.VMEM((width, row_count), jnp.bfloat16)],
    )(*[near(operand) for operand in operands])
    operands = [hidden, *first[0], *first[1], *rest, *downs]
    sent, kept, hidden = pl.pallas_call(
        rest_expert_kernel,
        name="expert_rest",
        compiler_params=pltpu.CompilerParams(vmem_limit_bytes=12 << 20),
        out_shape=(
            near_shape((row_count, width), jnp.bfloat16),
            near_shape((row_count, width), jnp.float32),
            hidden_shape,
        ),
        in_specs=[whole] * len(operands),
        out_specs=(whole,) * 3,
        scratch_shapes=[pltpu.VMEM((row_count, width), jnp.float32)] * 2,
    )(*[near(operand) for operand in operands])
    kept_first = pl.pallas_call(
        kept_expert_kernel,
        name="expert_kept",
        compiler_params=pltpu.CompilerParams(vmem_limit_bytes=12 << 20),
        out_shape=near_shape((row_count, width), jnp.float32),
        in_specs=[whole] * 3,
        out_specs=whole,
    )(*[near(operand) for operand in (hidden, *downs)])
    return [(sent_first, kept_first), (sent, kept)]


def attention_rows(
    queries, patch_keys, patch_values, other_keys, other_values, table, row_count, orders
):
    model_width = patch_values.shape[1]
    part_width = model_width // PARTS + LANES
    part_heads = HEADS // PARTS
    stages = len(orders[0])
    device_index = lax.axis_index("wide")
    masks = [
        [
            sum(
                (1 << order[stage])
                for stage in range(stages)
                if slot >> (stages - 1 - stage) & 1
            )
            for slot in range(1 << stages)
        ]
        for order in orders
    ]
    rows = row_count << stages
    whole = pl.BlockSpec(memory_space=pltpu.VMEM)

    def pair_shapes(rows):
        return (
            near_shape((rows, part_width), jnp.bfloat16),
            near_shape((rows, part_width), jnp.float32),
        )

    anywhere = pl.BlockSpec(memory_space=pltpu.HBM)
    query_rows, own_keys, own_values = pl.pallas_call(
        functools.partial(stage_kernel, row_count, masks),
        name="stage_in",
        compiler_params=pltpu.CompilerParams(vmem_limit_bytes=4 << 20),
        out_shape=(
            near_shape((rows, queries.shape[1]), jnp.bfloat16),
            near_shape(patch_keys.shape, jnp.bfloat16),
            near_shape(patch_values.shape, jnp.bfloat16),
        ),
        in_specs=[pl.BlockSpec(memory_space=pltpu.SMEM)] + [anywhere] * 3,
        out_specs=(whole,) * 3,
        scratch_shapes=[pltpu.SemaphoreType.DMA((2 + (1 << stages),))],
    )(device_index.reshape(1), far(queries), far(patch_keys), far(patch_values))
    operands = (query_rows, own_keys, other_keys, own_values, other_values)
    chains = []
    for part in range(PARTS):
        chains += pl.pallas_call(
            functools.partial(attend_kernel, HEADS, part, part_heads),
            compiler_params=pltpu.CompilerParams(vmem_limit_bytes=8 << 20),
            out_shape=pair_shapes(rows // 2),
            in_specs=[whole] * 5,
            out_specs=(whole, whole),
        )(*[near(operand) for operand in operands])
    finished = []
    for part in range(PARTS):
        sent, kept = chains[2 * part : 2 * part + 2]
        for stage in range(stages - 1):
            came = exchange(sent, orders, stage)
            rows = kept.shape[0]
            last = stage == stages - 2
            operands = [near(kept), near(came)]
            if last and part == 0:
                operands.append(near(table))
            sent, kept = pl.pallas_call(
                functools.partial(last_merge_kernel if last else merge_kernel, part_heads),
                compiler_params=pltpu.CompilerParams(vmem_limit_bytes=6 << 20),
                out_shape=pair_shapes(rows if last else rows // 2),
                in_specs=[whole] * len(operands),
                out_specs=(whole, whole),
            )(*operands)
        came = exchange(sent, orders, stages - 1)
        rows = kept.shape[0]
        width = model_width // PARTS
        operands = [near(kept), near(came)] + ([near(table)] if part == 0 else [])
        block, projected = pl.pallas_call(
            functools.partial(finish_kernel, part_heads),
            compiler_params=pltpu.CompilerParams(vmem_limit_bytes=6 << 20),
            out_shape=(
                near_shape((rows, width + (LANES if part == 0 else 0)), jnp.bfloat16),
                near_shape((row_count, width), jnp.bfloat16),
            ),
            in_specs=[whole] * len(operands),
            out_specs=(whole, whole),
        )(*operands)
        finished.append((block, projected))
    return finished


def on_device(
    queries, patch_keys, patch_values, norm_gain, route_experts, route_weights, w_gate, w_up, w_down
):
    row_count = route_experts.shape[0]
    model_width = patch_values.shape[1]
    devices = lax.axis_size("wide")
    device_index = lax.axis_index("wide")
    score_table = jnp.sum(
        jnp.where(
            route_experts[:, :, None] == jnp.arange(-TABLE_LANE, LANES - TABLE_LANE, dtype=jnp.int32),
            route_weights[:, :, None],
            0,
        ),
        axis=1,
    ).astype(jnp.bfloat16)
    merge_order, gather_order, scatter_order = plan_orders(
        devices, queries.shape[0] // row_count
    )
    other_keys = partner(patch_keys, "wide", 0)
    other_values = partner(patch_values, "wide", 0)
    halves, other_keys, other_values = lax.optimization_barrier(
        ((w_gate, w_up, w_down), other_keys, other_values)
    )
    weights = []
    for own in halves:
        weights += [own, partner(own, "wide", 0)]
    gain = norm_gain.reshape(1, model_width)
    finished = attention_rows(
        queries,
        patch_keys,
        patch_values,
        other_keys,
        other_values,
        score_table,
        row_count,
        merge_order,
    )
    blocks = [block for block, _ in finished]
    stages = len(gather_order[0][0])
    own_weights = weights[::2]
    arrived = {}
    for stage in range(stages):
        for part in range(PARTS):
            arrived[part] = exchange(blocks[part], gather_order[part], stage)
            if stage < stages - 1:
                blocks[part] = joined(blocks[part], arrived[part])
    came = [arrived[part] for part in range(PARTS)]
    device = device_index.reshape(1)
    gate_a, up_a, down_a = own_weights
    gate_b, up_b, down_b = weights[1::2]
    gates, ups, downs = (gate_a, gate_b), (up_a, up_b), (down_a, down_b)
    outputs = []
    for part, (sent, kept) in enumerate(
        expert_rows(device, gain, blocks, came, gates, ups, downs)
    ):
        for stage in range(stages + 1):
            arrived = exchange(sent, scatter_order[part], stage)
            kept = kept + arrived.astype(jnp.float32)
            half_rows = kept.shape[0] // 2
            if part == 0 and stage == stages - 2:
                quarters = kept.reshape(2, 2, half_rows // 2, -1)
                sent = quarters[:, 1].reshape(half_rows, -1).astype(jnp.bfloat16)
                kept = quarters[:, 0].reshape(half_rows, -1)
            elif stage < stages:
                sent = kept[half_rows:].astype(jnp.bfloat16)
                kept = kept[:half_rows]
        outputs.append((finished[part][1].astype(jnp.float32) + kept).astype(jnp.bfloat16))
    return jnp.concatenate(outputs, axis=1)


def solution(mesh):
    return mapped(mesh)


def mapped(mesh):
    return jax.shard_map(
        on_device,
        mesh=mesh,
        in_specs=(
            P("groups", None),
            P(("groups", "wide"), None),
            P(("groups", "wide"), None),
            P(),
            P(("groups", "wide"), None),
            P(("groups", "wide"), None),
            P("wide", None),
            P("wide", None),
            P("wide", None),
        ),
        out_specs=P(("groups", "wide"), None),
        check_vma=False,
    )
```

```python
import functools

import jax
import jax.numpy as jnp
from jax import lax
from jax.experimental import pallas as pl
from jax.experimental.pallas import tpu as pltpu
from jax.sharding import PartitionSpec as P


HEADS = 16
LANES = 128
TABLE_LANE = 64
UNITS = 256
PARTS = 2


def near(value):
    return pltpu.with_memory_space_constraint(value, pltpu.VMEM)


def far(value):
    return pltpu.with_memory_space_constraint(value, pltpu.HBM)


def near_shape(shape, dtype):
    return pltpu.VMEM(shape, dtype)


def partner(value, axis, stride):
    mask = 2**stride
    pairs = [(source, source ^ mask) for source in range(lax.axis_size(axis))]
    return lax.ppermute(value, axis, pairs)


def plan_orders(devices, group_size):
    near_bits = list(range(1, group_size.bit_length() - 1))
    all_bits = list(range(1, devices.bit_length() - 1))
    merge = (near_bits, near_bits[1:] + near_bits[:1])
    rest = [[bit for bit in all_bits if bit != order[-1]] for order in merge]
    gather = (rest[0][::-1], rest[1][2:][::-1] + rest[1][:2])
    crossed = [order[:-2] + order[-2:][::-1] for order in gather]
    scatter = [
        [order[::-1] + kept[-1:] for order, kept in zip(orders, merge)]
        for orders in (gather, crossed)
    ]
    return merge, (gather, crossed), scatter


def exchange(value, orders, stage):
    pairs = [
        (source, source ^ (1 << orders[source % 2][stage]))
        for source in range(lax.axis_size("wide"))
    ]
    return lax.ppermute(value, "wide", pairs)


def lane_iota(shape):
    return lax.broadcasted_iota(jnp.int32, shape, 1)


def expand_tile(columns, tile, value_size):
    first = tile * LANES // value_size
    last = (tile * LANES + LANES - 1) // value_size
    rows = columns[0].shape[0]
    out = jnp.broadcast_to(columns[first], (rows, LANES))
    for head in range(first + 1, last + 1):
        edge = head * value_size - tile * LANES
        out = jnp.where(lane_iota((rows, LANES)) < edge, out, columns[head])
    return out


def pack_stats(peak, total, head_count):
    lane = lane_iota(peak.shape)
    high = total.astype(jnp.bfloat16).astype(jnp.float32)
    low = total - high
    packed = jnp.where(lane < head_count, peak, 0.0)
    shifted = pltpu.roll(jnp.where(lane < head_count, high, 0.0), head_count, 1)
    shifted_low = pltpu.roll(jnp.where(lane < head_count, low, 0.0), 2 * head_count, 1)
    return packed + shifted + shifted_low


def total_of(stats, head_count):
    return pltpu.roll(stats, LANES - head_count, 1) + pltpu.roll(
        stats, LANES - 2 * head_count, 1
    )


def head_windows(head, size):
    return head * size // LANES, -(-(head + 1) * size // LANES)


def head_scores(head, head_count, query_ref, keys_ref):
    key_size = query_ref.shape[1] // head_count
    low, high = [LANES * tile for tile in head_windows(head, key_size)]
    window = lane_iota((query_ref.shape[0], high - low)) + low
    inside = (window >= head * key_size) & (window < (head + 1) * key_size)
    query = jnp.where(inside, query_ref[:, low:high], jnp.zeros((), jnp.bfloat16))
    return key_size ** (-0.5) * lax.dot_general(
        query,
        keys_ref[:, low:high],
        (((1,), (1,)), ((), ())),
        preferred_element_type=jnp.float32,
    )


def rounded_peak(scores):
    peak = jnp.max(scores, axis=1, keepdims=True)
    return peak.astype(jnp.bfloat16).astype(jnp.float32)


def head_sums(head, value_size, raised, values_ref):
    low, high = head_windows(head, value_size)
    return jnp.dot(
        raised.astype(jnp.bfloat16),
        values_ref[:, low * LANES : high * LANES],
        preferred_element_type=jnp.float32,
    )


def stage_kernel(
    row_count,
    masks,
    device_ref,
    queries_ref,
    keys_ref,
    values_ref,
    query_ref,
    near_keys_ref,
    near_values_ref,
    arrived,
):
    group_size = queries_ref.shape[0] // row_count
    device = device_ref[0]
    odd = lax.rem(device, 2) == 1
    own_block = lax.rem(device, group_size)
    copies = [
        pltpu.make_async_copy(keys_ref, near_keys_ref, arrived.at[0]),
        pltpu.make_async_copy(values_ref, near_values_ref, arrived.at[1]),
    ]
    for slot, (even_mask, odd_mask) in enumerate(zip(*masks)):
        block = own_block ^ jnp.where(odd, odd_mask, even_mask)
        start = pl.multiple_of(block * row_count, row_count)
        copies.append(
            pltpu.make_async_copy(
                queries_ref.at[pl.ds(start, row_count), :],
                query_ref.at[slot * row_count : (slot + 1) * row_count, :],
                arrived.at[2 + slot],
            )
        )
    for copy in copies:
        copy.start()
    for copy in copies:
        copy.wait()


def attend_kernel(
    head_count, part, part_heads, query_ref, keys_a, keys_b, values_a, values_b, sent_ref, kept_ref
):
    rows = query_ref.shape[0]
    half = rows // 2
    value_size = values_a.shape[1] // head_count
    part_tiles = part_heads * value_size // LANES
    base = part * part_tiles
    lane = lane_iota((rows, LANES))
    peaks = jnp.zeros((rows, LANES), jnp.float32)
    totals = jnp.zeros((rows, LANES), jnp.float32)

    def put(tile, value):
        columns = slice(tile * LANES, (tile + 1) * LANES)
        kept_ref[:, columns] = value[:half]
        sent_ref[:, columns] = value[half:].astype(jnp.bfloat16)

    for at in range(part_heads):
        head = part * part_heads + at
        scores_a = head_scores(head, head_count, query_ref, keys_a)
        scores_b = head_scores(head, head_count, query_ref, keys_b)
        peak = jnp.maximum(rounded_peak(scores_a), rounded_peak(scores_b))
        raised_a = jnp.exp(scores_a - peak)
        raised_b = jnp.exp(scores_b - peak)
        total = jnp.sum(raised_a + raised_b, axis=1, keepdims=True)
        peaks = jnp.where(lane == at, peak, peaks)
        totals = jnp.where(lane == at, total, totals)
        summed = head_sums(head, value_size, raised_a, values_a) + head_sums(
            head, value_size, raised_b, values_b
        )
        low, high = head_windows(head, value_size)
        for tile in range(low, high):
            value = summed[:, (tile - low) * LANES : (tile - low + 1) * LANES]
            edge = head * value_size - tile * LANES
            if edge > 0:
                value = jnp.where(lane < edge, waiting, value)
            waiting = value
            if (tile + 1) * LANES <= (head + 1) * value_size:
                put(tile - base, value)
    put(part_tiles, pack_stats(peaks, totals, part_heads))


def merged_parts(kept_ref, came_ref, head_count, model_width):
    stats_a = kept_ref[:, model_width:]
    stats_b = came_ref[:, model_width:].astype(jnp.float32)
    peak = jnp.maximum(stats_a, stats_b)
    factor_a = jnp.exp(stats_a - peak)
    factor_b = jnp.exp(stats_b - peak)
    total = total_of(stats_a, head_count) * factor_a + total_of(stats_b, head_count) * factor_b
    return peak, total, factor_a, factor_b


def head_columns(array, head_count):
    return [array[:, head : head + 1] for head in range(head_count)]


def merge_kernel(head_count, kept_ref, came_ref, sent_ref, next_ref):
    model_width = kept_ref.shape[1] - LANES
    half = kept_ref.shape[0] // 2
    peak, total, factor_a, factor_b = merged_parts(kept_ref, came_ref, head_count, model_width)
    columns_a = head_columns(factor_a, head_count)
    columns_b = head_columns(factor_b, head_count)
    for tile in range(model_width // LANES + 1):
        columns = slice(tile * LANES, (tile + 1) * LANES)
        if tile * LANES == model_width:
            value = pack_stats(peak, total, head_count)
        else:
            value = kept_ref[:, columns] * expand_tile(
                columns_a, tile, model_width // head_count
            ) + came_ref[:, columns].astype(jnp.float32) * expand_tile(
                columns_b, tile, model_width // head_count
            )
        next_ref[:, columns] = value[:half]
        sent_ref[:, columns] = value[half:].astype(jnp.bfloat16)


def last_merge_kernel(head_count, kept_ref, came_ref, *rest):
    tables, (sent_ref, next_ref) = rest[:-2], rest[-2:]
    model_width = kept_ref.shape[1] - LANES
    half = kept_ref.shape[0] // 2
    peak, total, factor_a, factor_b = merged_parts(kept_ref, came_ref, head_count, model_width)
    columns_a = head_columns(factor_a, head_count)
    columns_b = head_columns(factor_b, head_count)
    for tile in range(model_width // LANES + 1):
        columns = slice(tile * LANES, (tile + 1) * LANES)
        if tile * LANES == model_width:
            value = pack_stats(peak, total, head_count)
            own = value[:half]
            for table_ref in tables:
                own = own + table_ref[...].astype(jnp.float32)
        else:
            value = kept_ref[:, columns] * expand_tile(
                columns_a, tile, model_width // head_count
            ) + came_ref[:, columns].astype(jnp.float32) * expand_tile(
                columns_b, tile, model_width // head_count
            )
            own = value[:half]
        next_ref[:, columns] = value
        sent_ref[:half, columns] = value[half:].astype(jnp.bfloat16)
        sent_ref[half:, columns] = own.astype(jnp.bfloat16)


def finish_kernel(part_heads, kept_ref, came_ref, *rest):
    tables, (block_ref, projected_ref) = rest[:-2], rest[-2:]
    half = kept_ref.shape[0] // 2
    width = kept_ref.shape[1] - LANES
    _, total, factor_a, factor_b = merged_parts(kept_ref, came_ref, part_heads, width)
    columns_a = head_columns(factor_a / total, part_heads)
    columns_b = head_columns(factor_b / total, part_heads)
    for tile in range(width // LANES):
        columns = slice(tile * LANES, (tile + 1) * LANES)
        value = kept_ref[:, columns] * expand_tile(
            columns_a, tile, width // part_heads
        ) + came_ref[:, columns].astype(jnp.float32) * expand_tile(
            columns_b, tile, width // part_heads
        )
        rounded = value.astype(jnp.bfloat16)
        block_ref[:, columns] = rounded
        projected_ref[:, columns] = rounded[:half]
    for table_ref in tables:
        came_table = came_ref[half:, width:]
        lane = lane_iota(came_table.shape)
        block_ref[:half, width:] = table_ref[...]
        block_ref[half:, width:] = jnp.where(
            lane >= TABLE_LANE, came_table.astype(jnp.float32), 0.0
        ).astype(jnp.bfloat16)


def down_product(hidden_ref, down_refs, out_ref, start):
    width = out_ref.shape[1]
    units = down_refs[0].shape[0]
    step = width // 2 if width % (4 * LANES) else 4 * LANES
    for low in range(0, width, step):
        columns = slice(start + low, start + low + step)
        out_ref[:, low : low + step] = sum(
            jnp.dot(
                hidden_ref[:, half * units : (half + 1) * units],
                down_ref[:, columns],
                preferred_element_type=jnp.float32,
            )
            for half, down_ref in enumerate(down_refs)
        ).astype(out_ref.dtype)


def joined_kernel(own_ref, came_ref, out_ref):
    half = own_ref.shape[0]
    out_ref[:half, :] = own_ref[...]
    out_ref[half:, :] = came_ref[...]


def joined(own, came):
    rows, width = own.shape
    whole = pl.BlockSpec(memory_space=pltpu.VMEM)
    return pl.pallas_call(
        joined_kernel,
        compiler_params=pltpu.CompilerParams(vmem_limit_bytes=12 << 20),
        out_shape=near_shape((2 * rows, width), own.dtype),
        in_specs=[whole] * 2,
        out_specs=whole,
    )(near(own), near(came))


def turned_half(rows_ref, gain_ref, start, width, turned):
    square = jnp.zeros((rows_ref.shape[0], LANES), jnp.float32)
    for low in range(0, width, LANES):
        residual = rows_ref[:, low : low + LANES].astype(jnp.float32)
        square = square + residual * residual
        gained = residual * gain_ref[:, start + low : start + low + LANES]
        turned[low : low + LANES, :] = gained.astype(jnp.bfloat16).T
    return jnp.sum(square.T, axis=0, keepdims=True)


def part_expert_kernel(
    part,
    device_ref,
    gain_ref,
    rows_ref,
    gate_a,
    gate_b,
    up_a,
    up_b,
    gates_ref,
    ups_ref,
    stats_ref,
    turned,
):
    width = turned.shape[0]
    stats_ref[0:1, :] = turned_half(rows_ref, gain_ref, part * width, width, turned)
    if rows_ref.shape[1] > width:
        scores = rows_ref[:, width:].astype(jnp.float32).T
        lane = lax.broadcasted_iota(jnp.int32, scores.shape, 0)
        chosen = jnp.where(lane == lax.div(device_ref[0], 2) + TABLE_LANE, scores, 0.0)
        stats_ref[1:2, :] = jnp.sum(chosen, axis=0, keepdims=True) / jnp.sum(
            scores, axis=0, keepdims=True
        )
    rows = turned[...]
    units = gate_a.shape[0]
    for weight_ref, low, out_ref in (
        (gate_a, 0, gates_ref),
        (gate_b, units, gates_ref),
        (up_a, 0, ups_ref),
        (up_b, units, ups_ref),
    ):
        out_ref[low : low + units, :] = jnp.dot(
            weight_ref[:, part * width : (part + 1) * width],
            rows,
            preferred_element_type=jnp.float32,
        )


def lower_pair(early, late):
    half = early.shape[1] // 2
    return jnp.where(lane_iota(early.shape) < half, early, pltpu.roll(late, half, 1))


def upper_pair(early, late):
    half = early.shape[1] // 2
    return jnp.where(lane_iota(early.shape) < half, pltpu.roll(early, half, 1), late)


def hidden_of(gate_part, up_part, inverse, share):
    gate_part = inverse * gate_part
    silu = gate_part / (1.0 + jnp.exp(-gate_part))
    return (silu * (inverse * up_part) * share).T.astype(jnp.bfloat16)


def second_expert_kernel(
    gain_ref,
    rows_ref,
    gates_ref,
    ups_ref,
    stats_ref,
    early_gates,
    early_ups,
    early_stats,
    gate_a,
    gate_b,
    up_a,
    up_b,
    down_a,
    down_b,
    out_ref,
    hidden,
    late_gates,
    late_ups,
    late_stats,
    turned,
):
    width = turned.shape[0]
    square = turned_half(rows_ref, gain_ref, width, width, turned)
    late_stats[0:1, :] = square
    row = (8, square.shape[1])
    other = upper_pair(
        jnp.broadcast_to(early_stats[0:1, :], row), jnp.broadcast_to(square, row)
    )[0:1, :]
    inverse = lax.rsqrt((stats_ref[0:1, :] + other) / (2 * width) + 1e-06)
    share = stats_ref[1:2, :]
    rows = turned[...]
    units = gate_a.shape[0]
    for half, (gate_ref, up_ref) in enumerate(((gate_a, up_a), (gate_b, up_b))):
        for low in range(0, units, UNITS):
            chunk = slice(low, low + UNITS)
            at = slice(half * units + low, half * units + low + UNITS)
            gate_part = jnp.dot(
                gate_ref[chunk, width:], rows, preferred_element_type=jnp.float32
            )
            up_part = jnp.dot(up_ref[chunk, width:], rows, preferred_element_type=jnp.float32)
            late_gates[at, :] = gate_part
            late_ups[at, :] = up_part
            hidden[:, at] = hidden_of(
                gates_ref[at, :] + upper_pair(early_gates[at, :], gate_part),
                ups_ref[at, :] + upper_pair(early_ups[at, :], up_part),
                inverse,
                share,
            )
    down_product(hidden, (down_a, down_b), out_ref, 0)


def rest_expert_kernel(
    hidden_ref,
    gates_ref,
    ups_ref,
    stats_ref,
    early_gates,
    early_ups,
    early_stats,
    late_gates,
    late_ups,
    late_stats,
    down_a,
    down_b,
    sent_ref,
    hidden,
    leaving,
):
    width = sent_ref.shape[1]
    row = (8, stats_ref.shape[1])
    other = lower_pair(
        jnp.broadcast_to(early_stats[0:1, :], row), jnp.broadcast_to(late_stats[0:1, :], row)
    )[0:1, :]
    inverse = lax.rsqrt((stats_ref[0:1, :] + other) / (2 * width) + 1e-06)
    for low in range(0, gates_ref.shape[0], UNITS):
        at = slice(low, low + UNITS)
        hidden[:, at] = hidden_of(
            gates_ref[at, :] + lower_pair(early_gates[at, :], late_gates[at, :]),
            ups_ref[at, :] + lower_pair(early_ups[at, :], late_ups[at, :]),
            inverse,
            stats_ref[1:2, :],
        )
    half = leaving.shape[0] // 2
    leaving[:half, :] = hidden[half:, :]
    leaving[half:, :] = hidden_ref[half:, :]
    down_product(leaving, (down_a, down_b), sent_ref, width)


def kept_expert_kernel(early_ref, late_ref, down_a, down_b, first_ref, second_ref, staying):
    half = staying.shape[0] // 2
    down_product(early_ref, (down_a, down_b), first_ref, 0)
    staying[:half, :] = early_ref[:half, :]
    staying[half:, :] = late_ref[:half, :]
    down_product(staying, (down_a, down_b), second_ref, first_ref.shape[1])


def part_expert_rows(part, device, gain, rows, gates, ups):
    units, model_width = gates[0].shape
    row_count = rows.shape[0]
    whole = pl.BlockSpec(memory_space=pltpu.VMEM)
    return pl.pallas_call(
        functools.partial(part_expert_kernel, part),
        compiler_params=pltpu.CompilerParams(vmem_limit_bytes=12 << 20),
        out_shape=(near_shape((2 * units, row_count), jnp.float32),) * 2
        + (near_shape((8, row_count), jnp.float32),),
        in_specs=[pl.BlockSpec(memory_space=pltpu.SMEM)] + [whole] * 6,
        out_specs=(whole,) * 3,
        scratch_shapes=[pltpu.VMEM((model_width // PARTS, row_count), jnp.bfloat16)],
    )(device, near(gain), near(rows), *[near(half) for half in (*gates, *ups)])


def expert_rows(device, gain, early, late, gates, ups, downs):
    units, model_width = gates[0].shape
    row_count = early[0].shape[0]
    width = model_width // PARTS
    whole = pl.BlockSpec(memory_space=pltpu.VMEM)
    first = [part_expert_rows(part, device, gain, early[part], gates, ups) for part in range(PARTS)]
    half = part_expert_rows(0, device, gain, late[0], gates, ups)
    products = (near_shape((2 * units, row_count), jnp.float32),) * 2 + (
        near_shape((8, row_count), jnp.float32),
    )
    hidden_shape = near_shape((row_count, 2 * units), jnp.bfloat16)
    operands = [gain, late[1], *half, *first[1], *gates, *ups, *downs]
    sent_first, hidden, *rest = pl.pallas_call(
        second_expert_kernel,
        name="expert_second",
        compiler_params=pltpu.CompilerParams(vmem_limit_bytes=12 << 20),
        out_shape=(near_shape((row_count, width), jnp.bfloat16), hidden_shape) + products,
        in_specs=[whole] * len(operands),
        out_specs=(whole,) * 5,
        scratch_shapes=[pltpu.VMEM((width, row_count), jnp.bfloat16)],
    )(*[near(operand) for operand in operands])
    operands = [hidden, *first[0], *first[1], *rest, *downs]
    sent, early_hidden = pl.pallas_call(
        rest_expert_kernel,
        name="expert_rest",
        compiler_params=pltpu.CompilerParams(vmem_limit_bytes=12 << 20),
        out_shape=(near_shape((row_count, width), jnp.bfloat16), hidden_shape),
        in_specs=[whole] * len(operands),
        out_specs=(whole,) * 2,
        scratch_shapes=[pltpu.VMEM((row_count, 2 * units), jnp.bfloat16)],
    )(*[near(operand) for operand in operands])
    kept_first, kept = pl.pallas_call(
        kept_expert_kernel,
        name="expert_kept",
        compiler_params=pltpu.CompilerParams(vmem_limit_bytes=12 << 20),
        out_shape=(near_shape((row_count, width), jnp.float32),) * 2,
        in_specs=[whole] * 4,
        out_specs=(whole,) * 2,
        scratch_shapes=[pltpu.VMEM((row_count, 2 * units), jnp.bfloat16)],
    )(*[near(operand) for operand in (early_hidden, hidden, *downs)])
    return [(sent_first, kept_first), (sent, kept)]


def attention_rows(
    queries, patch_keys, patch_values, other_keys, other_values, table, row_count, orders
):
    model_width = patch_values.shape[1]
    part_width = model_width // PARTS + LANES
    part_heads = HEADS // PARTS
    stages = len(orders[0])
    device_index = lax.axis_index("wide")
    masks = [
        [
            sum(
                (1 << order[stage])
                for stage in range(stages)
                if slot >> (stages - 1 - stage) & 1
            )
            for slot in range(1 << stages)
        ]
        for order in orders
    ]
    rows = row_count << stages
    whole = pl.BlockSpec(memory_space=pltpu.VMEM)

    def pair_shapes(rows):
        return (
            near_shape((rows, part_width), jnp.bfloat16),
            near_shape((rows, part_width), jnp.float32),
        )

    anywhere = pl.BlockSpec(memory_space=pltpu.HBM)
    query_rows, own_keys, own_values = pl.pallas_call(
        functools.partial(stage_kernel, row_count, masks),
        name="stage_in",
        compiler_params=pltpu.CompilerParams(vmem_limit_bytes=4 << 20),
        out_shape=(
            near_shape((rows, queries.shape[1]), jnp.bfloat16),
            near_shape(patch_keys.shape, jnp.bfloat16),
            near_shape(patch_values.shape, jnp.bfloat16),
        ),
        in_specs=[pl.BlockSpec(memory_space=pltpu.SMEM)] + [anywhere] * 3,
        out_specs=(whole,) * 3,
        scratch_shapes=[pltpu.SemaphoreType.DMA((2 + (1 << stages),))],
    )(device_index.reshape(1), far(queries), far(patch_keys), far(patch_values))
    operands = (query_rows, own_keys, other_keys, own_values, other_values)
    chains = []
    for part in range(PARTS):
        chains += pl.pallas_call(
            functools.partial(attend_kernel, HEADS, part, part_heads),
            compiler_params=pltpu.CompilerParams(vmem_limit_bytes=8 << 20),
            out_shape=pair_shapes(rows // 2),
            in_specs=[whole] * 5,
            out_specs=(whole, whole),
        )(*[near(operand) for operand in operands])
    finished = []
    for part in range(PARTS):
        sent, kept = chains[2 * part : 2 * part + 2]
        for stage in range(stages - 1):
            came = exchange(sent, orders, stage)
            rows = kept.shape[0]
            last = stage == stages - 2
            operands = [near(kept), near(came)]
            if last and part == 0:
                operands.append(near(table))
            sent, kept = pl.pallas_call(
                functools.partial(last_merge_kernel if last else merge_kernel, part_heads),
                compiler_params=pltpu.CompilerParams(vmem_limit_bytes=6 << 20),
                out_shape=pair_shapes(rows if last else rows // 2),
                in_specs=[whole] * len(operands),
                out_specs=(whole, whole),
            )(*operands)
        came = exchange(sent, orders, stages - 1)
        rows = kept.shape[0]
        width = model_width // PARTS
        operands = [near(kept), near(came)] + ([near(table)] if part == 0 else [])
        block, projected = pl.pallas_call(
            functools.partial(finish_kernel, part_heads),
            compiler_params=pltpu.CompilerParams(vmem_limit_bytes=6 << 20),
            out_shape=(
                near_shape((rows, width + (LANES if part == 0 else 0)), jnp.bfloat16),
                near_shape((row_count, width), jnp.bfloat16),
            ),
            in_specs=[whole] * len(operands),
            out_specs=(whole, whole),
        )(*operands)
        finished.append((block, projected))
    return finished


def on_device(
    queries, patch_keys, patch_values, norm_gain, route_experts, route_weights, w_gate, w_up, w_down
):
    row_count = route_experts.shape[0]
    model_width = patch_values.shape[1]
    devices = lax.axis_size("wide")
    device_index = lax.axis_index("wide")
    score_table = jnp.sum(
        jnp.where(
            route_experts[:, :, None] == jnp.arange(-TABLE_LANE, LANES - TABLE_LANE, dtype=jnp.int32),
            route_weights[:, :, None],
            0,
        ),
        axis=1,
    ).astype(jnp.bfloat16)
    merge_order, gather_order, scatter_order = plan_orders(
        devices, queries.shape[0] // row_count
    )
    other_keys = partner(patch_keys, "wide", 0)
    other_values = partner(patch_values, "wide", 0)
    halves, other_keys, other_values = lax.optimization_barrier(
        ((w_gate, w_up, w_down), other_keys, other_values)
    )
    weights = []
    for own in halves:
        weights += [own, partner(own, "wide", 0)]
    gain = norm_gain.reshape(1, model_width)
    finished = attention_rows(
        queries,
        patch_keys,
        patch_values,
        other_keys,
        other_values,
        score_table,
        row_count,
        merge_order,
    )
    blocks = [block for block, _ in finished]
    stages = len(gather_order[0][0])
    own_weights = weights[::2]
    arrived = {}
    for stage in range(stages):
        for part in range(PARTS):
            arrived[part] = exchange(blocks[part], gather_order[part], stage)
            if stage < stages - 1:
                blocks[part] = joined(blocks[part], arrived[part])
    came = [arrived[part] for part in range(PARTS)]
    device = device_index.reshape(1)
    gate_a, up_a, down_a = own_weights
    gate_b, up_b, down_b = weights[1::2]
    gates, ups, downs = (gate_a, gate_b), (up_a, up_b), (down_a, down_b)
    outputs = []
    for part, (sent, kept) in enumerate(
        expert_rows(device, gain, blocks, came, gates, ups, downs)
    ):
        for stage in range(stages + 1):
            arrived = exchange(sent, scatter_order[part], stage)
            kept = kept + arrived.astype(jnp.float32)
            half_rows = kept.shape[0] // 2
            if stage < stages:
                sent = kept[half_rows:].astype(jnp.bfloat16)
                kept = kept[:half_rows]
        outputs.append((finished[part][1].astype(jnp.float32) + kept).astype(jnp.bfloat16))
    return jnp.concatenate(outputs, axis=1)


def solution(mesh):
    def step(queries, *rest):
        return mapped(mesh)(queries, *rest)

    return step


def mapped(mesh):
    return jax.shard_map(
        on_device,
        mesh=mesh,
        in_specs=(
            P("groups", None),
            P(("groups", "wide"), None),
            P(("groups", "wide"), None),
            P(),
            P(("groups", "wide"), None),
            P(("groups", "wide"), None),
            P("wide", None),
            P("wide", None),
            P("wide", None),
        ),
        out_specs=P(("groups", "wide"), None),
        check_vma=False,
    )
```
